32 devices in a mesh: wide: 16 (over z, y, core), narrow: 2 (over x).
Axes of the slice: x: 2, y: 2, z: 4, core: 2. Of those that a mesh axis runs over, the one named last changes fastest.
Arguments:
- frames_in: bfloat16 [32, 256, 1152], P(('wide', 'narrow')), may hold values from -6 to 6
- conditioning: bfloat16 [32, 1152], P(('wide', 'narrow')), may hold values from -5 to 5
- grid: int32 [32, 2], P(('wide', 'narrow')), may hold values from 8 to 32, as said below
- cotangent: bfloat16 [32, 256, 1152], P(('wide', 'narrow')), may hold values from -6 to 6
- mod_weight: float32 [1152, 6912], P(('wide', 'narrow')), may hold values from -0.1875 to 0.1875
- qkv_weight: float32 [1152, 3456], P(('wide', 'narrow')), may hold values from -0.1875 to 0.1875
- out_weight: float32 [1152, 1152], P(('wide', 'narrow')), may hold values from -1 to 1
- up_weight: float32 [1152, 4608], P(('wide', 'narrow')), may hold values from -0.1875 to 0.1875
- down_weight: float32 [4608, 1152], P(('wide', 'narrow')), may hold values from -0.09375 to 0.09375
- biases: float32 [16128], P(('wide', 'narrow')), may hold values from -1.2 to 1.2
- mod_state: float32 [3, 1152, 6912], P(None, ('wide', 'narrow')), as said below
- qkv_state: float32 [3, 1152, 3456], P(None, ('wide', 'narrow')), as said below
- out_state: float32 [3, 1152, 1152], P(None, ('wide', 'narrow')), as said below
- up_state: float32 [3, 1152, 4608], P(None, ('wide', 'narrow')), as said below
- down_state: float32 [3, 4608, 1152], P(None, ('wide', 'narrow')), as said below
- bias_state: float32 [3, 16128], P(None, ('wide', 'narrow')), as said below
Outputs:
- block_out: bfloat16 [32, 256, 1152], P(('wide', 'narrow'))
- frames_grad: bfloat16 [32, 256, 1152], P(('wide', 'narrow'))
- cond_grad: float32 [32, 1152], P(('wide', 'narrow'))
- grad_norm: float32 [], replicated
- mod_grad: float32 [1152, 6912], P(('wide', 'narrow'))
- qkv_grad: float32 [1152, 3456], P(('wide', 'narrow'))
- out_grad: float32 [1152, 1152], P(('wide', 'narrow'))
- up_grad: float32 [1152, 4608], P(('wide', 'narrow'))
- down_grad: float32 [4608, 1152], P(('wide', 'narrow'))
- bias_grad: float32 [16128], P(('wide', 'narrow'))
- mod_new: float32 [1152, 6912], P(('wide', 'narrow'))
- qkv_new: float32 [1152, 3456], P(('wide', 'narrow'))
- out_new: float32 [1152, 1152], P(('wide', 'narrow'))
- up_new: float32 [1152, 4608], P(('wide', 'narrow'))
- down_new: float32 [4608, 1152], P(('wide', 'narrow'))
- bias_new: float32 [16128], P(('wide', 'narrow'))
- mod_state_new: float32 [3, 1152, 6912], P(None, ('wide', 'narrow'))
- qkv_state_new: float32 [3, 1152, 3456], P(None, ('wide', 'narrow'))
- out_state_new: float32 [3, 1152, 1152], P(None, ('wide', 'narrow'))
- up_state_new: float32 [3, 1152, 4608], P(None, ('wide', 'narrow'))
- down_state_new: float32 [3, 4608, 1152], P(None, ('wide', 'narrow'))
- bias_state_new: float32 [3, 16128], P(None, ('wide', 'narrow'))
The draws below stay inside these ranges and needn't reach their ends.
Inputs may be any that keep to these rules, and one draw needn't show every extreme that they name: Each frame's grid is (16, 16), (12, 20) or (8, 32); frame 0 has the first and frame 1 the last. `mod_state`: slot 0 holds first moments, slot 1 second moments (positive), slot 2 the weight average. `qkv_state`: slot 0 holds first moments, slot 1 second moments (positive), slot 2 the weight average. `out_state`: slot 0 holds first moments, slot 1 second moments (positive), slot 2 the weight average. `up_state`: slot 0 holds first moments, slot 1 second moments (positive), slot 2 the weight average. `down_state`: slot 0 holds first moments, slot 1 second moments (positive), slot 2 the weight average. `bias_state`: slot 0 holds first moments, slot 1 second moments (positive), slot 2 the weight average.
All inputs are finite; a program needn't handle non-finite values.
Results may differ from the reference program's by a relative error of at most 0.014.
The reference program's roundings to bfloat16 on the way count: a program that leaves them out, or rounds other values in their place, can miss the bound.
Values may be sent and summed in bfloat16 or wider, within the bound.
A program may use at most 384 MiB of HBM per device.

```python
import math
import jax
import jax.numpy as jnp
from jax import lax

D = 1152
HEADS = 16
FF = 4608
SIDE = 16
STEPS = 4
BLOCK = 256
MOD = 6912
BIAS = 16128
FRAMES = 32
CLIP = 576


def moment_scale():
    return D // 2 / math.sqrt(18.0 * D * D)


def state_draw(key, shape, grad_size, weight_size):
    first_key, second_key, third_key = jax.random.split(key, 3)
    first = jnp.clip(jax.random.normal(first_key, shape, jnp.float32), -4.0, 4.0) * grad_size
    second = jnp.exp(jax.random.uniform(second_key, shape, jnp.float32, 0.0, math.log(4.0))) * (grad_size * grad_size)
    average = jnp.clip(jax.random.normal(third_key, shape, jnp.float32), -4.0, 4.0) * weight_size
    return jnp.stack([first, second, average])


def draw_mod_state(key, part):
    return state_draw(key, (D, MOD), moment_scale(), D ** (-0.5))


def draw_qkv_state(key, part):
    return state_draw(key, (D, 3 * D), moment_scale(), D ** (-0.5))


def draw_out_state(key, part):
    return state_draw(key, (D, D), moment_scale(), (D // 32) ** (-0.5))


def draw_up_state(key, part):
    return state_draw(key, (D, FF), moment_scale(), D ** (-0.5))


def draw_down_state(key, part):
    return state_draw(key, (FF, D), moment_scale(), FF ** (-0.5))


def draw_bias_state(key, part):
    return state_draw(key, (BIAS,), 2.0 * moment_scale(), 0.2)


def draw_grid(key, part):
    kinds = jax.random.randint(key, (FRAMES,), 0, 3)
    kinds = kinds.at[0].set(0).at[1].set(2)
    heights = jnp.array([SIDE, 3 * SIDE // 4, SIDE // 2], jnp.int32)
    widths = jnp.array([SIDE, 5 * SIDE // 4, 2 * SIDE], jnp.int32)
    return jnp.stack([heights[kinds], widths[kinds]], axis=1).astype(jnp.int32)


def raised(drawn, stream_key, source, target, shards_of, factor):
    owner, partner = [(jnp.arange(drawn.shape[axis_at]) // (drawn.shape[axis_at] // shards_of)).reshape([-1 if axis == axis_at else 1 for axis in range(drawn.ndim)]) for axis_at in (source, target)]
    chosen = jax.random.permutation(stream_key, shards_of)[partner]
    strong = (owner == chosen) | (owner == (partner + shards_of // 2) % shards_of)
    return jnp.where(strong, factor * drawn, drawn)


def block_levels(key, shape, cuts, low, largest):
    loudness, own = 1.0, jax.random.fold_in(key, 6)
    for dim, blocks in cuts:
        draws = jnp.exp(jax.random.uniform(jax.random.fold_in(own, dim), (blocks,), jnp.float32, low / len(cuts), largest / len(cuts)))
        loudness = loudness * jnp.repeat(draws, shape[dim] // blocks).reshape([-1 if axis == dim else 1 for axis in range(len(shape))])
    return loudness


def gaussian(rng, shape, width, reach, pieces=(), dtype=jnp.bfloat16):
    loudness = block_levels(rng, shape, pieces, -0.22, 0.18) if pieces else 1.0
    values = jax.random.normal(rng, shape, jnp.float32) * width * loudness
    return jnp.minimum(jnp.maximum(values, -reach), reach).astype(dtype)


def noise_with(key, dims, deviation, most, cuts, heavy, held_as=jnp.bfloat16):
    values = deviation * jax.random.normal(key, dims, jnp.float32)
    if cuts:
        values = values * block_levels(key, dims, cuts, -0.22, 0.18)
    return jnp.clip(raised(values, jax.random.fold_in(key, 3), *heavy), -most, most).astype(held_as)


def setup_inputs(seed: int = 0) -> dict:
    splits = jax.random.split(jax.random.key(seed), 17)
    frames_in = noise_with(splits[0], (FRAMES, BLOCK, D), 1.0, 6.0, ((0, 32),), (0, 2, 32, 2.75))
    conditioning = gaussian(splits[1], (FRAMES, D), 1.0, 5.0, ((0, 32),))
    grid = draw_grid(jax.random.fold_in(splits[16], 71), 0)
    cotangent = gaussian(splits[3], (FRAMES, BLOCK, D), 1.0, 6.0, ((0, 32),))
    mod_weight = gaussian(splits[4], (D, MOD), D ** -0.5, 0.1875, ((0, 32),), jnp.float32)
    qkv_weight = gaussian(splits[5], (D, 3 * D), D ** -0.5, 0.1875, ((0, 32),), jnp.float32)
    out_weight = gaussian(splits[6], (D, D), (D // 32) ** -0.5, 1.0, ((0, 32),), jnp.float32)
    up_weight = gaussian(splits[7], (D, FF), D ** -0.5, 0.1875, ((0, 32),), jnp.float32)
    down_weight = gaussian(splits[8], (FF, D), FF ** -0.5, 0.09375, ((0, 32),), jnp.float32)
    biases = gaussian(splits[9], (BIAS,), 0.2, 1.2, ((0, 32),), jnp.float32)
    mod_state = draw_mod_state(jax.random.fold_in(splits[16], 71), 0)
    qkv_state = draw_qkv_state(jax.random.fold_in(splits[16], 71), 0)
    out_state = draw_out_state(jax.random.fold_in(splits[16], 71), 0)
    up_state = draw_up_state(jax.random.fold_in(splits[16], 71), 0)
    down_state = draw_down_state(jax.random.fold_in(splits[16], 71), 0)
    bias_state = draw_bias_state(jax.random.fold_in(splits[16], 71), 0)
    return {"frames_in": frames_in, "conditioning": conditioning, "grid": grid, "cotangent": cotangent, "mod_weight": mod_weight, "qkv_weight": qkv_weight, "out_weight": out_weight, "up_weight": up_weight, "down_weight": down_weight, "biases": biases, "mod_state": mod_state, "qkv_state": qkv_state, "out_state": out_state, "up_state": up_state, "down_state": down_state, "bias_state": bias_state}


@jax.custom_vjp
def low(v):
    return lax.optimization_barrier(v.astype(jnp.bfloat16)).astype(jnp.float32)

@jax.custom_vjp
def low_back(v):
    return v

def low_keep(v):
    return (low(v), None)

def low_pass(kept, grad):
    return (grad,)

def back_keep(v):
    return (v, None)

def back_low(kept, grad):
    return (low(grad),)
low.defvjp(low_keep, low_pass)
low_back.defvjp(back_keep, back_low)
HIGHEST = lax.Precision.HIGHEST
NORM_EPS = 1e-06
RATE = 0.04
FIRST_DECAY = 0.5
SECOND_DECAY = 0.5
WEIGHT_DECAY = 0.1
ADAM_EPS = 1e-08
AVERAGE_DECAY = 0.9999
MASK_VALUE = -1e+30

def layer_norm(values):
    centre = lax.optimization_barrier(jnp.mean(values, axis=-1, keepdims=True))
    centred = values - centre
    spread = lax.optimization_barrier(jnp.mean(centred * centred, axis=-1, keepdims=True))
    return centred * lax.rsqrt(spread + NORM_EPS)

def modulate(values, shift_part, scale_part):
    return layer_norm(values) * (1.0 + scale_part) + shift_part

def silu_act(values):
    return values * jax.nn.sigmoid(values)

def gelu_tanh(values):
    inner = 0.7978845608028654 * (values + 0.044715 * values * values * values)
    return 0.5 * values * (1.0 + jnp.tanh(inner))

def slot_mask(grid, frame_len):
    area = grid[:, 0] * grid[:, 1]
    return lax.broadcasted_iota(jnp.int32, (grid.shape[0], frame_len), 1) < area[:, None]

def split_biases(biases, model_width, hidden_width):
    edges = [6 * model_width, 7 * model_width, 8 * model_width, 9 * model_width, 9 * model_width + hidden_width]
    return jnp.split(biases, edges)

def adam_update(weight, state, grad):
    first = FIRST_DECAY * state[0] + (1.0 - FIRST_DECAY) * grad
    second = SECOND_DECAY * state[1] + (1.0 - SECOND_DECAY) * grad * grad
    first_hat = first / (1.0 - FIRST_DECAY ** STEPS)
    second_hat = second / (1.0 - SECOND_DECAY ** STEPS)
    new_weight = weight - RATE * (first_hat / (jnp.sqrt(second_hat) + ADAM_EPS) + WEIGHT_DECAY * weight)
    average = AVERAGE_DECAY * state[2] + (1.0 - AVERAGE_DECAY) * new_weight
    return (new_weight, jnp.stack([first, second, average]))

def frame_group(lowered, frames_part, cond_part, valid_part):
    mod_low, qkv_low, out_low, up_low, down_low, bias_low = lowered
    frame_count, frame_len, model_width = frames_part.shape
    hidden_width = up_low.shape[1]
    head_size = model_width // HEADS
    mod_bias, query_bias, value_bias, out_bias, up_bias, down_bias = split_biases(bias_low, model_width, hidden_width)
    modulation = low_back(jnp.dot(low(silu_act(cond_part)), mod_low, precision=HIGHEST) + mod_bias)
    shift_attn, scale_attn, gate_attn, shift_mlp, scale_mlp, gate_mlp = jnp.split(modulation[:, None, :], 6, axis=-1)
    norm_one = low(modulate(frames_part, shift_attn, scale_attn))
    qkv_bias = jnp.concatenate([query_bias, jnp.zeros_like(query_bias), value_bias])
    qkv_vals = low(low_back(jnp.einsum('fbd,de->fbe', norm_one, qkv_low, precision=HIGHEST) + qkv_bias))
    split_heads = qkv_vals.reshape(frame_count, frame_len, 3, HEADS, head_size)
    query_heads = split_heads[:, :, 0]
    key_heads = split_heads[:, :, 1]
    value_heads = split_heads[:, :, 2]
    raw_scores = low_back(jnp.einsum('fqhs,fkhs->fhqk', query_heads, key_heads, precision=HIGHEST) * head_size ** (-0.5))
    scores = jnp.where(valid_part[:, None, None, :], raw_scores, MASK_VALUE)
    row_max = lax.optimization_barrier(jnp.max(scores, axis=-1, keepdims=True))
    exponent = jnp.exp(scores - row_max)
    attention = low(exponent / lax.optimization_barrier(jnp.sum(exponent, axis=-1, keepdims=True)))
    attended = jnp.einsum('fhqk,fkhs->fqhs', attention, value_heads, precision=HIGHEST)
    attended = low(low_back(attended.reshape(frame_count, frame_len, model_width)))
    branch = low_back(jnp.einsum('fbd,de->fbe', attended, out_low, precision=HIGHEST) + out_bias)
    midway = frames_part + gate_attn * branch
    norm_two = low(modulate(midway, shift_mlp, scale_mlp))
    up_values = low_back(jnp.einsum('fbd,de->fbe', norm_two, up_low, precision=HIGHEST) + up_bias)
    activated = low(gelu_tanh(up_values))
    down_values = low_back(jnp.einsum('fbe,ed->fbd', activated, down_low, precision=HIGHEST) + down_bias)
    return jnp.where(valid_part[:, :, None], midway + gate_mlp * down_values, 0.0)

def reference(frames_in, conditioning, grid, cotangent, mod_weight, qkv_weight, out_weight, up_weight, down_weight, biases, mod_state, qkv_state, out_state, up_state, down_state, bias_state):
    masters = (mod_weight, qkv_weight, out_weight, up_weight, down_weight, biases)
    states = (mod_state, qkv_state, out_state, up_state, down_state, bias_state)
    frame_count, frame_len, model_width = frames_in.shape
    valid_slots = slot_mask(grid, frame_len)
    groups = frame_count // 16
    group_fn = jax.checkpoint(frame_group)

    def whole(params, frames_f, cond_f):
        lowered = tuple((low(member) for member in params))
        stacked = (frames_f.reshape(groups, 16, frame_len, model_width), cond_f.reshape(groups, 16, model_width), valid_slots.reshape(groups, 16, frame_len))
        result = lax.map(lambda parts: group_fn(lowered, parts[0], parts[1], parts[2]), stacked)
        return result.reshape(frame_count, frame_len, model_width)
    block_out, pullback = jax.vjp(whole, masters, frames_in.astype(jnp.float32), conditioning.astype(jnp.float32))
    raw_grads, frames_grad, cond_grad = pullback(cotangent.astype(jnp.float32))
    total_sq = sum((jnp.sum(member * member) for member in raw_grads))
    grad_norm = jnp.sqrt(total_sq)
    factor = jnp.minimum(1.0, CLIP / (grad_norm + 1e-06))
    clipped = tuple((member * factor for member in raw_grads))
    updated = [adam_update(masters[index], states[index], clipped[index]) for index in range(6)]
    return (block_out.astype(jnp.bfloat16), frames_grad.astype(jnp.bfloat16), cond_grad, grad_norm, clipped[0], clipped[1], clipped[2], clipped[3], clipped[4], clipped[5], updated[0][0], updated[1][0], updated[2][0], updated[3][0], updated[4][0], updated[5][0], updated[0][1], updated[1][1], updated[2][1], updated[3][1], updated[4][1], updated[5][1])
```

```python
import functools
import jax
import jax.numpy as jnp
from jax import lax
from jax.experimental import pallas as pl
from jax.experimental.pallas import tpu as pltpu
from jax.sharding import PartitionSpec as P

HEADS = 16
STEPS = 4
CLIP = 576
NORM_EPS = 1e-06
RATE = 0.04
FIRST_DECAY = 0.5
SECOND_DECAY = 0.5
WEIGHT_DECAY = 0.1
ADAM_EPS = 1e-08
AVERAGE_DECAY = 0.9999
MASK_VALUE = -1e30
AXES = ("wide", "narrow")

MESH = pl.DeviceIdType.MESH
CORE = 1


def orders(bits, late):
    high = list(range(bits - 1, 2, -1))
    if late:
        pair = (high[:-1] + [0, 2] + high[-1:], high[:-1] + [2, 0] + high[-1:])
    else:
        pair = (high + [2, 0], high + [0, 2])
    return tuple(order + [CORE] for order in pair)


def masks(order, member):
    return sum(1 << bit for place, bit in enumerate(order) if member >> place & 1)


def me_index():
    return lax.axis_index("wide") * 2 + lax.axis_index("narrow")


def device(index):
    return (index // 2, lax.rem(index, 2))


def own_plane(me):
    return lax.rem(me // 2, 2)


def flip(index, mask):
    out = index
    bit = 0
    while mask >> bit:
        if mask >> bit & 1:
            value = lax.rem(out // (1 << bit), 2)
            out = out + (1 << bit) * (1 - 2 * value)
        bit += 1
    return out


def block_of(me, pair, member, bits):
    plane = own_plane(me)
    last = 1 << (bits - 1)
    if member & last:
        rest = member - last
        zero = flip(flip(me, 1 << CORE), masks(pair[1], rest))
        one = flip(flip(me, 1 << CORE), masks(pair[0], rest))
    else:
        zero = flip(me, masks(pair[0], member))
        one = flip(me, masks(pair[1], member))
    return jnp.where(plane == 0, zero, one)


def partner_of(me, pair, place):
    zero = flip(me, 1 << pair[0][place])
    if pair[0][place] == pair[1][place]:
        return zero
    return jnp.where(own_plane(me) == 0, zero, flip(me, 1 << pair[1][place]))


def greet(me, bits):
    barrier = pltpu.get_barrier_semaphore()
    partners = [flip(me, 1 << bit) for bit in range(bits)] + [flip(me, 3)]
    for partner in partners:
        pl.semaphore_signal(barrier, inc=1, device_id=device(partner), device_id_type=MESH)
    pl.semaphore_wait(barrier, len(partners))


def top_place(member):
    return member.bit_length() - 1


def gather_kernel(bits, rows, lates, a_src, b_src, c_src, a_out, b_out, c_out,
                  stage, block, c_block, quad_send, quad_recv, own_sem, keep_sem, send_sem, recv_sem):
    count = 1 << bits
    me = me_index()
    quad, spot = lax.rem(me, 4), me // 4
    pairs = [orders(bits, late) for late in lates]
    outs = (a_out, b_out, c_out)

    def place(kind, index):
        q, j = lax.rem(index, 4), index // 4
        return outs[kind].at[q, j] if kind < 2 else outs[kind].at[j, q]

    def send(kind, member, step, source):
        target = member | 1 << step
        return pltpu.make_async_remote_copy(
            src_ref=source,
            dst_ref=place(kind, block_of(me, pairs[kind], member, bits)),
            send_sem=send_sem.at[kind, target],
            recv_sem=recv_sem.at[kind, target],
            device_id=device(partner_of(me, pairs[kind], step)),
            device_id_type=MESH,
        )

    own = []
    for kind, source in enumerate((a_src, b_src)):
        own.append(pltpu.make_async_copy(source.at[quad], stage.at[kind, quad], own_sem.at[kind]))
    own.append(pltpu.make_async_copy(c_src, c_block, own_sem.at[2]))
    for copy in own:
        copy.start()
    greet(me, bits)
    quads = []
    for kind, source in enumerate((a_src, b_src)):
        for other in (1, 2, 3):
            copy = pltpu.make_async_remote_copy(
                src_ref=source.at[flip(quad, other)],
                dst_ref=stage.at[kind, quad],
                send_sem=quad_send.at[kind, other],
                recv_sem=quad_recv.at[kind, other],
                device_id=device(flip(me, other)),
                device_id_type=MESH,
            )
            copy.start()
            quads.append(copy)
    sends = []
    keeps = []

    def launch(kind, member, source):
        for step in range(top_place(member) + 1, bits):
            copy = send(kind, member, step, source)
            copy.start()
            sends.append(copy)

    def keep(kind, source):
        copy = pltpu.make_async_copy(source, place(kind, me), keep_sem.at[kind])
        copy.start()
        keeps.append(copy)

    own[2].wait()
    launch(2, 0, c_block)
    keep(2, c_block)
    padded = block.shape[1]
    for kind in (0, 1):
        own[kind].wait()
        for copy in quads[3 * kind:3 * kind + 3]:
            copy.wait_recv()
        for lane in range(0, stage.shape[3], 128):
            parts = [stage[kind, q, :, lane:lane + 128].astype(jnp.float32) for q in range(4)]
            if padded > 4 * rows:
                parts.append(jnp.zeros((padded - 4 * rows, 128), jnp.float32))
            block[kind, :, lane:lane + 128] = jnp.concatenate(parts, axis=0).astype(jnp.bfloat16)
        launch(kind, 0, block.at[kind])
        keep(kind, block.at[kind])

    def arrived(kind, member):
        spot_ref = place(kind, block_of(me, pairs[kind], member, bits))
        pltpu.make_async_copy(spot_ref, spot_ref, recv_sem.at[kind, member]).wait()
        return spot_ref

    for member in range(1, count):
        for kind in (2, 0, 1):
            launch(kind, member, arrived(kind, member))
    for copy in sends + quads:
        copy.wait_send()
    for copy in keeps:
        copy.wait()


def gather(a_src, b_src, c_src, count, lates=(False, False, False)):
    bits = count.bit_length() - 1
    rows, columns = a_src.shape[1:]
    padded = -(-4 * rows // 16) * 16
    c_padded = -(-c_src.shape[0] // 16) * 16
    if c_padded != c_src.shape[0]:
        c_src = jnp.pad(c_src, ((0, c_padded - c_src.shape[0]), (0, 0)))
    kinds = 3
    anywhere = pl.BlockSpec(memory_space=pl.ANY)
    big = jax.ShapeDtypeStruct((4, count // 4, padded, columns), jnp.bfloat16)
    tall = jax.ShapeDtypeStruct((count // 4, 4, c_padded, columns), jnp.bfloat16)
    a_all, b_all, c_all = pl.pallas_call(
        functools.partial(gather_kernel, bits, rows, lates),
        out_shape=(big, big, tall),
        in_specs=[anywhere] * 3,
        out_specs=(anywhere,) * 3,
        scratch_shapes=[
            pltpu.VMEM((2, 4, rows, columns), jnp.bfloat16),
            pltpu.VMEM((2, padded, columns), jnp.bfloat16),
            pltpu.VMEM((c_padded, columns), jnp.bfloat16),
            pltpu.SemaphoreType.DMA((2, 4)),
            pltpu.SemaphoreType.DMA((2, 4)),
            pltpu.SemaphoreType.DMA((3,)),
            pltpu.SemaphoreType.DMA((3,)),
            pltpu.SemaphoreType.DMA((kinds, count)),
            pltpu.SemaphoreType.DMA((kinds, count)),
        ],
        compiler_params=pltpu.CompilerParams(collective_id=0, has_side_effects=True),
        cost_estimate=pl.CostEstimate(flops=0, bytes_accessed=400_000_000, transcendentals=0),
        name="gather_weights",
    )(a_src, b_src, c_src)
    return a_all, b_all, c_all


def reduce_kernel(bits, rows, lates, a_in, b_in, c_in, a_out, b_out, c_out,
                  own, recv, quad_block, total, own_sem, send_sem, recv_sem, quad_send, quad_recv, quad_own, total_sem):
    count = 1 << bits
    half = count // 2
    me = me_index()
    quad = lax.rem(me, 4)
    pairs = [orders(bits, late) for late in lates]
    ins = (a_in, b_in, c_in)
    kinds = (2, 1, 0)

    def place(kind, index):
        q, j = lax.rem(index, 4), index // 4
        return ins[kind].at[q, j] if kind < 2 else ins[kind].at[j, q]

    loads = {}
    for member in range(half - 1, -1, -1):
        for kind in kinds:
            loads[kind, member] = pltpu.make_async_copy(
                place(kind, block_of(me, pairs[kind], member, bits)), own.at[kind, member], own_sem.at[kind, member]
            )
    sends = []

    def send(kind, member, source):
        step = top_place(member)
        copy = pltpu.make_async_remote_copy(
            src_ref=source,
            dst_ref=recv.at[kind, member],
            send_sem=send_sem.at[kind, member],
            recv_sem=recv_sem.at[kind, member],
            device_id=device(partner_of(me, pairs[kind], step)),
            device_id_type=MESH,
        )
        copy.start()
        sends.append(copy)

    for kind in kinds:
        loads[kind, half - 1].start()
    greet(me, bits)
    for member in range(half - 1, -1, -1):
        for kind in kinds:
            send(kind, member + half, place(kind, block_of(me, pairs[kind], member + half, bits)))
            if member < half - 1:
                loads[kind, member].start()

    padded, columns = own.shape[2:]

    def ready(kind, member):
        loads[kind, member].wait()
        parts = [member | 1 << step for step in range(top_place(member) + 1, bits)]
        for part in parts:
            pltpu.make_async_copy(recv.at[kind, part], recv.at[kind, part], recv_sem.at[kind, part]).wait()
        return parts

    def summed(kind, member, parts, where):
        value = own[kind, member, where, :].astype(jnp.float32)
        for part in parts:
            value = value + recv[kind, part, where, :].astype(jnp.float32)
        return value

    for member in range(half - 1, 0, -1):
        for kind in kinds:
            parts = ready(kind, member)

            def strip(s, carry, kind=kind, member=member, parts=parts):
                where = pl.ds(pl.multiple_of(s * 16, 16), 16)
                own[kind, member, where, :] = summed(kind, member, parts, where).astype(jnp.bfloat16)
                return carry

            lax.fori_loop(0, padded // 16, strip, 0)
            send(kind, member, own.at[kind, member])

    copies = []
    for kind in kinds:
        parts = ready(kind, 0)

        def strip(s, carry, kind=kind, parts=parts):
            where = pl.ds(pl.multiple_of(s * 16, 16), 16)
            total[kind, where, :] = summed(kind, 0, parts, where)
            return carry

        lax.fori_loop(0, padded // 16, strip, 0)
        if kind == 2:
            copy = pltpu.make_async_copy(total.at[2], c_out, total_sem)
            copy.start()
            copies.append(copy)
            continue
        out = (a_out, b_out)[kind]
        for lane in range(0, columns, 128):
            for q in range(4):
                quad_block[kind, q, :, lane:lane + 128] = total[kind, q * rows:(q + 1) * rows, lane:lane + 128].astype(jnp.bfloat16)
        copy = pltpu.make_async_copy(quad_block.at[kind, quad], out.at[quad], quad_own.at[kind])
        copy.start()
        copies.append(copy)
        for other in (1, 2, 3):
            copy = pltpu.make_async_remote_copy(
                src_ref=quad_block.at[kind, flip(quad, other)],
                dst_ref=out.at[quad],
                send_sem=quad_send.at[kind, other],
                recv_sem=quad_recv.at[kind, other],
                device_id=device(flip(me, other)),
                device_id_type=MESH,
            )
            copy.start()
            copies.append(copy)
    for copy in copies:
        copy.wait()
    for copy in sends:
        copy.wait_send()


def reduce(a_in, b_in, c_in, rows, lates=(False, False, False)):
    count = a_in.shape[1] * 4
    bits = count.bit_length() - 1
    padded, columns = a_in.shape[2:]
    anywhere = pl.BlockSpec(memory_space=pl.ANY)
    share = jax.ShapeDtypeStruct((4, rows, columns), jnp.bfloat16)
    return pl.pallas_call(
        functools.partial(reduce_kernel, bits, rows, lates),
        out_shape=(share, share, jax.ShapeDtypeStruct((padded, columns), jnp.float32)),
        in_specs=[anywhere] * 3,
        out_specs=(anywhere,) * 3,
        scratch_shapes=[
            pltpu.VMEM((3, count // 2, padded, columns), jnp.bfloat16),
            pltpu.VMEM((3, count, padded, columns), jnp.bfloat16),
            pltpu.VMEM((2, 4, rows, columns), jnp.bfloat16),
            pltpu.VMEM((3, padded, columns), jnp.float32),
            pltpu.SemaphoreType.DMA((3, count // 2)),
            pltpu.SemaphoreType.DMA((3, count)),
            pltpu.SemaphoreType.DMA((3, count)),
            pltpu.SemaphoreType.DMA((2, 4)),
            pltpu.SemaphoreType.DMA((2, 4)),
            pltpu.SemaphoreType.DMA((2,)),
            pltpu.SemaphoreType.DMA,
        ],
        compiler_params=pltpu.CompilerParams(collective_id=1, has_side_effects=True, vmem_limit_bytes=62 * 1024 * 1024),
        cost_estimate=pl.CostEstimate(flops=0, bytes_accessed=400_000_000, transcendentals=0),
        name="reduce_gradients",
    )(a_in, b_in, c_in)


def layer_norm(values):
    centre = jnp.mean(values, axis=-1, keepdims=True)
    centred = values - centre
    spread = jnp.mean(centred * centred, axis=-1, keepdims=True)
    return centred * lax.rsqrt(spread + NORM_EPS)


def modulate(values, shift_part, scale_part):
    return layer_norm(values) * (1.0 + scale_part) + shift_part


def silu_act(values):
    return values * jax.nn.sigmoid(values)


def gelu_tanh(values):
    inner = 0.7978845608028654 * (values + 0.044715 * values * values * values)
    return 0.5 * values * (1.0 + jnp.tanh(inner))


def slot_mask(grid, frame_len):
    area = grid[:, 0] * grid[:, 1]
    return lax.broadcasted_iota(jnp.int32, (grid.shape[0], frame_len), 1) < area[:, None]


def split_biases(biases, model_width, hidden_width):
    edges = [
        6 * model_width,
        7 * model_width,
        8 * model_width,
        9 * model_width,
        9 * model_width + hidden_width,
    ]
    return jnp.split(biases, edges)


def adam_update(weight, state, grad):
    first = FIRST_DECAY * state[0] + (1.0 - FIRST_DECAY) * grad
    second = SECOND_DECAY * state[1] + (1.0 - SECOND_DECAY) * grad * grad
    first_hat = first / (1.0 - FIRST_DECAY**STEPS)
    second_hat = second / (1.0 - SECOND_DECAY**STEPS)
    new_weight = weight - RATE * (
        first_hat / (jnp.sqrt(second_hat) + ADAM_EPS) + WEIGHT_DECAY * weight
    )
    average = AVERAGE_DECAY * state[2] + (1.0 - AVERAGE_DECAY) * new_weight
    return (new_weight, jnp.stack([first, second, average]))


def attention_scores(query_heads, key_heads, valid_slots, score_scale):
    scores = (
        jnp.einsum("fqhs,fkhs->fhqk", query_heads, key_heads, preferred_element_type=jnp.float32)
        * score_scale
    )
    return jnp.where(valid_slots[:, None, None, :], scores, MASK_VALUE)


def token_sum(values):
    return jnp.sum(values, axis=(0, 1), dtype=jnp.float32)


def exchange(packets):
    return lax.all_to_all(packets, AXES, split_axis=0, concat_axis=0, tiled=True)


def shards(
    frames_in,
    conditioning,
    grid,
    cotangent,
    mod_weight,
    qkv_weight,
    out_weight,
    up_weight,
    down_weight,
    biases,
    mod_state,
    qkv_state,
    out_state,
    up_state,
    down_state,
    bias_state,
):
    frame_count, frame_len, model_width = frames_in.shape
    hidden_width = up_weight.shape[1]
    head_size = model_width // HEADS
    score_scale = head_size ** (-0.5)
    head_shape = (frame_count, frame_len, HEADS, head_size)
    count = lax.axis_size("wide") * lax.axis_size("narrow")
    rows = mod_weight.shape[0]
    tall_rows = down_weight.shape[0]
    low = jnp.bfloat16

    def slices(member):
        return member.reshape(rows, 4, model_width).transpose(1, 0, 2)

    a_src = slices(jnp.concatenate([qkv_weight.astype(low), out_weight.astype(low)], axis=1))
    b_src = slices(up_weight.astype(low))
    a_all, b_all, c_all = gather(a_src, b_src, down_weight.astype(low), count, (False, False, True))
    a_all = a_all[:, :, : 4 * rows].reshape(4, model_width, model_width)
    up_low = b_all[:, :, : 4 * rows].reshape(4, model_width, model_width)
    down_low = c_all[:, :, :tall_rows].reshape(hidden_width, model_width)
    query_low, key_low, value_low, out_low = (a_all[index] for index in range(4))

    cond_f = conditioning.astype(jnp.float32)
    silu_low = silu_act(cond_f).astype(low)
    mod_low = mod_weight.astype(low)
    first = exchange(
        jnp.concatenate(
            [
                silu_low.reshape(count, rows),
                jnp.broadcast_to(biases.astype(low)[None], (count, biases.shape[0])),
            ],
            axis=1,
        )
    )
    silu_rows = first[:, :rows]
    bias_low = first[:, rows:].reshape(-1)
    mod_terms = exchange(jnp.dot(silu_rows, mod_low, preferred_element_type=jnp.float32))
    mod_bias, query_bias, value_bias, out_bias, up_bias, down_bias = split_biases(
        bias_low.astype(jnp.float32), model_width, hidden_width
    )
    modulation = jnp.sum(mod_terms, axis=0, keepdims=True) + mod_bias
    valid_slots = slot_mask(grid, frame_len)
    row_mask = valid_slots[:, :, None].astype(jnp.float32)
    frames_f = frames_in.astype(jnp.float32)
    shift_attn, scale_attn, gate_attn, shift_mlp, scale_mlp, gate_mlp = jnp.split(
        modulation[:, None, :], 6, axis=-1
    )
    norm_one = modulate(frames_f, shift_attn, scale_attn).astype(low)

    def project(values, weight):
        return jnp.einsum("fbd,de->fbe", values, weight, preferred_element_type=jnp.float32)

    query_heads = (project(norm_one, query_low) + query_bias).astype(low).reshape(head_shape)
    key_heads = project(norm_one, key_low).astype(low).reshape(head_shape)
    value_heads = (project(norm_one, value_low) + value_bias).astype(low).reshape(head_shape)
    scores = attention_scores(query_heads, key_heads, valid_slots, score_scale)
    row_max = jnp.max(scores, axis=-1, keepdims=True)
    exponent = jnp.exp(scores - row_max)
    row_total = jnp.sum(exponent, axis=-1, keepdims=True)
    log_total = row_max + jnp.log(row_total)
    attention = (exponent / row_total).astype(low)
    attended = jnp.einsum(
        "fhqk,fkhs->fqhs", attention, value_heads, preferred_element_type=jnp.float32
    )
    attended = attended.reshape(frame_count, frame_len, model_width).astype(low)
    branch = project(attended, out_low) + out_bias
    midway = frames_f + gate_attn * branch
    norm_two = modulate(midway, shift_mlp, scale_mlp).astype(low)
    up_values = (
        jnp.einsum("fbd,sde->fbse", norm_two, up_low, preferred_element_type=jnp.float32).reshape(
            frame_count, frame_len, hidden_width
        )
        + up_bias
    )
    activated = gelu_tanh(up_values).astype(low)
    down_values = project(activated, down_low) + down_bias
    block_out = ((midway + gate_mlp * down_values) * row_mask).astype(low)
    upstream = cotangent.astype(jnp.float32) * row_mask
    d_gate_mlp = jnp.sum(upstream * down_values, axis=1, keepdims=True)
    d_down = (upstream * gate_mlp).astype(low)
    grad_down = jnp.einsum("fbe,fbd->ed", activated, d_down, preferred_element_type=jnp.float32)
    grad_down_bias = token_sum(d_down)
    d_activated = jnp.einsum("fbd,ed->fbe", d_down, down_low, preferred_element_type=jnp.float32)
    gelu_pull = jax.vjp(gelu_tanh, up_values)[1]
    d_up = gelu_pull(d_activated)[0].astype(low)
    d_up_parts = d_up.reshape(frame_count, frame_len, 4, model_width)
    grad_up = jnp.einsum("fbd,fbse->sde", norm_two, d_up_parts, preferred_element_type=jnp.float32)
    grad_up_bias = token_sum(d_up)
    d_norm_two = jnp.einsum("fbse,sde->fbd", d_up_parts, up_low, preferred_element_type=jnp.float32)
    second_pull = jax.vjp(modulate, midway, shift_mlp, scale_mlp)[1]
    d_midway, d_shift_mlp, d_scale_mlp = second_pull(d_norm_two)
    d_midway = d_midway + upstream
    d_gate_attn = jnp.sum(d_midway * branch, axis=1, keepdims=True)
    d_branch = (d_midway * gate_attn).astype(low)
    grad_out = jnp.einsum("fbd,fbe->de", attended, d_branch, preferred_element_type=jnp.float32)
    grad_out_bias = token_sum(d_branch)
    d_attended = jnp.einsum("fbe,de->fbd", d_branch, out_low, preferred_element_type=jnp.float32)
    d_attended = d_attended.astype(low).reshape(head_shape)
    scores = attention_scores(query_heads, key_heads, valid_slots, score_scale)
    soft = jnp.exp(scores - log_total)
    d_soft = jnp.einsum(
        "fqhs,fkhs->fhqk", d_attended, value_heads, preferred_element_type=jnp.float32
    )
    d_value_heads = jnp.einsum(
        "fhqk,fqhs->fkhs", attention, d_attended, preferred_element_type=jnp.float32
    )
    d_scores = (soft * (d_soft - jnp.sum(soft * d_soft, axis=-1, keepdims=True))).astype(low)
    d_query_heads = (
        jnp.einsum("fhqk,fkhs->fqhs", d_scores, key_heads, preferred_element_type=jnp.float32)
        * score_scale
    )
    d_key_heads = (
        jnp.einsum("fhqk,fqhs->fkhs", d_scores, query_heads, preferred_element_type=jnp.float32)
        * score_scale
    )
    flat_shape = (frame_count, frame_len, model_width)
    d_query = d_query_heads.reshape(flat_shape).astype(low)
    d_key = d_key_heads.reshape(flat_shape).astype(low)
    d_value = d_value_heads.reshape(flat_shape).astype(low)
    grad_query, grad_key, grad_value = (
        jnp.einsum("fbd,fbe->de", norm_one, member, preferred_element_type=jnp.float32)
        for member in (d_query, d_key, d_value)
    )
    grad_query_bias = token_sum(d_query)
    grad_value_bias = token_sum(d_value)
    d_norm_one = sum(
        jnp.einsum("fbe,de->fbd", member, weight, preferred_element_type=jnp.float32)
        for member, weight in ((d_query, query_low), (d_key, key_low), (d_value, value_low))
    )
    first_pull = jax.vjp(modulate, frames_f, shift_attn, scale_attn)[1]
    d_frames, d_shift_attn, d_scale_attn = first_pull(d_norm_one)
    frames_grad = (d_frames + d_midway).astype(low)
    d_modulation = jnp.concatenate(
        [d_shift_attn, d_scale_attn, d_gate_attn, d_shift_mlp, d_scale_mlp, d_gate_mlp], axis=-1
    )[:, 0, :].astype(low)
    grad_mod_bias = d_modulation[0].astype(jnp.float32)
    grad_bias = jnp.concatenate(
        [
            grad_mod_bias,
            grad_query_bias,
            grad_value_bias,
            grad_out_bias,
            grad_up_bias,
            grad_down_bias,
        ]
    )
    terms = exchange(
        jnp.concatenate(
            [
                jnp.broadcast_to(d_modulation, (count, d_modulation.shape[1])),
                grad_bias.reshape(count, -1).astype(low),
            ],
            axis=1,
        )
    )
    d_mod_all, bias_terms = terms[:, : d_modulation.shape[1]], terms[:, d_modulation.shape[1] :]

    def grouped(member, group_rows):
        member = member.astype(low).reshape(4, count // 4, 4 * rows, model_width)
        return jnp.pad(member, ((0, 0), (0, 0), (0, group_rows - 4 * rows), (0, 0)))

    group_rows = -(-4 * rows // 16) * 16
    tall_group = -(-tall_rows // 16) * 16
    a_sum, b_sum, c_sum = reduce(
        grouped(jnp.stack([grad_query, grad_key, grad_value, grad_out]), group_rows),
        grouped(grad_up, group_rows),
        jnp.pad(
            grad_down.astype(low).reshape(count // 4, 4, tall_rows, model_width),
            ((0, 0), (0, 0), (0, tall_group - tall_rows), (0, 0)),
        ),
        rows,
        (True, False, False),
    )
    red_mod = lax.dot_general(
        silu_rows, d_mod_all, (((0,), (0,)), ((), ())), preferred_element_type=jnp.float32
    )
    a_sum = a_sum.astype(jnp.float32)
    red_qkv = a_sum[:3].transpose(1, 0, 2).reshape(rows, 3 * model_width)
    red_out = a_sum[3]
    red_up = b_sum.astype(jnp.float32).transpose(1, 0, 2).reshape(rows, hidden_width)
    red_down = c_sum[:tall_rows]
    red_bias = jnp.sum(bias_terms.astype(jnp.float32), axis=0)
    d_silu = lax.dot_general(
        d_mod_all, mod_low, (((1,), (1,)), ((), ())), preferred_element_type=jnp.float32
    )
    reduced = (red_mod, red_qkv, red_out, red_up, red_down, red_bias)
    partial_sq = sum((jnp.sum(member * member) for member in reduced))
    last = exchange(
        jnp.concatenate([d_silu, jnp.broadcast_to(partial_sq, (count, 1))], axis=1)
    )
    total_sq = jnp.sum(last[:, rows])
    silu_pull = jax.vjp(silu_act, cond_f)[1]
    cond_grad = silu_pull(last[:, :rows].reshape(1, model_width))[0]
    grad_norm = jnp.sqrt(total_sq)
    factor = jnp.minimum(1.0, CLIP / (grad_norm + 1e-06))
    clipped = tuple((member * factor for member in reduced))
    masters = (mod_weight, qkv_weight, out_weight, up_weight, down_weight, biases)
    states = (mod_state, qkv_state, out_state, up_state, down_state, bias_state)
    updated = [adam_update(masters[index], states[index], clipped[index]) for index in range(6)]
    return (
        (block_out, frames_grad, cond_grad, grad_norm)
        + clipped
        + tuple(pair[0] for pair in updated)
        + tuple(pair[1] for pair in updated)
    )


def solution(mesh):
    tokens = P(AXES, None, None)
    matrix = P(AXES, None)
    vector = P(AXES)
    state = P(None, AXES, None)
    weights = (matrix,) * 5 + (vector,)
    states = (state,) * 5 + (P(None, AXES),)
    return jax.shard_map(
        shards,
        mesh=mesh,
        in_specs=(tokens, matrix, matrix, tokens) + weights + states,
        out_specs=(tokens, tokens, matrix, P()) + weights + weights + states,
        check_vma=False,
    )
```

```python
import functools
import jax
import jax.numpy as jnp
from jax import lax
from jax.experimental import pallas as pl
from jax.experimental.pallas import tpu as pltpu
from jax.sharding import PartitionSpec as P

HEADS = 16
STEPS = 4
CLIP = 576
NORM_EPS = 1e-06
RATE = 0.04
FIRST_DECAY = 0.5
SECOND_DECAY = 0.5
WEIGHT_DECAY = 0.1
ADAM_EPS = 1e-08
AVERAGE_DECAY = 0.9999
MASK_VALUE = -1e30
AXES = ("wide", "narrow")

MESH = pl.DeviceIdType.MESH
CORE = 1
ROUND = 16


def orders(bits, late):
    high = list(range(bits - 1, 2, -1))
    if late:
        pair = (high[:-1] + [0, 2] + high[-1:], high[:-1] + [2, 0] + high[-1:])
    else:
        pair = (high + [2, 0], high + [0, 2])
    return tuple(order + [CORE] for order in pair)


def top_place(member):
    return member.bit_length() - 1


def quotient(value, by):
    return lax.div(value, jnp.int32(by))


def remainder(value, by):
    return lax.rem(value, jnp.int32(by))


class Spots:
    def __init__(self, bits):
        wide, narrow = lax.axis_index("wide"), lax.axis_index("narrow")
        self.bits = bits
        self.me = wide * 2 + narrow
        self.quad = remainder(self.me, 4)
        self.group = quotient(self.me, 4)
        self.digit = [remainder(quotient(self.me, 1 << bit), 2) for bit in range(bits)]
        self.core = self.digit[CORE]
        self.delta = [(1 << bit) * (1 - 2 * self.digit[bit]) for bit in range(bits)]
        self.device = [
            (wide, 1 - narrow) if bit == 0 else (wide + (1 << bit - 1) * (1 - 2 * self.digit[bit]), narrow)
            for bit in range(bits)
        ]
        self.steps = {}
        first = self.core == 0
        for late in (False, True):
            pair = orders(bits, late)
            own, other, devices = [], [], []
            for place in range(bits):
                zero, one = pair[0][place], pair[1][place]
                if zero == one:
                    own.append(self.delta[zero])
                    other.append(self.delta[zero])
                    devices.append(self.device[zero])
                else:
                    own.append(jnp.where(first, self.delta[zero], self.delta[one]))
                    other.append(jnp.where(first, self.delta[one], self.delta[zero]))
                    devices.append(
                        tuple(jnp.where(first, a, b) for a, b in zip(self.device[zero], self.device[one]))
                    )
            self.steps[late] = (own, other, devices)
        self.opposite = (self.device[CORE][0], self.device[0][1])

    def block(self, late, member):
        own, other, _ = self.steps[late]
        last = self.bits - 1
        table = other if member >> last & 1 else own
        index = self.me
        for place in range(self.bits):
            if member >> place & 1:
                index = index + table[place]
        return index

    def partner(self, late, place):
        return self.steps[late][2][place]

    def near(self, other):
        if other == 3:
            return self.opposite, 3 - self.quad
        bit = other - 1
        return self.device[bit], self.quad + self.delta[bit]

    def greet(self):
        barrier = pltpu.get_barrier_semaphore()
        partners = self.device + [self.opposite]
        for partner in partners:
            pl.semaphore_signal(barrier, inc=1, device_id=partner, device_id_type=MESH)
        pl.semaphore_wait(barrier, len(partners))


def remote(source, target, send_sem, recv_sem, device):
    copy = pltpu.make_async_remote_copy(
        src_ref=source, dst_ref=target, send_sem=send_sem, recv_sem=recv_sem, device_id=device, device_id_type=MESH
    )
    copy.start()
    return copy


def local(source, target, sem):
    copy = pltpu.make_async_copy(source, target, sem)
    copy.start()
    return copy


def await_bytes(spot, sem):
    pltpu.make_async_copy(spot, spot, sem).wait()


def aligned(start, size, by=16):
    return pl.ds(pl.multiple_of(start, by), size)


def repeat(times, body):
    def run(index, carry):
        body(index)
        return carry

    lax.fori_loop(0, times, run, 0)


class Agenda:
    def __init__(self):
        self.services = []
        self.steps = []
        self.now = 0.0

    def service(self, when, action):
        self.services.append((when, len(self.services), action))

    def step(self, takes, action, after=0.0):
        self.steps.append((takes, action, after))

    def emit(self):
        while self.services or self.steps:
            self.services.sort(key=lambda item: item[:2])
            due = self.services[0][0] if self.services else None
            after = self.steps[0][2] if self.steps else None
            if self.services and (not self.steps or due <= self.now or (after > self.now and due <= after)):
                when, _, action = self.services.pop(0)
                self.now = max(self.now, when) + 0.1
            else:
                takes, action, after = self.steps.pop(0)
                self.now = max(self.now, after) + takes
            action()


def nn(left, right):
    return jnp.dot(left, right, preferred_element_type=jnp.float32)


def nt(left, right):
    return lax.dot_general(left, right, (((1,), (1,)), ((), ())), preferred_element_type=jnp.float32)


def tn(left, right):
    return lax.dot_general(left, right, (((0,), (0,)), ((), ())), preferred_element_type=jnp.float32)


def gelu_parts(value):
    bend = jnp.tanh(0.7978845608028654 * (value + 0.044715 * value * value * value))
    slope = 0.7978845608028654 * (1.0 + 0.134145 * value * value)
    return 0.5 * value * (1.0 + bend), 0.5 * (1.0 + bend) + 0.5 * value * (1.0 - bend * bend) * slope


def normalized(value):
    centre = jnp.mean(value, axis=-1, keepdims=True)
    centred = value - centre
    spread = jnp.mean(centred * centred, axis=-1, keepdims=True)
    root = lax.rsqrt(spread + NORM_EPS)
    return centred * root, root


def head_window(head, size):
    first, last = head * size // 128, (head * size + size - 1) // 128
    return first * 128, (last + 1 - first) * 128, head * size - first * 128


def only_head(values, offset, size):
    lane = lax.broadcasted_iota(jnp.int32, values.shape, 1)
    return jnp.where(jnp.logical_and(lane >= offset, lane < offset + size), values, jnp.zeros((), values.dtype))


STRIP = 32
TILE = 384


def forward_kernel(bits, rows, pieces, clock,
                   a_src, b_src, c_src, terms_in, mod_bias, bias_rows, frames, cot, key_mask, row_mask,
                   a_out, b_out, c_out, mod_out, query_out, key_out, value_out, total_out,
                   branch_out, midway_out, slope_out, active_out, change_out, turned_out, down_out, bias_out,
                   stage, block, c_block, terms, landed, x_ref, first, query, key, value, totals, joined, attended,
                   branch, midway, second, active, active_turned, other_turned, change, other_change, turned,
                   weight, slope_stage, down_stage,
                   quad_send, quad_recv, own_sem, keep_sem, send_sem, recv_sem, term_send, term_recv,
                   pair_send, pair_recv, load_sem, weight_sem, save_sem, slope_sem, down_sem):
    count = 1 << bits
    spots = Spots(bits)
    quad, core = spots.quad, spots.core
    sibling = spots.device[CORE]
    outs = (a_out, b_out, c_out)
    tall_rows = c_src.shape[0]
    tokens, width = first.shape
    size = width // HEADS
    scale = size ** (-0.5)
    low = jnp.bfloat16
    finals = []

    def save(source, target, index):
        finals.append(local(source, target, save_sem.at[index]).wait)

    def place(piece, index):
        kind, start, length, _ = pieces[piece]
        if kind == 2:
            return c_out.at[aligned(index * tall_rows + start, length)]
        return outs[kind].at[remainder(index, 4), aligned(quotient(index, 4) * (4 * rows) + start, length)]

    def of_kind(kind):
        return [piece for piece, entry in enumerate(pieces) if entry[0] == kind]

    own = [local(source.at[quad], stage.at[kind, quad], own_sem.at[kind]) for kind, source in enumerate((a_src, b_src))]
    own.append(local(c_src, c_block, own_sem.at[2]))
    loads = [local(terms_in, terms, load_sem.at[0]), local(frames, x_ref, load_sem.at[1])]
    spots.greet()
    quads = []

    def start_quad(kind, source):
        for other in (1, 2, 3):
            device, spot = spots.near(other)
            copy = remote(source.at[spot], stage.at[kind, quad], quad_send.at[kind, other], quad_recv.at[kind, other], device)
            quads.append(copy)
            finals.append(copy.wait_send)

    keeps = {}

    def launch(piece, member, source):
        late = pieces[piece][3]
        spot = spots.block(late, member)
        for step in range(top_place(member) + 1, bits):
            target = member | 1 << step
            copy = remote(
                source, place(piece, spot), send_sem.at[piece, target], recv_sem.at[piece, target], spots.partner(late, step)
            )
            finals.append(copy.wait_send)

    def open_pieces(kind, source):
        for piece in of_kind(kind):
            _, start, length, _ = pieces[piece]
            part = source.at[pl.ds(start, length)]
            launch(piece, 0, part)
            keeps[piece] = local(part, place(piece, spots.me), keep_sem.at[piece])

    def arrived(piece, member):
        spot = place(piece, spots.block(pieces[piece][3], member))
        await_bytes(spot, recv_sem.at[piece, member])
        return spot

    def open_quad(kind):
        own[kind].wait()
        for copy in quads[3 * kind : 3 * kind + 3]:
            copy.wait_recv()
        for lane in range(0, width, 128):
            parts = [stage[kind, q, :, lane : lane + 128].astype(jnp.float32) for q in range(4)]
            block[kind, :, lane : lane + 128] = jnp.concatenate(parts, axis=0).astype(low)
        open_pieces(kind, block.at[kind])

    crossed = [CORE, 0] + list(range(2, bits))
    term_copies = []

    def start_term(step):
        given = tuple(spots.digit[bit] for bit in crossed[:step]) + (1 - spots.digit[crossed[step]],)
        copy = remote(terms.at[given], landed[step], term_send.at[step], term_recv.at[step], spots.device[crossed[step]])
        term_copies.append(copy)
        finals.append(copy.wait_send)

    def end_term(step):
        kept = tuple(spots.digit[bit] for bit in crossed[: step + 1])
        term_copies[step].wait_recv()
        terms[kept] = terms[kept] + landed[step][...]
        if step + 1 < bits:
            start_term(step + 1)
            return
        parts = terms[kept] + mod_bias[...]
        per = width // 128
        for at in range(6 * per):
            part, lane = at // per, at % per * 128
            mod_out[part : part + 1, lane : lane + 128] = parts[at : at + 1, :]

    start_quad(0, a_src)
    loads[0].wait()
    start_term(0)
    own[2].wait()
    open_pieces(2, c_block)
    open_quad(0)
    start_quad(1, b_src)
    open_quad(1)
    agenda = Agenda()
    for step in range(bits):
        agenda.service(clock["terms"][0] + clock["terms"][1] * step, functools.partial(end_term, step))
    full = [0.0] * 3
    for piece, (kind, _, _, _) in enumerate(pieces):
        begin, pace = clock["pieces"][piece]
        for member in range(1, count // 2):
            agenda.service(
                begin + pace * member,
                lambda piece=piece, member=member: launch(piece, member, arrived(piece, member)),
            )
        full[kind] = max(full[kind], begin + pace * (count // 2) + clock["settle"])

    def finish(kind):
        for piece in of_kind(kind):
            for member in range(count // 2, count):
                arrived(piece, member)
            keeps[piece].wait()

    def load_weight(kind, q, slot):
        return local(outs[kind].at[q], weight.at[slot], weight_sem.at[slot])

    def over_strips(body):
        repeat(tokens // STRIP, lambda s: body(aligned(s * STRIP, STRIP, STRIP)))

    def over_tiles(body):
        repeat(width // TILE, lambda t: body(aligned(t * TILE, TILE, 128)))

    pairs = {}

    def trade(index, source, target):
        pairs[index] = remote(source, target, pair_send.at[index], pair_recv.at[index], sibling)
        finals.append(pairs[index].wait_send)

    def turn(source, index):
        repeat(
            width // 128,
            lambda t: turned.__setitem__(
                (index, aligned(t * 128, 128, 128)), source[:, aligned(t * 128, 128, 128)].T
            ),
        )
        save(turned.at[index], turned_out.at[index, 0], 8 + index)
        trade(index, turned.at[index], turned_out.at[index, 1])
        finals.append(pairs[index].wait_recv)

    def norm_first():
        loads[1].wait()

        def body(where):
            unit, _ = normalized(x_ref[where, :].astype(jnp.float32))
            first[where, :] = (unit * (1.0 + mod_out[1:2, :]) + mod_out[0:1, :]).astype(low)
            upstream = cot[where, :].astype(jnp.float32) * row_mask[where, :]
            change[where, :] = (mod_out[5:6, :] * upstream).astype(low)

        over_strips(body)
        save(change, change_out, 0)
        trade(3, change, other_change)
        bias_out[...] = jnp.zeros_like(bias_out)
        bias_out[0:1, :] = jnp.sum(change[...].astype(jnp.float32), axis=0, keepdims=True)

    weight_loads = {}

    def begin_first():
        finish(0)
        for s in range(2):
            weight_loads[s] = load_weight(0, s, s)

    def project(s, target, bias):
        slot = s % 2
        weight_loads[s].wait()

        def body(where):
            result = nn(first[...], weight[slot, :, where])
            if bias is not None:
                result = result + bias_rows[bias : bias + 1, where]
            target[:, where] = result.astype(low)

        over_tiles(body)
        if s + 2 < 4:
            weight_loads[s + 2] = load_weight(0, s + 2, slot)
        save(target, (query_out, key_out, value_out)[s], 1 + s)

    def clear():
        joined[...] = jnp.zeros_like(joined)
        totals[...] = jnp.zeros_like(totals)

    def attend(head):
        start, span, offset = head_window(head, size)
        where = slice(start, start + span)
        scores = nt(only_head(query[:, where], offset, size), key[:, where])
        scores = jnp.where(key_mask[0:1, :] > 0, scores * scale, MASK_VALUE)
        peak = jnp.max(scores, axis=-1, keepdims=True)
        power = jnp.exp(scores - peak)
        total = jnp.sum(power, axis=-1, keepdims=True)
        attention = (power / total).astype(low)
        joined[:, where] = joined[:, where] + nn(attention, only_head(value[:, where], offset, size))
        lane = lax.broadcasted_iota(jnp.int32, (tokens, 128), 1)
        totals[...] = jnp.where(lane == head, peak + jnp.log(total), totals[...])

    def leave_attention():
        attended[...] = joined[...].astype(low)
        save(totals, total_out, 4)
        weight_loads[3].wait()

        def body(where):
            result = nn(attended[...], weight[1, :, where]) + bias_rows[2:3, where]
            branch[:, where] = result
            midway[:, where] = x_ref[:, where].astype(jnp.float32) + mod_out[2:3, where] * result

        over_tiles(body)
        save(branch, branch_out, 5)
        save(midway, midway_out, 6)

    def norm_second():
        def body(where):
            unit, _ = normalized(midway[where, :])
            second[where, :] = (unit * (1.0 + mod_out[4:5, :]) + mod_out[3:4, :]).astype(low)

        over_strips(body)

    up_loads = {}
    slope_copies = {}

    def begin_up():
        finish(1)
        for s in range(2):
            up_loads[s] = load_weight(1, s, s)

    def raise_up(s):
        slot = s % 2
        up_loads[s].wait()
        if s >= 2:
            slope_copies[s - 2].wait()

        def body(t):
            where = aligned(t * TILE, TILE, 128)
            wide = aligned(s * width + t * TILE, TILE, 128)
            bent, slope = gelu_parts(nn(second[...], weight[slot, :, where]) + bias_rows[aligned(3 + s, 1, 1), where])
            active[:, wide] = bent.astype(low)
            active_turned[wide, :] = bent.astype(low).T
            slope_stage[slot, :, where] = slope

        repeat(width // TILE, body)
        if s + 2 < 4:
            up_loads[s + 2] = load_weight(1, s + 2, slot)
        slope_copies[s] = local(
            slope_stage.at[slot], slope_out.at[:, pl.ds(s * width, width)], slope_sem.at[slot]
        )

    span = 2 * tall_rows

    def plane_rows(j, plane):
        return aligned((2 * j + plane) * span, span)

    def trade_active():
        save(active, active_out, 7)
        for j in range(count // 4):
            trade(4 + j, active_turned.at[plane_rows(j, 1 - core)], other_turned.at[pl.ds(j * span, span)])

    down_copies = {}

    def down_gradient(j):
        slot = j % 2
        if j == 0:
            pairs[3].wait_recv()
        if j >= 2:
            down_copies[j - 2].wait()
        pairs[4 + j].wait_recv()

        def body(where):
            result = nn(active_turned[plane_rows(j, core), :], change[:, where])
            result = result + nn(other_turned[j * span : (j + 1) * span, :], other_change[:, where])
            down_stage[slot, :, where] = result.astype(low)

        over_tiles(body)
        down_copies[j] = local(down_stage.at[slot], down_out.at[pl.ds(j * span, span)], down_sem.at[slot])

    takes = clock["takes"]
    agenda.step(takes["norm"], norm_first, clock["terms"][0] + clock["terms"][1] * bits)
    agenda.step(takes["turn"], lambda: turn(first, 0))
    agenda.step(0.3, begin_first, full[0])
    for s, (target, bias) in enumerate(((query, 0), (key, None), (value, 1))):
        agenda.step(takes["matmul"], functools.partial(project, s, target, bias))
    agenda.step(0.3, clear)
    for head in range(HEADS):
        agenda.step(takes["head"], functools.partial(attend, head))
    agenda.step(takes["matmul"], leave_attention)
    agenda.step(takes["norm"], norm_second)
    agenda.step(0.3, begin_up, full[1])
    for s in range(4):
        agenda.step(takes["up"], functools.partial(raise_up, s))
    agenda.step(0.3, trade_active)
    agenda.step(takes["turn"], lambda: turn(attended, 1))
    agenda.step(takes["turn"], lambda: turn(second, 2))
    for j in range(count // 4):
        agenda.step(takes["down"], functools.partial(down_gradient, j))
    agenda.emit()
    finish(2)
    for done in finals:
        done()
    for table in (slope_copies, down_copies):
        for index in sorted(table)[-2:]:
            table[index].wait()


PIECES = ((0, 0, 96, False), (0, 96, 48, True), (1, 0, 96, False), (1, 96, 48, True), (2, 0, 96, False), (2, 96, 48, True))
CLOCK = {
    "terms": (12.0, 5.0),
    "pieces": ((8.0, 2.4), (8.0, 2.4), (16.0, 4.6), (16.0, 4.6), (24.0, 6.6), (24.0, 6.6)),
    "settle": 3.0,
    "takes": {"norm": 2.0, "turn": 0.6, "matmul": 2.0, "head": 0.8, "up": 3.5, "down": 1.2},
}


def forward(a_src, b_src, c_src, terms, mod_bias, bias_rows, frames, cot, key_mask, row_mask, pieces=PIECES, clock=CLOCK):
    rows, width = a_src.shape[1:]
    tall = c_src.shape[0]
    bits = terms.ndim - 2
    count = 1 << bits
    tokens = frames.shape[0]
    hidden = tall * count
    low, wide = jnp.bfloat16, jnp.float32

    def shaped(*sizes, dtype=low):
        return jax.ShapeDtypeStruct(sizes, dtype)

    anywhere = pl.BlockSpec(memory_space=pl.ANY)
    near = pl.BlockSpec(memory_space=pltpu.VMEM)
    token = shaped(tokens, width)
    token_wide = shaped(tokens, width, dtype=wide)
    outs = (
        shaped(4, width, width), shaped(4, width, width), shaped(hidden, width),
        shaped(8, width, dtype=wide),
        token, token, token, shaped(tokens, 128, dtype=wide),
        token_wide, token_wide,
        shaped(tokens, hidden, dtype=wide), shaped(tokens, hidden), token,
        shaped(3, 2, width, tokens),
        shaped(hidden // 2, width), shaped(8, width, dtype=wide),
    )
    out_specs = [anywhere] * len(outs)
    out_specs[3] = near
    out_specs[-1] = near
    dma = pltpu.SemaphoreType.DMA
    v = pltpu.VMEM
    scratch = [
        v((2, 4, rows, width), low), v((2, 4 * rows, width), low), v((tall, width), low),
        v(terms.shape, wide), tuple(v(terms.shape[step + 1 :], wide) for step in range(bits)),
        v((tokens, width), low), v((tokens, width), low),
        v((tokens, width), low), v((tokens, width), low), v((tokens, width), low),
        v((tokens, 128), wide), v((tokens, width), wide), v((tokens, width), low),
        v((tokens, width), wide), v((tokens, width), wide), v((tokens, width), low),
        v((tokens, hidden), low), v((hidden, tokens), low), v((hidden // 2, tokens), low),
        v((tokens, width), low), v((tokens, width), low), v((3, width, tokens), low),
        v((2, width, width), low), v((2, tokens, width), wide), v((2, 2 * tall, width), low),
        dma((2, 4)), dma((2, 4)), dma((3,)), dma((len(pieces),)), dma((len(pieces), count)), dma((len(pieces), count)),
        dma((bits,)), dma((bits,)), dma((4 + count // 4,)), dma((4 + count // 4,)),
        dma((2,)), dma((2,)), dma((16,)), dma((2,)), dma((2,)),
    ]
    return pl.pallas_call(
        functools.partial(forward_kernel, bits, rows, pieces, clock),
        out_shape=outs,
        in_specs=[anywhere] * 4 + [near] * 2 + [anywhere] + [near] * 3,
        out_specs=out_specs,
        scratch_shapes=scratch,
        compiler_params=pltpu.CompilerParams(collective_id=0, has_side_effects=True, vmem_limit_bytes=56 * 1024 * 1024),
        cost_estimate=pl.CostEstimate(flops=10_000_000_000, bytes_accessed=400_000_000, transcendentals=3_000_000),
        name="forward_gather",
    )(a_src, b_src, c_src, terms, mod_bias, bias_rows, frames, cot, key_mask, row_mask)


def backward_kernel(bits, rows, tall_rows, pieces, clock,
                    a_all, b_all, c_all, mod, bias_rows, key_mask, row_mask, frames, cot_in, query_in, key_in, value_in,
                    total_in, branch_in, midway_in, slope_in, active_in, change_in, turned_in, down_in,
                    block_out, frames_out, dmod, bias_out, a_out, b_out, c_out,
                    weight, slabs, other_up, other_low, active, slope, query, key, value, x_ref, cot, change, d_attended,
                    midway, branch, down_acc, d_norm, d_midway, turned, totals, first_grads, second_grads, recv, total,
                    quad_block, block_stage, frames_stage,
                    weight_sem, stream_sem, load_sem, save_sem, send_sem, recv_sem, pair_send, pair_recv,
                    quad_send, quad_recv, quad_own):
    count = 1 << bits
    spots = Spots(bits)
    core = spots.core
    sibling = spots.device[CORE]
    tokens, width = x_ref.shape
    size = width // HEADS
    scale = size ** (-0.5)
    low, wide = jnp.bfloat16, jnp.float32
    span = 2 * tall_rows
    finals = []

    grads_load = local(down_in, first_grads, load_sem.at[0])
    order = [(c_all, s, True) for s in range(4)] + [(b_all, s, False) for s in range(4)]
    order += [(a_all, 3, False), (a_all, 0, False), (a_all, 1, False), (a_all, 2, False)]
    weights = {}

    def load_weight(index):
        if index < len(order):
            source, s, flat = order[index]
            part = source.at[pl.ds(s * width, width)] if flat else source.at[s]
            weights[index] = local(part, weight.at[index % 2], weight_sem.at[index % 2])

    streams = {}

    def load_stream(s):
        if s < 4:
            where = pl.ds(s * width, width)
            streams[s] = (
                local(slope_in.at[:, where], slope.at[s % 2], stream_sem.at[0, s % 2]),
                local(active_in.at[:, where], active.at[s % 2], stream_sem.at[1, s % 2]),
            )

    change_load = local(change_in, change, load_sem.at[1])
    load_weight(0)
    load_stream(0)
    load_weight(1)
    load_stream(1)
    loads = {
        name: local(source, target, load_sem.at[2 + index])
        for index, (name, source, target) in enumerate(
            (
                ("second", turned_in.at[2], turned.at[2]), ("midway", midway_in, midway), ("cot", cot_in, cot),
                ("branch", branch_in, branch), ("value", value_in, value), ("query", query_in, query), ("key", key_in, key),
                ("totals", total_in, totals), ("first", turned_in.at[0], turned.at[0]),
                ("attended", turned_in.at[1], turned.at[1]), ("x", frames, x_ref),
            )
        )
    }
    spots.greet()
    dmod[...] = jnp.zeros_like(dmod)
    bias_out[...] = jnp.zeros_like(bias_out)

    grads = (first_grads, second_grads, first_grads)

    def own(piece, member):
        kind, start, length, late = pieces[piece]
        index = spots.block(late, member)
        row = remainder(index, 2) * (tall_rows if kind == 2 else width)
        row = row + quotient(index, 4) * (span if kind == 2 else 4 * rows)
        return grads[kind].at[aligned(row + start, length)]

    def landed(piece, member):
        kind, start, length, _ = pieces[piece]
        return recv.at[kind, member - 1, pl.ds(start, length)]

    sent = {kind: [] for kind in range(3)}

    def pass_on(piece, member):
        kind, _, _, late = pieces[piece]
        place = top_place(member)
        sent[kind].append(
            remote(
                own(piece, member), landed(piece, member), send_sem.at[piece, member], recv_sem.at[piece, member],
                spots.partner(late, place),
            )
        )

    def summed(piece, member, body):
        parts = [member | 1 << place for place in range(top_place(member) + 1, bits - 1)]
        for part in parts:
            await_bytes(landed(piece, part), recv_sem.at[piece, part])
        kind, start, length, _ = pieces[piece]
        mine = own(piece, member)

        def strip(s):
            where = aligned(s * ROUND, ROUND)
            value = mine[where, :].astype(wide)
            for part in parts:
                value = value + recv[kind, part - 1, aligned(start + s * ROUND, ROUND), :].astype(wide)
            body(mine, where, s, value)

        repeat(length // ROUND, strip)

    def relay(piece, member):
        def body(mine, where, s, value):
            mine[where, :] = value.astype(low)

        summed(piece, member, body)
        pass_on(piece, member)

    left = {kind: len([1 for entry in pieces if entry[0] == kind]) for kind in range(3)}

    def settle(piece):
        kind, start, length, _ = pieces[piece]

        def body(mine, where, s, value):
            total[kind, aligned(start + s * ROUND, ROUND), :] = value

        summed(piece, 0, body)
        left[kind] -= 1
        if left[kind]:
            return
        if kind == 2:
            finals.append(local(total.at[2], c_out, save_sem.at[0]).wait)
            return
        for lane in range(0, width, 128):
            for q in range(4):
                part = total[kind, q * rows : (q + 1) * rows, lane : lane + 128]
                quad_block[kind, q, :, lane : lane + 128] = part.astype(low)
        out = (a_out, b_out)[kind]
        finals.append(local(quad_block.at[kind, spots.quad], out.at[spots.quad], quad_own.at[kind]).wait)
        for other in (1, 2, 3):
            device, spot = spots.near(other)
            copy = remote(
                quad_block.at[kind, spot], out.at[spots.quad], quad_send.at[kind, other], quad_recv.at[kind, other], device
            )
            finals.append(copy.wait)

    agenda = Agenda()

    def open_kind(kind):
        half = count // 2
        for member in range(half - 1, half // 2 - 1, -1):
            for piece, entry in enumerate(pieces):
                if entry[0] == kind:
                    pass_on(piece, member)
        begin, pace = clock["open"][kind]
        for piece, entry in enumerate(pieces):
            if entry[0] == kind:
                for at, member in enumerate(range(half // 2 - 1, 0, -1)):
                    agenda.service(agenda.now + begin + pace * at, functools.partial(relay, piece, member))
                agenda.service(agenda.now + begin + pace * (half // 2 - 1), functools.partial(settle, piece))

    def open_down():
        grads_load.wait()
        open_kind(2)

    pairs = {}

    def trade(index, source, target):
        pairs[index] = remote(source, target, pair_send.at[index], pair_recv.at[index], sibling)

    def over_strips(body):
        repeat(tokens // STRIP, lambda s: body(aligned(s * STRIP, STRIP, STRIP)))

    def over_tiles(body):
        repeat(width // TILE, lambda t: body(aligned(t * TILE, TILE, 128)))

    def add_row(ref, row, where, values):
        ref[row : row + 1, where] = ref[row : row + 1, where] + jnp.sum(values, axis=0, keepdims=True)

    everything = slice(None)

    def down_slice(s):
        slot = s % 2
        if s == 0:
            change_load.wait()
        weights[s].wait()
        for copy in streams[s]:
            copy.wait()

        def body(where):
            d_up = (nt(change[...], weight[slot, where, :]) * slope[slot, :, where]).astype(low)
            slabs[s, :, where] = d_up
            add_row(bias_out, 3 + s, where, d_up.astype(wide))
            part = nn(active[slot], weight[slot, :, where])
            down_acc[:, where] = part if s == 0 else down_acc[:, where] + part

        over_tiles(body)
        load_weight(s + 2)
        load_stream(s + 2)

    def trade_up():
        for t in range(2):
            trade(t, slabs.at[2 * (1 - core) + t], other_up.at[t])

    def up_gradient(t):
        if t == 0:
            loads["second"].wait()
        pairs[t].wait_recv()

        def body(where):
            def strip(m):
                down = aligned(m * 288, 288)
                result = nn(turned[2, 0, down, :], slabs[2 * core + t, :, where])
                result = result + nn(turned[2, 1, down, :], other_up[t, :, where])
                second_grads[aligned(t * width + m * 288, 288), where] = result.astype(low)

            repeat(width // 288, strip)

        over_tiles(body)

    def norm_two_slice(s):
        weights[4 + s].wait()

        def body(where):
            part = nt(slabs[s], weight[s % 2, where, :])
            d_norm[:, where] = part if s == 0 else d_norm[:, where] + part

        over_tiles(body)
        load_weight(6 + s)

    def upstream_of(where):
        return cot[where, :].astype(wide) * row_mask[where, :]

    def norm_back(values, gradient, gain):
        unit, root = normalized(values)
        spread = gain * gradient
        back = root * (
            spread
            - jnp.mean(spread, axis=-1, keepdims=True)
            - unit * jnp.mean(spread * unit, axis=-1, keepdims=True)
        )
        return unit, back

    def back_second():
        for name in ("midway", "cot", "branch"):
            loads[name].wait()
        for t in range(2):
            pairs[t].wait_send()

        def body(where):
            gradient = d_norm[where, :]
            unit, back = norm_back(midway[where, :], gradient, 1.0 + mod[4:5, :])
            middle = upstream_of(where) + back
            d_midway[where, :] = middle
            d_branch = (mod[2:3, :] * middle).astype(low)
            slabs[3, where, :] = d_branch
            add_row(dmod, 3, everything, gradient)
            add_row(dmod, 4, everything, gradient * unit)
            add_row(dmod, 2, everything, middle * branch[where, :])
            add_row(bias_out, 2, everything, d_branch.astype(wide))

        over_strips(body)

    def back_attended():
        weights[8].wait()

        def body(where):
            d_attended[:, where] = nt(slabs[3], weight[0, where, :]).astype(low)

        over_tiles(body)
        load_weight(10)
        for name in ("value", "query", "key", "totals"):
            loads[name].wait()
        slope[...] = jnp.zeros_like(slope)
        branch[...] = jnp.zeros_like(branch)

    def attend_back(head):
        start, reach, offset = head_window(head, size)
        where = slice(start, start + reach)
        chosen = only_head(query[:, where], offset, size)
        scores = nt(chosen, key[:, where])
        scores = jnp.where(key_mask[0:1, :] > 0, scores * scale, MASK_VALUE)
        soft = jnp.exp(scores - totals[:, head : head + 1])
        given = only_head(d_attended[:, where], offset, size)
        d_soft = nt(given, value[:, where])
        d_scores = (soft * (d_soft - jnp.sum(soft * d_soft, axis=-1, keepdims=True))).astype(low)
        slope[0, :, where] = slope[0, :, where] + nn(d_scores, only_head(key[:, where], offset, size))
        slope[1, :, where] = slope[1, :, where] + tn(d_scores, chosen)
        branch[:, where] = branch[:, where] + tn(soft.astype(low), given)

    def leave_attention():
        slabs[0] = (slope[0] * scale).astype(low)
        slabs[1] = (slope[1] * scale).astype(low)
        slabs[2] = branch[...].astype(low)
        for t in range(2):
            trade(2 + t, slabs.at[2 * (1 - core) + t], other_low.at[t])
        bias_out[0:1, :] = jnp.sum(slabs[0].astype(wide), axis=0, keepdims=True)
        bias_out[1:2, :] = jnp.sum(slabs[2].astype(wide), axis=0, keepdims=True)

    def leave_block():
        def body(where):
            down = down_acc[where, :] + bias_rows[7:8, :]
            add_row(dmod, 5, everything, upstream_of(where) * down)
            block_stage[where, :] = ((midway[where, :] + mod[5:6, :] * down) * row_mask[where, :]).astype(low)

        over_strips(body)
        finals.append(local(block_stage, block_out, save_sem.at[1]).wait)

    def low_gradient(t):
        if t == 0:
            loads["first"].wait()
            loads["attended"].wait()
            for copy in sent[2]:
                copy.wait_send()
        pairs[2 + t].wait_recv()
        at = 2 * core + t
        which = quotient(at, 3)

        def body(where):
            def strip(m):
                down = aligned(m * 288, 288)
                result = nn(turned[which, 0, down, :], slabs[at, :, where])
                result = result + nn(turned[which, 1, down, :], other_low[t, :, where])
                first_grads[aligned(t * width + m * 288, 288), where] = result.astype(low)

            repeat(width // 288, strip)

        over_tiles(body)

    def norm_one_slice(s):
        weights[9 + s].wait()

        def body(where):
            part = nt(slabs[s], weight[(9 + s) % 2, where, :])
            d_norm[:, where] = part if s == 0 else d_norm[:, where] + part

        over_tiles(body)
        load_weight(11 + s)

    def back_first():
        loads["x"].wait()

        def body(where):
            gradient = d_norm[where, :]
            unit, back = norm_back(x_ref[where, :].astype(wide), gradient, 1.0 + mod[1:2, :])
            add_row(dmod, 0, everything, gradient)
            add_row(dmod, 1, everything, gradient * unit)
            frames_stage[where, :] = (back + d_midway[where, :]).astype(low)

        over_strips(body)
        finals.append(local(frames_stage, frames_out, save_sem.at[2]).wait)

    takes = clock["takes"]
    agenda.step(2.0, open_down)
    for s in range(4):
        agenda.step(takes["down"], functools.partial(down_slice, s))
    agenda.step(0.3, trade_up)
    for t in range(2):
        agenda.step(takes["gradient"], functools.partial(up_gradient, t))
    agenda.step(0.5, lambda: open_kind(1))
    for s in range(4):
        agenda.step(takes["matmul"], functools.partial(norm_two_slice, s))
    agenda.step(takes["norm"], back_second)
    agenda.step(takes["matmul"], back_attended)
    for head in range(HEADS):
        agenda.step(takes["head"], functools.partial(attend_back, head))
    agenda.step(1.0, leave_attention)
    agenda.step(takes["norm"], leave_block)
    for t in range(2):
        agenda.step(takes["gradient"], functools.partial(low_gradient, t))
    agenda.step(0.5, lambda: open_kind(0))
    for s in range(3):
        agenda.step(takes["matmul"], functools.partial(norm_one_slice, s))
    agenda.step(takes["norm"], back_first)
    agenda.emit()
    for kind in (0, 1):
        for copy in sent[kind]:
            copy.wait_send()
    for t in range(2):
        pairs[2 + t].wait_send()
    for done in finals:
        done()


BACK_CLOCK = {
    "open": ((18.0, 4.5), (26.0, 5.5), (22.0, 5.0)),
    "takes": {"down": 4.5, "gradient": 4.0, "matmul": 2.2, "norm": 3.0, "head": 1.8},
}


def backward(weights, mod, bias_rows, key_mask, row_mask, frames, cot, saved, rows, bits, pieces=PIECES, clock=BACK_CLOCK):
    a_all, b_all, c_all = weights
    width = a_all.shape[-1]
    count = 1 << bits
    hidden = c_all.shape[0]
    tall = hidden // count
    tokens = frames.shape[0]
    low, wide = jnp.bfloat16, jnp.float32

    def shaped(*sizes, dtype=low):
        return jax.ShapeDtypeStruct(sizes, dtype)

    anywhere = pl.BlockSpec(memory_space=pl.ANY)
    near = pl.BlockSpec(memory_space=pltpu.VMEM)
    dma = pltpu.SemaphoreType.DMA
    v = pltpu.VMEM
    kinds = len(pieces)
    scratch = [
        v((2, width, width), low), v((4, tokens, width), low),
        v((2, tokens, width), low), v((2, tokens, width), low),
        v((2, tokens, width), low), v((2, tokens, width), wide),
        v((tokens, width), low), v((tokens, width), low), v((tokens, width), low),
        v((tokens, width), low), v((tokens, width), low), v((tokens, width), low), v((tokens, width), low),
        v((tokens, width), wide), v((tokens, width), wide),
        v((tokens, width), wide), v((tokens, width), wide), v((tokens, width), wide),
        v((3, 2, width, tokens), low), v((tokens, 128), wide),
        v((2 * width, width), low), v((2 * width, width), low),
        v((3, count // 2 - 1, 4 * rows, width), low), v((3, 4 * rows, width), wide), v((2, 4, rows, width), low),
        v((tokens, width), low), v((tokens, width), low),
        dma((2,)), dma((2, 2)), dma((13,)), dma((3,)), dma((kinds, count // 2)), dma((kinds, count // 2)),
        dma((4,)), dma((4,)), dma((2, 4)), dma((2, 4)), dma((2,)),
    ]
    share = shaped(4, rows, width)
    return pl.pallas_call(
        functools.partial(backward_kernel, bits, rows, tall, pieces, clock),
        out_shape=(
            shaped(tokens, width), shaped(tokens, width), shaped(8, width, dtype=wide), shaped(8, width, dtype=wide),
            share, share, shaped(tall, width, dtype=wide),
        ),
        in_specs=[anywhere] * 3 + [near] * 4 + [anywhere] * (2 + len(saved)),
        out_specs=[anywhere] * 2 + [near] * 2 + [anywhere] * 3,
        scratch_shapes=scratch,
        compiler_params=pltpu.CompilerParams(collective_id=1, has_side_effects=True, vmem_limit_bytes=62 * 1024 * 1024),
        cost_estimate=pl.CostEstimate(flops=18_000_000_000, bytes_accessed=400_000_000, transcendentals=3_000_000),
        name="backward_reduce",
    )(a_all, b_all, c_all, mod, bias_rows, key_mask, row_mask, frames, cot, *saved)


def masks(order, member):
    return sum(1 << bit for place, bit in enumerate(order) if member >> place & 1)


def me_index():
    return lax.axis_index("wide") * 2 + lax.axis_index("narrow")


def device(index):
    return (index // 2, lax.rem(index, 2))


def own_plane(me):
    return lax.rem(me // 2, 2)


def flip(index, mask):
    out = index
    bit = 0
    while mask >> bit:
        if mask >> bit & 1:
            value = lax.rem(out // (1 << bit), 2)
            out = out + (1 << bit) * (1 - 2 * value)
        bit += 1
    return out


def block_of(me, pair, member, bits):
    plane = own_plane(me)
    last = 1 << (bits - 1)
    if member & last:
        rest = member - last
        zero = flip(flip(me, 1 << CORE), masks(pair[1], rest))
        one = flip(flip(me, 1 << CORE), masks(pair[0], rest))
    else:
        zero = flip(me, masks(pair[0], member))
        one = flip(me, masks(pair[1], member))
    return jnp.where(plane == 0, zero, one)


def partner_of(me, pair, place):
    zero = flip(me, 1 << pair[0][place])
    if pair[0][place] == pair[1][place]:
        return zero
    return jnp.where(own_plane(me) == 0, zero, flip(me, 1 << pair[1][place]))


def greet(me, bits):
    barrier = pltpu.get_barrier_semaphore()
    partners = [flip(me, 1 << bit) for bit in range(bits)] + [flip(me, 3)]
    for partner in partners:
        pl.semaphore_signal(barrier, inc=1, device_id=device(partner), device_id_type=MESH)
    pl.semaphore_wait(barrier, len(partners))


def gather_kernel(bits, rows, lates, a_src, b_src, c_src, a_out, b_out, c_out,
                  stage, block, c_block, quad_send, quad_recv, own_sem, keep_sem, send_sem, recv_sem):
    count = 1 << bits
    me = me_index()
    quad, spot = lax.rem(me, 4), me // 4
    pairs = [orders(bits, late) for late in lates]
    outs = (a_out, b_out, c_out)

    def place(kind, index):
        q, j = lax.rem(index, 4), index // 4
        return outs[kind].at[q, j] if kind < 2 else outs[kind].at[j, q]

    def send(kind, member, step, source):
        target = member | 1 << step
        return pltpu.make_async_remote_copy(
            src_ref=source,
            dst_ref=place(kind, block_of(me, pairs[kind], member, bits)),
            send_sem=send_sem.at[kind, target],
            recv_sem=recv_sem.at[kind, target],
            device_id=device(partner_of(me, pairs[kind], step)),
            device_id_type=MESH,
        )

    own = []
    for kind, source in enumerate((a_src, b_src)):
        own.append(pltpu.make_async_copy(source.at[quad], stage.at[kind, quad], own_sem.at[kind]))
    own.append(pltpu.make_async_copy(c_src, c_block, own_sem.at[2]))
    for copy in own:
        copy.start()
    greet(me, bits)
    quads = []
    for kind, source in enumerate((a_src, b_src)):
        for other in (1, 2, 3):
            copy = pltpu.make_async_remote_copy(
                src_ref=source.at[flip(quad, other)],
                dst_ref=stage.at[kind, quad],
                send_sem=quad_send.at[kind, other],
                recv_sem=quad_recv.at[kind, other],
                device_id=device(flip(me, other)),
                device_id_type=MESH,
            )
            copy.start()
            quads.append(copy)
    sends = []
    keeps = []

    def launch(kind, member, source):
        for step in range(top_place(member) + 1, bits):
            copy = send(kind, member, step, source)
            copy.start()
            sends.append(copy)

    def keep(kind, source):
        copy = pltpu.make_async_copy(source, place(kind, me), keep_sem.at[kind])
        copy.start()
        keeps.append(copy)

    own[2].wait()
    launch(2, 0, c_block)
    keep(2, c_block)
    padded = block.shape[1]
    for kind in (0, 1):
        own[kind].wait()
        for copy in quads[3 * kind:3 * kind + 3]:
            copy.wait_recv()
        for lane in range(0, stage.shape[3], 128):
            parts = [stage[kind, q, :, lane:lane + 128].astype(jnp.float32) for q in range(4)]
            if padded > 4 * rows:
                parts.append(jnp.zeros((padded - 4 * rows, 128), jnp.float32))
            block[kind, :, lane:lane + 128] = jnp.concatenate(parts, axis=0).astype(jnp.bfloat16)
        launch(kind, 0, block.at[kind])
        keep(kind, block.at[kind])

    def arrived(kind, member):
        spot_ref = place(kind, block_of(me, pairs[kind], member, bits))
        pltpu.make_async_copy(spot_ref, spot_ref, recv_sem.at[kind, member]).wait()
        return spot_ref

    for member in range(1, count):
        for kind in (2, 0, 1):
            launch(kind, member, arrived(kind, member))
    for copy in sends + quads:
        copy.wait_send()
    for copy in keeps:
        copy.wait()


def gather(a_src, b_src, c_src, count, lates=(False, False, False)):
    bits = count.bit_length() - 1
    rows, columns = a_src.shape[1:]
    padded = -(-4 * rows // 16) * 16
    c_padded = -(-c_src.shape[0] // 16) * 16
    if c_padded != c_src.shape[0]:
        c_src = jnp.pad(c_src, ((0, c_padded - c_src.shape[0]), (0, 0)))
    kinds = 3
    anywhere = pl.BlockSpec(memory_space=pl.ANY)
    big = jax.ShapeDtypeStruct((4, count // 4, padded, columns), jnp.bfloat16)
    tall = jax.ShapeDtypeStruct((count // 4, 4, c_padded, columns), jnp.bfloat16)
    a_all, b_all, c_all = pl.pallas_call(
        functools.partial(gather_kernel, bits, rows, lates),
        out_shape=(big, big, tall),
        in_specs=[anywhere] * 3,
        out_specs=(anywhere,) * 3,
        scratch_shapes=[
            pltpu.VMEM((2, 4, rows, columns), jnp.bfloat16),
            pltpu.VMEM((2, padded, columns), jnp.bfloat16),
            pltpu.VMEM((c_padded, columns), jnp.bfloat16),
            pltpu.SemaphoreType.DMA((2, 4)),
            pltpu.SemaphoreType.DMA((2, 4)),
            pltpu.SemaphoreType.DMA((3,)),
            pltpu.SemaphoreType.DMA((3,)),
            pltpu.SemaphoreType.DMA((kinds, count)),
            pltpu.SemaphoreType.DMA((kinds, count)),
        ],
        compiler_params=pltpu.CompilerParams(collective_id=2, has_side_effects=True),
        cost_estimate=pl.CostEstimate(flops=0, bytes_accessed=400_000_000, transcendentals=0),
        name="gather_weights",
    )(a_src, b_src, c_src)
    return a_all, b_all, c_all


def reduce_kernel(bits, rows, lates, a_in, b_in, c_in, a_out, b_out, c_out,
                  own, recv, quad_block, total, own_sem, send_sem, recv_sem, quad_send, quad_recv, quad_own, total_sem):
    count = 1 << bits
    half = count // 2
    me = me_index()
    quad = lax.rem(me, 4)
    pairs = [orders(bits, late) for late in lates]
    ins = (a_in, b_in, c_in)
    kinds = (2, 1, 0)

    def place(kind, index):
        q, j = lax.rem(index, 4), index // 4
        return ins[kind].at[q, j] if kind < 2 else ins[kind].at[j, q]

    loads = {}
    for member in range(half - 1, -1, -1):
        for kind in kinds:
            loads[kind, member] = pltpu.make_async_copy(
                place(kind, block_of(me, pairs[kind], member, bits)), own.at[kind, member], own_sem.at[kind, member]
            )
    sends = []

    def send(kind, member, source):
        step = top_place(member)
        copy = pltpu.make_async_remote_copy(
            src_ref=source,
            dst_ref=recv.at[kind, member],
            send_sem=send_sem.at[kind, member],
            recv_sem=recv_sem.at[kind, member],
            device_id=device(partner_of(me, pairs[kind], step)),
            device_id_type=MESH,
        )
        copy.start()
        sends.append(copy)

    for kind in kinds:
        loads[kind, half - 1].start()
    greet(me, bits)
    for member in range(half - 1, -1, -1):
        for kind in kinds:
            send(kind, member + half, place(kind, block_of(me, pairs[kind], member + half, bits)))
            if member < half - 1:
                loads[kind, member].start()

    padded, columns = own.shape[2:]

    def ready(kind, member):
        loads[kind, member].wait()
        parts = [member | 1 << step for step in range(top_place(member) + 1, bits)]
        for part in parts:
            pltpu.make_async_copy(recv.at[kind, part], recv.at[kind, part], recv_sem.at[kind, part]).wait()
        return parts

    def summed(kind, member, parts, where):
        value = own[kind, member, where, :].astype(jnp.float32)
        for part in parts:
            value = value + recv[kind, part, where, :].astype(jnp.float32)
        return value

    for member in range(half - 1, 0, -1):
        for kind in kinds:
            parts = ready(kind, member)

            def strip(s, carry, kind=kind, member=member, parts=parts):
                where = pl.ds(pl.multiple_of(s * 16, 16), 16)
                own[kind, member, where, :] = summed(kind, member, parts, where).astype(jnp.bfloat16)
                return carry

            lax.fori_loop(0, padded // 16, strip, 0)
            send(kind, member, own.at[kind, member])

    copies = []
    for kind in kinds:
        parts = ready(kind, 0)

        def strip(s, carry, kind=kind, parts=parts):
            where = pl.ds(pl.multiple_of(s * 16, 16), 16)
            total[kind, where, :] = summed(kind, 0, parts, where)
            return carry

        lax.fori_loop(0, padded // 16, strip, 0)
        if kind == 2:
            copy = pltpu.make_async_copy(total.at[2], c_out, total_sem)
            copy.start()
            copies.append(copy)
            continue
        out = (a_out, b_out)[kind]
        for lane in range(0, columns, 128):
            for q in range(4):
                quad_block[kind, q, :, lane:lane + 128] = total[kind, q * rows:(q + 1) * rows, lane:lane + 128].astype(jnp.bfloat16)
        copy = pltpu.make_async_copy(quad_block.at[kind, quad], out.at[quad], quad_own.at[kind])
        copy.start()
        copies.append(copy)
        for other in (1, 2, 3):
            copy = pltpu.make_async_remote_copy(
                src_ref=quad_block.at[kind, flip(quad, other)],
                dst_ref=out.at[quad],
                send_sem=quad_send.at[kind, other],
                recv_sem=quad_recv.at[kind, other],
                device_id=device(flip(me, other)),
                device_id_type=MESH,
            )
            copy.start()
            copies.append(copy)
    for copy in copies:
        copy.wait()
    for copy in sends:
        copy.wait_send()


def reduce(a_in, b_in, c_in, rows, lates=(False, False, False)):
    count = a_in.shape[1] * 4
    bits = count.bit_length() - 1
    padded, columns = a_in.shape[2:]
    anywhere = pl.BlockSpec(memory_space=pl.ANY)
    share = jax.ShapeDtypeStruct((4, rows, columns), jnp.bfloat16)
    return pl.pallas_call(
        functools.partial(reduce_kernel, bits, rows, lates),
        out_shape=(share, share, jax.ShapeDtypeStruct((padded, columns), jnp.float32)),
        in_specs=[anywhere] * 3,
        out_specs=(anywhere,) * 3,
        scratch_shapes=[
            pltpu.VMEM((3, count // 2, padded, columns), jnp.bfloat16),
            pltpu.VMEM((3, count, padded, columns), jnp.bfloat16),
            pltpu.VMEM((2, 4, rows, columns), jnp.bfloat16),
            pltpu.VMEM((3, padded, columns), jnp.float32),
            pltpu.SemaphoreType.DMA((3, count // 2)),
            pltpu.SemaphoreType.DMA((3, count)),
            pltpu.SemaphoreType.DMA((3, count)),
            pltpu.SemaphoreType.DMA((2, 4)),
            pltpu.SemaphoreType.DMA((2, 4)),
            pltpu.SemaphoreType.DMA((2,)),
            pltpu.SemaphoreType.DMA,
        ],
        compiler_params=pltpu.CompilerParams(collective_id=3, has_side_effects=True, vmem_limit_bytes=62 * 1024 * 1024),
        cost_estimate=pl.CostEstimate(flops=0, bytes_accessed=400_000_000, transcendentals=0),
        name="reduce_gradients",
    )(a_in, b_in, c_in)


def layer_norm(values):
    centre = jnp.mean(values, axis=-1, keepdims=True)
    centred = values - centre
    spread = jnp.mean(centred * centred, axis=-1, keepdims=True)
    return centred * lax.rsqrt(spread + NORM_EPS)


def modulate(values, shift_part, scale_part):
    return layer_norm(values) * (1.0 + scale_part) + shift_part


def silu_act(values):
    return values * jax.nn.sigmoid(values)


def gelu_tanh(values):
    inner = 0.7978845608028654 * (values + 0.044715 * values * values * values)
    return 0.5 * values * (1.0 + jnp.tanh(inner))


def slot_mask(grid, frame_len):
    area = grid[:, 0] * grid[:, 1]
    return lax.broadcasted_iota(jnp.int32, (grid.shape[0], frame_len), 1) < area[:, None]


def split_biases(biases, model_width, hidden_width):
    edges = [
        6 * model_width,
        7 * model_width,
        8 * model_width,
        9 * model_width,
        9 * model_width + hidden_width,
    ]
    return jnp.split(biases, edges)


def adam_update(weight, state, grad):
    first = FIRST_DECAY * state[0] + (1.0 - FIRST_DECAY) * grad
    second = SECOND_DECAY * state[1] + (1.0 - SECOND_DECAY) * grad * grad
    first_hat = first / (1.0 - FIRST_DECAY**STEPS)
    second_hat = second / (1.0 - SECOND_DECAY**STEPS)
    new_weight = weight - RATE * (
        first_hat / (jnp.sqrt(second_hat) + ADAM_EPS) + WEIGHT_DECAY * weight
    )
    average = AVERAGE_DECAY * state[2] + (1.0 - AVERAGE_DECAY) * new_weight
    return (new_weight, jnp.stack([first, second, average]))


def attention_scores(query_heads, key_heads, valid_slots, score_scale):
    scores = (
        jnp.einsum("fqhs,fkhs->fhqk", query_heads, key_heads, preferred_element_type=jnp.float32)
        * score_scale
    )
    return jnp.where(valid_slots[:, None, None, :], scores, MASK_VALUE)


def token_sum(values):
    return jnp.sum(values, axis=(0, 1), dtype=jnp.float32)


def exchange(packets):
    return lax.all_to_all(packets, AXES, split_axis=0, concat_axis=0, tiled=True)


def plain_shards(
    frames_in,
    conditioning,
    grid,
    cotangent,
    mod_weight,
    qkv_weight,
    out_weight,
    up_weight,
    down_weight,
    biases,
    mod_state,
    qkv_state,
    out_state,
    up_state,
    down_state,
    bias_state,
):
    frame_count, frame_len, model_width = frames_in.shape
    hidden_width = up_weight.shape[1]
    head_size = model_width // HEADS
    score_scale = head_size ** (-0.5)
    head_shape = (frame_count, frame_len, HEADS, head_size)
    count = lax.axis_size("wide") * lax.axis_size("narrow")
    rows = mod_weight.shape[0]
    tall_rows = down_weight.shape[0]
    low = jnp.bfloat16

    def slices(member):
        return member.reshape(rows, 4, model_width).transpose(1, 0, 2)

    a_src = slices(jnp.concatenate([qkv_weight.astype(low), out_weight.astype(low)], axis=1))
    b_src = slices(up_weight.astype(low))
    a_all, b_all, c_all = gather(a_src, b_src, down_weight.astype(low), count, (False, False, True))
    a_all = a_all[:, :, : 4 * rows].reshape(4, model_width, model_width)
    up_low = b_all[:, :, : 4 * rows].reshape(4, model_width, model_width)
    down_low = c_all[:, :, :tall_rows].reshape(hidden_width, model_width)
    query_low, key_low, value_low, out_low = (a_all[index] for index in range(4))

    cond_f = conditioning.astype(jnp.float32)
    silu_low = silu_act(cond_f).astype(low)
    mod_low = mod_weight.astype(low)
    first = exchange(
        jnp.concatenate(
            [
                silu_low.reshape(count, rows),
                jnp.broadcast_to(biases.astype(low)[None], (count, biases.shape[0])),
            ],
            axis=1,
        )
    )
    silu_rows = first[:, :rows]
    bias_low = first[:, rows:].reshape(-1)
    mod_terms = exchange(jnp.dot(silu_rows, mod_low, preferred_element_type=jnp.float32))
    mod_bias, query_bias, value_bias, out_bias, up_bias, down_bias = split_biases(
        bias_low.astype(jnp.float32), model_width, hidden_width
    )
    modulation = jnp.sum(mod_terms, axis=0, keepdims=True) + mod_bias
    valid_slots = slot_mask(grid, frame_len)
    row_mask = valid_slots[:, :, None].astype(jnp.float32)
    frames_f = frames_in.astype(jnp.float32)
    shift_attn, scale_attn, gate_attn, shift_mlp, scale_mlp, gate_mlp = jnp.split(
        modulation[:, None, :], 6, axis=-1
    )
    norm_one = modulate(frames_f, shift_attn, scale_attn).astype(low)

    def project(values, weight):
        return jnp.einsum("fbd,de->fbe", values, weight, preferred_element_type=jnp.float32)

    query_heads = (project(norm_one, query_low) + query_bias).astype(low).reshape(head_shape)
    key_heads = project(norm_one, key_low).astype(low).reshape(head_shape)
    value_heads = (project(norm_one, value_low) + value_bias).astype(low).reshape(head_shape)
    scores = attention_scores(query_heads, key_heads, valid_slots, score_scale)
    row_max = jnp.max(scores, axis=-1, keepdims=True)
    exponent = jnp.exp(scores - row_max)
    row_total = jnp.sum(exponent, axis=-1, keepdims=True)
    log_total = row_max + jnp.log(row_total)
    attention = (exponent / row_total).astype(low)
    attended = jnp.einsum(
        "fhqk,fkhs->fqhs", attention, value_heads, preferred_element_type=jnp.float32
    )
    attended = attended.reshape(frame_count, frame_len, model_width).astype(low)
    branch = project(attended, out_low) + out_bias
    midway = frames_f + gate_attn * branch
    norm_two = modulate(midway, shift_mlp, scale_mlp).astype(low)
    up_values = (
        jnp.einsum("fbd,sde->fbse", norm_two, up_low, preferred_element_type=jnp.float32).reshape(
            frame_count, frame_len, hidden_width
        )
        + up_bias
    )
    activated = gelu_tanh(up_values).astype(low)
    down_values = project(activated, down_low) + down_bias
    block_out = ((midway + gate_mlp * down_values) * row_mask).astype(low)
    upstream = cotangent.astype(jnp.float32) * row_mask
    d_gate_mlp = jnp.sum(upstream * down_values, axis=1, keepdims=True)
    d_down = (upstream * gate_mlp).astype(low)
    grad_down = jnp.einsum("fbe,fbd->ed", activated, d_down, preferred_element_type=jnp.float32)
    grad_down_bias = token_sum(d_down)
    d_activated = jnp.einsum("fbd,ed->fbe", d_down, down_low, preferred_element_type=jnp.float32)
    gelu_pull = jax.vjp(gelu_tanh, up_values)[1]
    d_up = gelu_pull(d_activated)[0].astype(low)
    d_up_parts = d_up.reshape(frame_count, frame_len, 4, model_width)
    grad_up = jnp.einsum("fbd,fbse->sde", norm_two, d_up_parts, preferred_element_type=jnp.float32)
    grad_up_bias = token_sum(d_up)
    d_norm_two = jnp.einsum("fbse,sde->fbd", d_up_parts, up_low, preferred_element_type=jnp.float32)
    second_pull = jax.vjp(modulate, midway, shift_mlp, scale_mlp)[1]
    d_midway, d_shift_mlp, d_scale_mlp = second_pull(d_norm_two)
    d_midway = d_midway + upstream
    d_gate_attn = jnp.sum(d_midway * branch, axis=1, keepdims=True)
    d_branch = (d_midway * gate_attn).astype(low)
    grad_out = jnp.einsum("fbd,fbe->de", attended, d_branch, preferred_element_type=jnp.float32)
    grad_out_bias = token_sum(d_branch)
    d_attended = jnp.einsum("fbe,de->fbd", d_branch, out_low, preferred_element_type=jnp.float32)
    d_attended = d_attended.astype(low).reshape(head_shape)
    scores = attention_scores(query_heads, key_heads, valid_slots, score_scale)
    soft = jnp.exp(scores - log_total)
    d_soft = jnp.einsum(
        "fqhs,fkhs->fhqk", d_attended, value_heads, preferred_element_type=jnp.float32
    )
    d_value_heads = jnp.einsum(
        "fhqk,fqhs->fkhs", attention, d_attended, preferred_element_type=jnp.float32
    )
    d_scores = (soft * (d_soft - jnp.sum(soft * d_soft, axis=-1, keepdims=True))).astype(low)
    d_query_heads = (
        jnp.einsum("fhqk,fkhs->fqhs", d_scores, key_heads, preferred_element_type=jnp.float32)
        * score_scale
    )
    d_key_heads = (
        jnp.einsum("fhqk,fqhs->fkhs", d_scores, query_heads, preferred_element_type=jnp.float32)
        * score_scale
    )
    flat_shape = (frame_count, frame_len, model_width)
    d_query = d_query_heads.reshape(flat_shape).astype(low)
    d_key = d_key_heads.reshape(flat_shape).astype(low)
    d_value = d_value_heads.reshape(flat_shape).astype(low)
    grad_query, grad_key, grad_value = (
        jnp.einsum("fbd,fbe->de", norm_one, member, preferred_element_type=jnp.float32)
        for member in (d_query, d_key, d_value)
    )
    grad_query_bias = token_sum(d_query)
    grad_value_bias = token_sum(d_value)
    d_norm_one = sum(
        jnp.einsum("fbe,de->fbd", member, weight, preferred_element_type=jnp.float32)
        for member, weight in ((d_query, query_low), (d_key, key_low), (d_value, value_low))
    )
    first_pull = jax.vjp(modulate, frames_f, shift_attn, scale_attn)[1]
    d_frames, d_shift_attn, d_scale_attn = first_pull(d_norm_one)
    frames_grad = (d_frames + d_midway).astype(low)
    d_modulation = jnp.concatenate(
        [d_shift_attn, d_scale_attn, d_gate_attn, d_shift_mlp, d_scale_mlp, d_gate_mlp], axis=-1
    )[:, 0, :].astype(low)
    grad_mod_bias = d_modulation[0].astype(jnp.float32)
    grad_bias = jnp.concatenate(
        [
            grad_mod_bias,
            grad_query_bias,
            grad_value_bias,
            grad_out_bias,
            grad_up_bias,
            grad_down_bias,
        ]
    )
    terms = exchange(
        jnp.concatenate(
            [
                jnp.broadcast_to(d_modulation, (count, d_modulation.shape[1])),
                grad_bias.reshape(count, -1).astype(low),
            ],
            axis=1,
        )
    )
    d_mod_all, bias_terms = terms[:, : d_modulation.shape[1]], terms[:, d_modulation.shape[1] :]

    def grouped(member, group_rows):
        member = member.astype(low).reshape(4, count // 4, 4 * rows, model_width)
        return jnp.pad(member, ((0, 0), (0, 0), (0, group_rows - 4 * rows), (0, 0)))

    group_rows = -(-4 * rows // 16) * 16
    tall_group = -(-tall_rows // 16) * 16
    a_sum, b_sum, c_sum = reduce(
        grouped(jnp.stack([grad_query, grad_key, grad_value, grad_out]), group_rows),
        grouped(grad_up, group_rows),
        jnp.pad(
            grad_down.astype(low).reshape(count // 4, 4, tall_rows, model_width),
            ((0, 0), (0, 0), (0, tall_group - tall_rows), (0, 0)),
        ),
        rows,
        (True, False, False),
    )
    red_mod = lax.dot_general(
        silu_rows, d_mod_all, (((0,), (0,)), ((), ())), preferred_element_type=jnp.float32
    )
    a_sum = a_sum.astype(jnp.float32)
    red_qkv = a_sum[:3].transpose(1, 0, 2).reshape(rows, 3 * model_width)
    red_out = a_sum[3]
    red_up = b_sum.astype(jnp.float32).transpose(1, 0, 2).reshape(rows, hidden_width)
    red_down = c_sum[:tall_rows]
    red_bias = jnp.sum(bias_terms.astype(jnp.float32), axis=0)
    d_silu = lax.dot_general(
        d_mod_all, mod_low, (((1,), (1,)), ((), ())), preferred_element_type=jnp.float32
    )
    reduced = (red_mod, red_qkv, red_out, red_up, red_down, red_bias)
    partial_sq = sum((jnp.sum(member * member) for member in reduced))
    last = exchange(
        jnp.concatenate([d_silu, jnp.broadcast_to(partial_sq, (count, 1))], axis=1)
    )
    total_sq = jnp.sum(last[:, rows])
    silu_pull = jax.vjp(silu_act, cond_f)[1]
    cond_grad = silu_pull(last[:, :rows].reshape(1, model_width))[0]
    grad_norm = jnp.sqrt(total_sq)
    factor = jnp.minimum(1.0, CLIP / (grad_norm + 1e-06))
    clipped = tuple((member * factor for member in reduced))
    masters = (mod_weight, qkv_weight, out_weight, up_weight, down_weight, biases)
    states = (mod_state, qkv_state, out_state, up_state, down_state, bias_state)
    updated = [adam_update(masters[index], states[index], clipped[index]) for index in range(6)]
    return (
        (block_out, frames_grad, cond_grad, grad_norm)
        + clipped
        + tuple(pair[0] for pair in updated)
        + tuple(pair[1] for pair in updated)
    )


def fused_shards(
    frames_in,
    conditioning,
    grid,
    cotangent,
    mod_weight,
    qkv_weight,
    out_weight,
    up_weight,
    down_weight,
    biases,
    mod_state,
    qkv_state,
    out_state,
    up_state,
    down_state,
    bias_state,
):
    frame_count, frame_len, model_width = frames_in.shape
    hidden_width = up_weight.shape[1]
    count = lax.axis_size("wide") * lax.axis_size("narrow")
    rows = mod_weight.shape[0]
    tall_rows = down_weight.shape[0]
    low = jnp.bfloat16

    def slices(member):
        return member.reshape(rows, 4, model_width).transpose(1, 0, 2)

    a_src = slices(jnp.concatenate([qkv_weight.astype(low), out_weight.astype(low)], axis=1))
    b_src = slices(up_weight.astype(low))
    cond_f = conditioning.astype(jnp.float32)
    silu_low = silu_act(cond_f).astype(low)
    mod_low = mod_weight.astype(low)
    first = exchange(
        jnp.concatenate(
            [
                silu_low.reshape(count, rows),
                jnp.broadcast_to(biases.astype(low)[None], (count, biases.shape[0])),
            ],
            axis=1,
        )
    )
    silu_rows = first[:, :rows]
    bias_f = first[:, rows:].reshape(-1).astype(jnp.float32)
    bits = count.bit_length() - 1
    crossed = [CORE, 0] + list(range(2, bits))
    sorted_rows = silu_rows.reshape((2,) * bits + (rows,)).transpose(
        [bits - 1 - bit for bit in crossed] + [bits]
    )
    terms = jnp.dot(
        sorted_rows.reshape(count, rows), mod_low, preferred_element_type=jnp.float32
    ).reshape((2,) * bits + (6 * model_width // 128, 128))
    mod_bias = bias_f[: 6 * model_width].reshape(-1, 128)
    bias_rows = bias_f[6 * model_width :].reshape(-1, model_width)
    valid_slots = slot_mask(grid, frame_len)
    row_mask = valid_slots[:, :, None].astype(jnp.float32)
    key_mask = jnp.broadcast_to(valid_slots.astype(jnp.float32), (8, frame_len))
    forward_out = forward(
        a_src, b_src, down_weight.astype(low), terms, mod_bias, bias_rows, frames_in[0], cotangent[0], key_mask, row_mask[0],
    )
    weights, mod_parts, kept, down_sums = forward_out[:3], forward_out[3], forward_out[4:-1], forward_out[-1]
    block_out, frames_grad, d_mod, bias_sums, a_sum, b_sum, c_sum = backward(
        weights, mod_parts, bias_rows, key_mask, row_mask[0], frames_in[0], cotangent[0], kept, rows, bits
    )
    block_out, frames_grad = block_out[None], frames_grad[None]
    d_modulation = d_mod[:6].reshape(1, 6 * model_width).astype(low)
    grad_bias = jnp.concatenate(
        [d_modulation[0].astype(jnp.float32), bias_sums[:7].reshape(-1), down_sums[0]]
    )
    terms = exchange(
        jnp.concatenate(
            [
                jnp.broadcast_to(d_modulation, (count, d_modulation.shape[1])),
                grad_bias.reshape(count, -1).astype(low),
            ],
            axis=1,
        )
    )
    d_mod_all, bias_terms = terms[:, : d_modulation.shape[1]], terms[:, d_modulation.shape[1] :]

    red_mod = lax.dot_general(
        silu_rows, d_mod_all, (((0,), (0,)), ((), ())), preferred_element_type=jnp.float32
    )
    a_sum = a_sum.astype(jnp.float32)
    red_qkv = a_sum[:3].transpose(1, 0, 2).reshape(rows, 3 * model_width)
    red_out = a_sum[3]
    red_up = b_sum.astype(jnp.float32).transpose(1, 0, 2).reshape(rows, hidden_width)
    red_down = c_sum
    red_bias = jnp.sum(bias_terms.astype(jnp.float32), axis=0)
    d_silu = lax.dot_general(
        d_mod_all, mod_low, (((1,), (1,)), ((), ())), preferred_element_type=jnp.float32
    )
    reduced = (red_mod, red_qkv, red_out, red_up, red_down, red_bias)
    partial_sq = sum((jnp.sum(member * member) for member in reduced))
    last = exchange(
        jnp.concatenate([d_silu, jnp.broadcast_to(partial_sq, (count, 1))], axis=1)
    )
    total_sq = jnp.sum(last[:, rows])
    silu_pull = jax.vjp(silu_act, cond_f)[1]
    cond_grad = silu_pull(last[:, :rows].reshape(1, model_width))[0]
    grad_norm = jnp.sqrt(total_sq)
    factor = jnp.minimum(1.0, CLIP / (grad_norm + 1e-06))
    clipped = tuple((member * factor for member in reduced))
    masters = (mod_weight, qkv_weight, out_weight, up_weight, down_weight, biases)
    states = (mod_state, qkv_state, out_state, up_state, down_state, bias_state)
    updated = [adam_update(masters[index], states[index], clipped[index]) for index in range(6)]
    return (
        (block_out, frames_grad, cond_grad, grad_norm)
        + clipped
        + tuple(pair[0] for pair in updated)
        + tuple(pair[1] for pair in updated)
    )


def shards(*arrays):
    rows, tall_rows = arrays[4].shape[0], arrays[8].shape[0]
    fits = 4 * rows % ROUND == 0 and tall_rows % ROUND == 0
    return (fused_shards if fits else plain_shards)(*arrays)


def solution(mesh):
    tokens = P(AXES, None, None)
    matrix = P(AXES, None)
    vector = P(AXES)
    state = P(None, AXES, None)
    weights = (matrix,) * 5 + (vector,)
    states = (state,) * 5 + (P(None, AXES),)
    return jax.shard_map(
        shards,
        mesh=mesh,
        in_specs=(tokens, matrix, matrix, tokens) + weights + states,
        out_specs=(tokens, tokens, matrix, P()) + weights + weights + states,
        check_vma=False,
    )
```

```python
import functools
import jax
import jax.numpy as jnp
from jax import lax
from jax.experimental import pallas as pl
from jax.experimental.pallas import tpu as pltpu
from jax.sharding import PartitionSpec as P

HEADS = 16
STEPS = 4
CLIP = 576
NORM_EPS = 1e-06
RATE = 0.04
FIRST_DECAY = 0.5
SECOND_DECAY = 0.5
WEIGHT_DECAY = 0.1
ADAM_EPS = 1e-08
AVERAGE_DECAY = 0.9999
MASK_VALUE = -1e30
AXES = ("wide", "narrow")

MESH = pl.DeviceIdType.MESH
CORE = 1
ROUND = 16


def orders(bits, late):
    high = list(range(bits - 1, 2, -1))
    if late:
        pair = (high[:-1] + [0, 2] + high[-1:], high[:-1] + [2, 0] + high[-1:])
    else:
        pair = (high + [2, 0], high + [0, 2])
    return tuple(order + [CORE] for order in pair)


def top_place(member):
    return member.bit_length() - 1


def quotient(value, by):
    return lax.div(value, jnp.int32(by))


def remainder(value, by):
    return lax.rem(value, jnp.int32(by))


class Spots:
    def __init__(self, bits):
        wide, narrow = lax.axis_index("wide"), lax.axis_index("narrow")
        self.bits = bits
        self.me = wide * 2 + narrow
        self.quad = remainder(self.me, 4)
        self.group = quotient(self.me, 4)
        self.digit = [remainder(quotient(self.me, 1 << bit), 2) for bit in range(bits)]
        self.core = self.digit[CORE]
        self.delta = [(1 << bit) * (1 - 2 * self.digit[bit]) for bit in range(bits)]
        self.device = [
            (wide, 1 - narrow) if bit == 0 else (wide + (1 << bit - 1) * (1 - 2 * self.digit[bit]), narrow)
            for bit in range(bits)
        ]
        self.steps = {}
        first = self.core == 0
        for late in (False, True):
            pair = orders(bits, late)
            own, other, devices = [], [], []
            for place in range(bits):
                zero, one = pair[0][place], pair[1][place]
                if zero == one:
                    own.append(self.delta[zero])
                    other.append(self.delta[zero])
                    devices.append(self.device[zero])
                else:
                    own.append(jnp.where(first, self.delta[zero], self.delta[one]))
                    other.append(jnp.where(first, self.delta[one], self.delta[zero]))
                    devices.append(
                        tuple(jnp.where(first, a, b) for a, b in zip(self.device[zero], self.device[one]))
                    )
            self.steps[late] = (own, other, devices)
        self.opposite = (self.device[CORE][0], self.device[0][1])

    def block(self, late, member):
        own, other, _ = self.steps[late]
        last = self.bits - 1
        table = other if member >> last & 1 else own
        index = self.me
        for place in range(self.bits):
            if member >> place & 1:
                index = index + table[place]
        return index

    def partner(self, late, place):
        return self.steps[late][2][place]

    def near(self, other):
        if other == 3:
            return self.opposite, 3 - self.quad
        bit = other - 1
        return self.device[bit], self.quad + self.delta[bit]

    def greet(self):
        barrier = pltpu.get_barrier_semaphore()
        partners = self.device + [self.opposite]
        for partner in partners:
            pl.semaphore_signal(barrier, inc=1, device_id=partner, device_id_type=MESH)
        pl.semaphore_wait(barrier, len(partners))


def remote(source, target, send_sem, recv_sem, device):
    copy = pltpu.make_async_remote_copy(
        src_ref=source, dst_ref=target, send_sem=send_sem, recv_sem=recv_sem, device_id=device, device_id_type=MESH
    )
    copy.start()
    return copy


def local(source, target, sem):
    copy = pltpu.make_async_copy(source, target, sem)
    copy.start()
    return copy


def await_bytes(spot, sem):
    pltpu.make_async_copy(spot, spot, sem).wait()


def aligned(start, size, by=16):
    return pl.ds(pl.multiple_of(start, by), size)


def repeat(times, body):
    def run(index, carry):
        body(index)
        return carry

    lax.fori_loop(0, times, run, 0)


class Agenda:
    def __init__(self):
        self.services = []
        self.steps = []
        self.now = 0.0

    def service(self, when, action):
        self.services.append((when, len(self.services), action))

    def step(self, takes, action, after=0.0):
        self.steps.append((takes, action, after))

    def emit(self):
        while self.services or self.steps:
            self.services.sort(key=lambda item: item[:2])
            due = self.services[0][0] if self.services else None
            after = self.steps[0][2] if self.steps else None
            if self.services and (not self.steps or due <= self.now or (after > self.now and due <= after)):
                when, _, action = self.services.pop(0)
                self.now = max(self.now, when) + 0.1
            else:
                takes, action, after = self.steps.pop(0)
                self.now = max(self.now, after) + takes
            action()


def nn(left, right):
    return jnp.dot(left, right, preferred_element_type=jnp.float32)


def nt(left, right):
    return lax.dot_general(left, right, (((1,), (1,)), ((), ())), preferred_element_type=jnp.float32)


def tn(left, right):
    return lax.dot_general(left, right, (((0,), (0,)), ((), ())), preferred_element_type=jnp.float32)


def gelu_parts(value):
    bend = jnp.tanh(0.7978845608028654 * (value + 0.044715 * value * value * value))
    slope = 0.7978845608028654 * (1.0 + 0.134145 * value * value)
    return 0.5 * value * (1.0 + bend), 0.5 * (1.0 + bend) + 0.5 * value * (1.0 - bend * bend) * slope


def normalized(value):
    centre = jnp.mean(value, axis=-1, keepdims=True)
    centred = value - centre
    spread = jnp.mean(centred * centred, axis=-1, keepdims=True)
    root = lax.rsqrt(spread + NORM_EPS)
    return centred * root, root


def head_window(head, size):
    first, last = head * size // 128, (head * size + size - 1) // 128
    return first * 128, (last + 1 - first) * 128, head * size - first * 128


def only_head(values, offset, size):
    lane = lax.broadcasted_iota(jnp.int32, values.shape, 1)
    return jnp.where(jnp.logical_and(lane >= offset, lane < offset + size), values, jnp.zeros((), values.dtype))


STRIP = 32
TILE = 384


def forward_kernel(bits, rows, pieces, clock,
                   a_src, b_src, c_src, terms_in, mod_bias, bias_rows, frames, cot, key_mask, row_mask,
                   a_out, b_out, c_out, mod_out, query_out, key_out, value_out, total_out,
                   branch_out, midway_out, slope_out, active_out, change_out, turned_out, down_out, bias_out,
                   stage, block, c_block, terms, landed, x_ref, first, query, key, value, totals, joined, attended,
                   branch, midway, second, active, active_turned, other_turned, change, other_change, turned,
                   weight, slope_stage, down_stage,
                   quad_send, quad_recv, own_sem, keep_sem, send_sem, recv_sem, term_send, term_recv,
                   pair_send, pair_recv, load_sem, weight_sem, save_sem, slope_sem, down_sem):
    count = 1 << bits
    spots = Spots(bits)
    quad, core = spots.quad, spots.core
    sibling = spots.device[CORE]
    outs = (a_out, b_out, c_out)
    tall_rows = c_src.shape[0]
    tokens, width = first.shape
    size = width // HEADS
    scale = size ** (-0.5)
    low = jnp.bfloat16
    finals = []

    def save(source, target, index):
        finals.append(local(source, target, save_sem.at[index]).wait)

    def place(piece, index):
        kind, start, length, _ = pieces[piece]
        if kind == 2:
            return c_out.at[aligned(index * tall_rows + start, length)]
        return outs[kind].at[remainder(index, 4), aligned(quotient(index, 4) * (4 * rows) + start, length)]

    def of_kind(kind):
        return [piece for piece, entry in enumerate(pieces) if entry[0] == kind]

    own = [local(source.at[quad], stage.at[kind, quad], own_sem.at[kind]) for kind, source in enumerate((a_src, b_src))]
    own.append(local(c_src, c_block, own_sem.at[2]))
    loads = [local(terms_in, terms, load_sem.at[0]), local(frames, x_ref, load_sem.at[1])]
    spots.greet()
    quads = []

    def start_quad(kind, source):
        for other in (1, 2, 3):
            device, spot = spots.near(other)
            copy = remote(source.at[spot], stage.at[kind, quad], quad_send.at[kind, other], quad_recv.at[kind, other], device)
            quads.append(copy)
            finals.append(copy.wait_send)

    keeps = {}

    def launch(piece, member, source):
        late = pieces[piece][3]
        spot = spots.block(late, member)
        for step in range(top_place(member) + 1, bits):
            target = member | 1 << step
            copy = remote(
                source, place(piece, spot), send_sem.at[piece, target], recv_sem.at[piece, target], spots.partner(late, step)
            )
            finals.append(copy.wait_send)

    def open_pieces(kind, source):
        for piece in of_kind(kind):
            _, start, length, _ = pieces[piece]
            part = source.at[pl.ds(start, length)]
            launch(piece, 0, part)
            keeps[piece] = local(part, place(piece, spots.me), keep_sem.at[piece])

    def arrived(piece, member):
        spot = place(piece, spots.block(pieces[piece][3], member))
        await_bytes(spot, recv_sem.at[piece, member])
        return spot

    def open_quad(kind):
        own[kind].wait()
        for copy in quads[3 * kind : 3 * kind + 3]:
            copy.wait_recv()
        for lane in range(0, width, 128):
            parts = [stage[kind, q, :, lane : lane + 128].astype(jnp.float32) for q in range(4)]
            block[kind, :, lane : lane + 128] = jnp.concatenate(parts, axis=0).astype(low)
        open_pieces(kind, block.at[kind])

    crossed = [CORE, 0] + list(range(2, bits))
    term_copies = []

    def start_term(step):
        given = tuple(spots.digit[bit] for bit in crossed[:step]) + (1 - spots.digit[crossed[step]],)
        copy = remote(terms.at[given], landed[step], term_send.at[step], term_recv.at[step], spots.device[crossed[step]])
        term_copies.append(copy)
        finals.append(copy.wait_send)

    def end_term(step):
        kept = tuple(spots.digit[bit] for bit in crossed[: step + 1])
        term_copies[step].wait_recv()
        terms[kept] = terms[kept] + landed[step][...]
        if step + 1 < bits:
            start_term(step + 1)
            return
        parts = terms[kept] + mod_bias[...]
        per = width // 128
        for at in range(6 * per):
            part, lane = at // per, at % per * 128
            mod_out[part : part + 1, lane : lane + 128] = parts[at : at + 1, :]

    start_quad(0, a_src)
    loads[0].wait()
    start_term(0)
    own[2].wait()
    open_pieces(2, c_block)
    open_quad(0)
    start_quad(1, b_src)
    open_quad(1)
    agenda = Agenda()
    for step in range(bits):
        agenda.service(clock["terms"][0] + clock["terms"][1] * step, functools.partial(end_term, step))
    full = [0.0] * 3
    for piece, (kind, _, _, _) in enumerate(pieces):
        begin, pace = clock["pieces"][piece]
        for member in range(1, count // 2):
            agenda.service(
                begin + pace * member,
                lambda piece=piece, member=member: launch(piece, member, arrived(piece, member)),
            )
        full[kind] = max(full[kind], begin + pace * (count // 2) + clock["settle"])

    def finish(kind):
        for piece in of_kind(kind):
            for member in range(count // 2, count):
                arrived(piece, member)
            keeps[piece].wait()

    def load_weight(kind, q, slot):
        return local(outs[kind].at[q], weight.at[slot], weight_sem.at[slot])

    def over_strips(body):
        repeat(tokens // STRIP, lambda s: body(aligned(s * STRIP, STRIP, STRIP)))

    def over_tiles(body):
        repeat(width // TILE, lambda t: body(aligned(t * TILE, TILE, 128)))

    pairs = {}

    def trade(index, source, target):
        pairs[index] = remote(source, target, pair_send.at[index], pair_recv.at[index], sibling)
        finals.append(pairs[index].wait_send)

    def turn(source, index):
        repeat(
            width // 128,
            lambda t: turned.__setitem__(
                (index, aligned(t * 128, 128, 128)), source[:, aligned(t * 128, 128, 128)].T
            ),
        )
        save(turned.at[index], turned_out.at[index, 0], 8 + index)
        trade(index, turned.at[index], turned_out.at[index, 1])
        finals.append(pairs[index].wait_recv)

    def norm_first():
        loads[1].wait()

        def body(where):
            unit, _ = normalized(x_ref[where, :].astype(jnp.float32))
            first[where, :] = (unit * (1.0 + mod_out[1:2, :]) + mod_out[0:1, :]).astype(low)
            upstream = cot[where, :].astype(jnp.float32) * row_mask[where, :]
            change[where, :] = (mod_out[5:6, :] * upstream).astype(low)

        over_strips(body)
        save(change, change_out, 0)
        trade(3, change, other_change)
        bias_out[...] = jnp.zeros_like(bias_out)
        bias_out[0:1, :] = jnp.sum(change[...].astype(jnp.float32), axis=0, keepdims=True)

    weight_loads = {}

    def begin_first():
        finish(0)
        for s in range(2):
            weight_loads[s] = load_weight(0, s, s)

    def project(s, target, bias):
        slot = s % 2
        weight_loads[s].wait()

        def body(where):
            result = nn(first[...], weight[slot, :, where])
            if bias is not None:
                result = result + bias_rows[bias : bias + 1, where]
            target[:, where] = result.astype(low)

        over_tiles(body)
        if s + 2 < 4:
            weight_loads[s + 2] = load_weight(0, s + 2, slot)
        save(target, (query_out, key_out, value_out)[s], 1 + s)

    def clear():
        joined[...] = jnp.zeros_like(joined)
        totals[...] = jnp.zeros_like(totals)

    def attend(head):
        start, span, offset = head_window(head, size)
        where = slice(start, start + span)
        scores = nt(only_head(query[:, where], offset, size), key[:, where])
        scores = jnp.where(key_mask[0:1, :] > 0, scores * scale, MASK_VALUE)
        peak = jnp.max(scores, axis=-1, keepdims=True)
        power = jnp.exp(scores - peak)
        total = jnp.sum(power, axis=-1, keepdims=True)
        attention = (power / total).astype(low)
        joined[:, where] = joined[:, where] + nn(attention, only_head(value[:, where], offset, size))
        lane = lax.broadcasted_iota(jnp.int32, (tokens, 128), 1)
        totals[...] = jnp.where(lane == head, peak + jnp.log(total), totals[...])

    def leave_attention():
        attended[...] = joined[...].astype(low)
        save(totals, total_out, 4)
        weight_loads[3].wait()

        def body(where):
            result = nn(attended[...], weight[1, :, where]) + bias_rows[2:3, where]
            branch[:, where] = result
            midway[:, where] = x_ref[:, where].astype(jnp.float32) + mod_out[2:3, where] * result

        over_tiles(body)
        save(branch, branch_out, 5)
        save(midway, midway_out, 6)

    def norm_second():
        def body(where):
            unit, _ = normalized(midway[where, :])
            second[where, :] = (unit * (1.0 + mod_out[4:5, :]) + mod_out[3:4, :]).astype(low)

        over_strips(body)

    up_loads = {}
    slope_copies = {}

    def begin_up():
        finish(1)
        for s in range(2):
            up_loads[s] = load_weight(1, s, s)

    def raise_up(s):
        slot = s % 2
        up_loads[s].wait()
        if s >= 2:
            slope_copies[s - 2].wait()

        def body(t):
            where = aligned(t * TILE, TILE, 128)
            wide = aligned(s * width + t * TILE, TILE, 128)
            bent, slope = gelu_parts(nn(second[...], weight[slot, :, where]) + bias_rows[aligned(3 + s, 1, 1), where])
            active[:, wide] = bent.astype(low)
            active_turned[wide, :] = bent.astype(low).T
            slope_stage[slot, :, where] = slope

        repeat(width // TILE, body)
        if s + 2 < 4:
            up_loads[s + 2] = load_weight(1, s + 2, slot)
        slope_copies[s] = local(
            slope_stage.at[slot], slope_out.at[:, pl.ds(s * width, width)], slope_sem.at[slot]
        )

    span = 2 * tall_rows

    def plane_rows(j, plane):
        return aligned((2 * j + plane) * span, span)

    def trade_active():
        save(active, active_out, 7)
        for j in range(count // 4):
            trade(4 + j, active_turned.at[plane_rows(j, 1 - core)], other_turned.at[pl.ds(j * span, span)])

    down_copies = {}

    def down_gradient(j):
        slot = j % 2
        if j == 0:
            pairs[3].wait_recv()
        if j >= 2:
            down_copies[j - 2].wait()
        pairs[4 + j].wait_recv()

        def body(where):
            result = nn(active_turned[plane_rows(j, core), :], change[:, where])
            result = result + nn(other_turned[j * span : (j + 1) * span, :], other_change[:, where])
            down_stage[slot, :, where] = result.astype(low)

        over_tiles(body)
        down_copies[j] = local(down_stage.at[slot], down_out.at[pl.ds(j * span, span)], down_sem.at[slot])

    takes = clock["takes"]
    agenda.step(takes["norm"], norm_first, clock["terms"][0] + clock["terms"][1] * bits)
    agenda.step(takes["turn"], lambda: turn(first, 0))
    agenda.step(0.3, begin_first, full[0])
    for s, (target, bias) in enumerate(((query, 0), (key, None), (value, 1))):
        agenda.step(takes["matmul"], functools.partial(project, s, target, bias))
    agenda.step(0.3, clear)
    for head in range(HEADS):
        agenda.step(takes["head"], functools.partial(attend, head))
    agenda.step(takes["matmul"], leave_attention)
    agenda.step(takes["norm"], norm_second)
    agenda.step(0.3, begin_up, full[1])
    for s in range(4):
        agenda.step(takes["up"], functools.partial(raise_up, s))
    agenda.step(0.3, trade_active)
    agenda.step(takes["turn"], lambda: turn(attended, 1))
    agenda.step(takes["turn"], lambda: turn(second, 2))
    for j in range(count // 4):
        agenda.step(takes["down"], functools.partial(down_gradient, j))
    agenda.emit()
    finish(2)
    for done in finals:
        done()
    for table in (slope_copies, down_copies):
        for index in sorted(table)[-2:]:
            table[index].wait()


PIECES = ((0, 0, 96, False), (0, 96, 48, True), (1, 0, 96, False), (1, 96, 48, True), (2, 0, 96, False), (2, 96, 48, True))
CLOCK = {
    "terms": (12.0, 5.0),
    "pieces": ((8.0, 2.4), (8.0, 2.4), (16.0, 4.6), (16.0, 4.6), (24.0, 6.6), (24.0, 6.6)),
    "settle": 3.0,
    "takes": {"norm": 2.0, "turn": 0.6, "matmul": 2.0, "head": 0.8, "up": 3.5, "down": 1.2},
}


def forward(a_src, b_src, c_src, terms, mod_bias, bias_rows, frames, cot, key_mask, row_mask, pieces=PIECES, clock=CLOCK):
    rows, width = a_src.shape[1:]
    tall = c_src.shape[0]
    bits = terms.ndim - 2
    count = 1 << bits
    tokens = frames.shape[0]
    hidden = tall * count
    low, wide = jnp.bfloat16, jnp.float32

    def shaped(*sizes, dtype=low):
        return jax.ShapeDtypeStruct(sizes, dtype)

    anywhere = pl.BlockSpec(memory_space=pl.ANY)
    near = pl.BlockSpec(memory_space=pltpu.VMEM)
    token = shaped(tokens, width)
    token_wide = shaped(tokens, width, dtype=wide)
    outs = (
        shaped(4, width, width), shaped(4, width, width), shaped(hidden, width),
        shaped(8, width, dtype=wide),
        token, token, token, shaped(tokens, 128, dtype=wide),
        token_wide, token_wide,
        shaped(tokens, hidden, dtype=wide), shaped(tokens, hidden), token,
        shaped(3, 2, width, tokens),
        shaped(hidden // 2, width), shaped(8, width, dtype=wide),
    )
    out_specs = [anywhere] * len(outs)
    out_specs[3] = near
    out_specs[-1] = near
    dma = pltpu.SemaphoreType.DMA
    v = pltpu.VMEM
    scratch = [
        v((2, 4, rows, width), low), v((2, 4 * rows, width), low), v((tall, width), low),
        v(terms.shape, wide), tuple(v(terms.shape[step + 1 :], wide) for step in range(bits)),
        v((tokens, width), low), v((tokens, width), low),
        v((tokens, width), low), v((tokens, width), low), v((tokens, width), low),
        v((tokens, 128), wide), v((tokens, width), wide), v((tokens, width), low),
        v((tokens, width), wide), v((tokens, width), wide), v((tokens, width), low),
        v((tokens, hidden), low), v((hidden, tokens), low), v((hidden // 2, tokens), low),
        v((tokens, width), low), v((tokens, width), low), v((3, width, tokens), low),
        v((2, width, width), low), v((2, tokens, width), wide), v((2, 2 * tall, width), low),
        dma((2, 4)), dma((2, 4)), dma((3,)), dma((len(pieces),)), dma((len(pieces), count)), dma((len(pieces), count)),
        dma((bits,)), dma((bits,)), dma((4 + count // 4,)), dma((4 + count // 4,)),
        dma((2,)), dma((2,)), dma((16,)), dma((2,)), dma((2,)),
    ]
    return pl.pallas_call(
        functools.partial(forward_kernel, bits, rows, pieces, clock),
        out_shape=outs,
        in_specs=[anywhere] * 4 + [near] * 2 + [anywhere] + [near] * 3,
        out_specs=out_specs,
        scratch_shapes=scratch,
        compiler_params=pltpu.CompilerParams(collective_id=0, has_side_effects=True, vmem_limit_bytes=56 * 1024 * 1024),
        cost_estimate=pl.CostEstimate(flops=10_000_000_000, bytes_accessed=400_000_000, transcendentals=3_000_000),
        name="forward_gather",
    )(a_src, b_src, c_src, terms, mod_bias, bias_rows, frames, cot, key_mask, row_mask)


def SPREAD(bits):
    return list(range(bits - 1, 1, -1)) + [0, CORE]


def folded_rows(values):
    whole = values.shape[0] // 8 * 8
    result = sum(values[at : at + 8, :] for at in range(0, whole, 8))
    if whole < values.shape[0]:
        rest = values[whole:, :]
        result = result + jnp.concatenate([rest, jnp.zeros((8 - rest.shape[0], rest.shape[1]), rest.dtype)], axis=0)
    return result


def bias_sums(halves, count):
    shape = (ROUND, ROUND * count // 2)
    pick = jnp.where(
        remainder(lax.broadcasted_iota(jnp.int32, shape, 1), ROUND) == lax.broadcasted_iota(jnp.int32, shape, 0), 1.0, 0.0
    ).astype(jnp.bfloat16)
    return nn(pick, halves[0]) + nn(pick, halves[1])


def lifted(lift, part, halves, count):
    half = ROUND * count // 2
    return nn(lift[part, :, :half], halves[0]) + nn(lift[part, :, half:], halves[1])


def backward_kernel(bits, rows, tall_rows, pieces, clock,
                    a_all, b_all, c_all, mod, bias_rows, down_sums, key_mask, row_mask, lift, mod_low, frames, cot_in, query_in, key_in, value_in,
                    total_in, branch_in, midway_in, slope_in, active_in, change_in, turned_in, down_in,
                    block_out, frames_out, spread_out, a_out, b_out, c_out, ordered, norm_out,
                    weight, slabs, other_up, other_low, active, slope, query, key, value, x_ref, cot, change, d_attended,
                    midway, branch, down_acc, d_norm, d_midway, turned, totals, first_grads, second_grads, third_grads, recv, total,
                    quad_block, dmod, bias_out, spread, squares, table, answers,
                    weight_sem, stream_sem, load_sem, save_sem, send_sem, recv_sem, pair_send, pair_recv,
                    quad_send, quad_recv, quad_own, spread_send, spread_recv, spread_own,
                    answer_send, answer_recv):
    count = 1 << bits
    spots = Spots(bits)
    core = spots.core
    sibling = spots.device[CORE]
    tokens, width = x_ref.shape
    size = width // HEADS
    scale = size ** (-0.5)
    low, wide = jnp.bfloat16, jnp.float32
    span = 2 * tall_rows
    finals = []

    grads_load = local(down_in, first_grads, load_sem.at[0])
    order = [(c_all, s, True) for s in range(4)] + [(b_all, s, False) for s in range(4)]
    order += [(a_all, 3, False), (a_all, 0, False), (a_all, 1, False), (a_all, 2, False)]
    weights = {}

    def load_weight(index):
        if index < len(order):
            source, s, flat = order[index]
            part = source.at[pl.ds(s * width, width)] if flat else source.at[s]
            weights[index] = local(part, weight.at[index % 2], weight_sem.at[index % 2])

    streams = {}

    def load_stream(s):
        if s < 4:
            where = pl.ds(s * width, width)
            streams[s] = (
                local(slope_in.at[:, where], slope.at[s % 2], stream_sem.at[0, s % 2]),
                local(active_in.at[:, where], active.at[s % 2], stream_sem.at[1, s % 2]),
            )

    change_load = local(change_in, change, load_sem.at[1])
    load_weight(0)
    load_stream(0)
    load_weight(1)
    load_stream(1)
    loads = {
        name: local(source, target, load_sem.at[2 + index])
        for index, (name, source, target) in enumerate(
            (
                ("second", turned_in.at[2], turned.at[2]), ("midway", midway_in, midway), ("cot", cot_in, cot),
                ("branch", branch_in, branch), ("value", value_in, value), ("query", query_in, query), ("key", key_in, key),
                ("totals", total_in, totals), ("first", turned_in.at[0], turned.at[0]),
                ("attended", turned_in.at[1], turned.at[1]), ("x", frames, x_ref),
            )
        )
    }
    spots.greet()
    dmod[...] = jnp.zeros_like(dmod)
    bias_out[...] = jnp.zeros_like(bias_out)
    squares[...] = jnp.zeros_like(squares)

    grads = (third_grads, second_grads, first_grads)
    sums_at = (0, 1, 0)
    block_stage, frames_stage = change, d_attended
    down_copies = []

    def own(piece, member):
        kind, start, length, late = pieces[piece]
        index = spots.block(late, member)
        row = remainder(index, 2) * (tall_rows if kind == 2 else width)
        row = row + quotient(index, 4) * (span if kind == 2 else 4 * rows)
        return grads[kind].at[aligned(row + start, length)]

    def landed(piece, member):
        kind, start, length, _ = pieces[piece]
        return recv.at[kind, member - 1, pl.ds(start, length)]

    sent = {kind: [] for kind in range(3)}

    def pass_on(piece, member):
        kind, _, _, late = pieces[piece]
        place = top_place(member)
        sent[kind].append(
            remote(
                own(piece, member), landed(piece, member), send_sem.at[piece, member], recv_sem.at[piece, member],
                spots.partner(late, place),
            )
        )

    def summed(piece, member, body):
        parts = [member | 1 << place for place in range(top_place(member) + 1, bits - 1)]
        for part in parts:
            await_bytes(landed(piece, part), recv_sem.at[piece, part])
        kind, start, length, _ = pieces[piece]
        mine = own(piece, member)

        def strip(s):
            where = aligned(s * ROUND, ROUND)
            value = mine[where, :].astype(wide)
            for part in parts:
                value = value + recv[kind, part - 1, aligned(start + s * ROUND, ROUND), :].astype(wide)
            body(mine, where, s, value)

        repeat(length // ROUND, strip)

    def relay(piece, member):
        def body(mine, where, s, value):
            mine[where, :] = value.astype(low)

        summed(piece, member, body)
        pass_on(piece, member)

    left = {kind: len([1 for entry in pieces if entry[0] == kind]) for kind in range(3)}

    def settle(piece):
        kind, start, length, _ = pieces[piece]

        def body(mine, where, s, value):
            total[sums_at[kind], aligned(start + s * ROUND, ROUND), :] = value
            squares[...] = squares[...] + value * value

        if kind == 0:
            while down_copies:
                down_copies.pop().wait()
        summed(piece, 0, body)
        left[kind] -= 1
        if left[kind]:
            return
        if kind == 2:
            down_copies.append(local(total.at[0], c_out, save_sem.at[0]))
            return
        for lane in range(0, width, 128):
            for q in range(4):
                part = total[sums_at[kind], q * rows : (q + 1) * rows, lane : lane + 128]
                quad_block[kind, q, :, lane : lane + 128] = part.astype(low)
        out = (a_out, b_out)[kind]
        finals.append(local(quad_block.at[kind, spots.quad], out.at[spots.quad], quad_own.at[kind]).wait)
        for other in (1, 2, 3):
            device, spot = spots.near(other)
            copy = remote(
                quad_block.at[kind, spot], out.at[spots.quad], quad_send.at[kind, other], quad_recv.at[kind, other], device
            )
            finals.append(copy.wait)

    agenda = Agenda()

    def open_kind(kind):
        half = count // 2
        for member in range(half - 1, half // 2 - 1, -1):
            for piece, entry in enumerate(pieces):
                if entry[0] == kind:
                    pass_on(piece, member)
        begin, pace = clock["open"][kind]
        for piece, entry in enumerate(pieces):
            if entry[0] == kind:
                for at, member in enumerate(range(half // 2 - 1, 0, -1)):
                    agenda.service(agenda.now + begin + pace * at, functools.partial(relay, piece, member))
                agenda.service(agenda.now + begin + pace * (half // 2 - 1), functools.partial(settle, piece))

    def open_down():
        grads_load.wait()
        open_kind(2)

    pairs = {}

    def trade(index, source, target):
        pairs[index] = remote(source, target, pair_send.at[index], pair_recv.at[index], sibling)

    def over_strips(body):
        repeat(tokens // STRIP, lambda s: body(aligned(s * STRIP, STRIP, STRIP)))

    def over_tiles(body):
        repeat(width // TILE, lambda t: body(aligned(t * TILE, TILE, 128)))

    def add_row(ref, row, where, values):
        ref[row : row + 1, where] = ref[row : row + 1, where] + jnp.sum(values, axis=0, keepdims=True)

    everything = slice(None)

    def down_slice(s):
        slot = s % 2
        if s == 0:
            change_load.wait()
        weights[s].wait()
        for copy in streams[s]:
            copy.wait()

        def body(where):
            d_up = (nt(change[...], weight[slot, where, :]) * slope[slot, :, where]).astype(low)
            slabs[s, :, where] = d_up
            add_row(bias_out, 3 + s, where, d_up.astype(wide))
            part = nn(active[slot], weight[slot, :, where])
            down_acc[:, where] = part if s == 0 else down_acc[:, where] + part

        over_tiles(body)
        load_weight(s + 2)
        load_stream(s + 2)

    def trade_up():
        for t in range(2):
            trade(t, slabs.at[2 * (1 - core) + t], other_up.at[t])

    def up_gradient(t):
        if t == 0:
            loads["second"].wait()
        pairs[t].wait_recv()

        def body(where):
            def strip(m):
                down = aligned(m * 288, 288)
                result = nn(turned[2, 0, down, :], slabs[2 * core + t, :, where])
                result = result + nn(turned[2, 1, down, :], other_up[t, :, where])
                second_grads[aligned(t * width + m * 288, 288), where] = result.astype(low)

            repeat(width // 288, strip)

        over_tiles(body)

    def norm_two_slice(s):
        weights[4 + s].wait()

        def body(where):
            part = nt(slabs[s], weight[s % 2, where, :])
            d_norm[:, where] = part if s == 0 else d_norm[:, where] + part

        over_tiles(body)
        load_weight(6 + s)

    def upstream_of(where):
        return cot[where, :].astype(wide) * row_mask[where, :]

    def norm_back(values, gradient, gain):
        unit, root = normalized(values)
        spread = gain * gradient
        back = root * (
            spread
            - jnp.mean(spread, axis=-1, keepdims=True)
            - unit * jnp.mean(spread * unit, axis=-1, keepdims=True)
        )
        return unit, back

    def back_second():
        for name in ("midway", "cot", "branch"):
            loads[name].wait()
        for t in range(2):
            pairs[t].wait_send()

        def body(where):
            gradient = d_norm[where, :]
            unit, back = norm_back(midway[where, :], gradient, 1.0 + mod[4:5, :])
            middle = upstream_of(where) + back
            d_midway[where, :] = middle
            d_branch = (mod[2:3, :] * middle).astype(low)
            slabs[3, where, :] = d_branch
            add_row(dmod, 3, everything, gradient)
            add_row(dmod, 4, everything, gradient * unit)
            add_row(dmod, 2, everything, middle * branch[where, :])
            add_row(bias_out, 2, everything, d_branch.astype(wide))

        over_strips(body)

    def back_attended():
        weights[8].wait()

        def body(where):
            d_attended[:, where] = nt(slabs[3], weight[0, where, :]).astype(low)

        over_tiles(body)
        load_weight(10)
        for name in ("value", "query", "key", "totals"):
            loads[name].wait()
        slope[...] = jnp.zeros_like(slope)
        branch[...] = jnp.zeros_like(branch)

    def attend_back(head):
        start, reach, offset = head_window(head, size)
        where = slice(start, start + reach)
        chosen = only_head(query[:, where], offset, size)
        scores = nt(chosen, key[:, where])
        scores = jnp.where(key_mask[0:1, :] > 0, scores * scale, MASK_VALUE)
        soft = jnp.exp(scores - totals[:, head : head + 1])
        given = only_head(d_attended[:, where], offset, size)
        d_soft = nt(given, value[:, where])
        d_scores = (soft * (d_soft - jnp.sum(soft * d_soft, axis=-1, keepdims=True))).astype(low)
        slope[0, :, where] = slope[0, :, where] + nn(d_scores, only_head(key[:, where], offset, size))
        slope[1, :, where] = slope[1, :, where] + tn(d_scores, chosen)
        branch[:, where] = branch[:, where] + tn(soft.astype(low), given)

    def leave_attention():
        slabs[0] = (slope[0] * scale).astype(low)
        slabs[1] = (slope[1] * scale).astype(low)
        slabs[2] = branch[...].astype(low)
        for t in range(2):
            trade(2 + t, slabs.at[2 * (1 - core) + t], other_low.at[t])
        bias_out[0:1, :] = jnp.sum(slabs[0].astype(wide), axis=0, keepdims=True)
        bias_out[1:2, :] = jnp.sum(slabs[2].astype(wide), axis=0, keepdims=True)

    def leave_block():
        def body(where):
            down = down_acc[where, :] + bias_rows[7:8, :]
            add_row(dmod, 5, everything, upstream_of(where) * down)
            block_stage[where, :] = ((midway[where, :] + mod[5:6, :] * down) * row_mask[where, :]).astype(low)

        over_strips(body)
        finals.append(local(block_stage, block_out, save_sem.at[1]).wait)

    def low_gradient(t):
        if t == 0:
            loads["first"].wait()
            loads["attended"].wait()
        pairs[2 + t].wait_recv()
        at = 2 * core + t
        which = quotient(at, 3)

        def body(where):
            def strip(m):
                down = aligned(m * 288, 288)
                result = nn(turned[which, 0, down, :], slabs[at, :, where])
                result = result + nn(turned[which, 1, down, :], other_low[t, :, where])
                third_grads[aligned(t * width + m * 288, 288), where] = result.astype(low)

            repeat(width // 288, strip)

        over_tiles(body)

    def norm_one_slice(s):
        weights[9 + s].wait()

        def body(where):
            part = nt(slabs[s], weight[(9 + s) % 2, where, :])
            d_norm[:, where] = part if s == 0 else d_norm[:, where] + part

        over_tiles(body)
        load_weight(11 + s)

    def back_first():
        loads["x"].wait()

        def body(where):
            gradient = d_norm[where, :]
            unit, back = norm_back(x_ref[where, :].astype(wide), gradient, 1.0 + mod[1:2, :])
            add_row(dmod, 0, everything, gradient)
            add_row(dmod, 1, everything, gradient * unit)
            frames_stage[where, :] = (back + d_midway[where, :]).astype(low)

        over_strips(body)
        finals.append(local(frames_stage, frames_out, save_sem.at[2]).wait)

    spread_copies = []

    def spread_step(step):
        if step == 0:
            spread_start.wait()
        else:
            spread_copies[step - 1].wait_recv()
        if step == bits:
            use_spread()
            return
        held = pl.ds(0, ROUND << step)
        copy = remote(
            spread_out.at[held], spread_out.at[pl.ds(ROUND << step, ROUND << step)], spread_send.at[step],
            spread_recv.at[step], spots.device[SPREAD(bits)[step]],
        )
        spread_copies.append(copy)
        finals.append(copy.wait_send)
        agenda.service(agenda.now + clock["spread"], functools.partial(spread_step, step + 1))

    def start_spread():
        nonlocal spread_start
        bias_out[7:8, :] = down_sums[0:1, :]
        spread[...] = jnp.concatenate([dmod[...], bias_out[...]], axis=0).astype(low)
        spread_start = local(spread, spread_out.at[pl.ds(0, ROUND)], spread_own)
        agenda.service(agenda.now + 1.0, functools.partial(spread_step, 0))

    def use_spread():
        half = ROUND * count // 2
        copies = [local(spread_out.at[pl.ds(t * half, half)], active.at[t], stream_sem.at[1, t]) for t in range(2)]
        for copy in copies:
            copy.wait()
        both = bias_sums(active, count)
        squares[...] = squares[...] + both * both * (1.0 / count)
        member = remainder(lax.broadcasted_iota(jnp.int32, (half, rows), 0), ROUND)
        partial = [jnp.zeros((half, rows), wide) for _ in range(2)]
        for part in range(6):
            where = slice(part * width, (part + 1) * width)
            value = lifted(lift, part, active, count)
            squares[0:8, :] = squares[0:8, :] + folded_rows(value * value)
            for t in range(2):
                partial[t] = partial[t] + jnp.where(member == part, nt(active[t], mod_low[:, where]), 0.0)
        table[...] = jnp.zeros_like(table)
        shape = (count // 2, half)
        gathers = jnp.where(
            quotient(lax.broadcasted_iota(jnp.int32, shape, 1), ROUND) == lax.broadcasted_iota(jnp.int32, shape, 0), 1.0, 0.0
        )
        for t in range(2):
            table[t * count // 2 : (t + 1) * count // 2, 0:rows] = jnp.dot(
                gathers, partial[t], preferred_element_type=wide, precision=lax.Precision.HIGHEST
            )

    def answer():
        total_square = jnp.sum(squares[...], axis=0, keepdims=True)
        folded = sum(total_square[:, at : at + 128] for at in range(0, width, 128))
        table[count : count + 8, :] = jnp.broadcast_to(folded, (8, 128))
        slot = lax.broadcasted_iota(jnp.int32, (count, 128), 0)
        for step, bit in enumerate(SPREAD(bits)):
            copy = remote(table, answers.at[step], answer_send.at[step], answer_recv.at[step], spots.device[bit])
            copy.wait()
            given = jnp.where(remainder(quotient(slot, 1 << step), 2) == 1, answers[step, 0:count, :], table[0:count, :])
            summed_up = table[count : count + 8, :] + answers[step, count : count + 8, :]
            table[0:count, :] = given
            table[count : count + 8, :] = summed_up
        for member in range(count):
            index = spots.me
            for step, bit in enumerate(SPREAD(bits)):
                if member >> step & 1:
                    index = index + spots.delta[bit]
            ordered[pl.ds(index, 1), :] = table[member : member + 1, :]
        norm_out[...] = jnp.broadcast_to(jnp.sqrt(jnp.sum(table[count : count + 8, :], axis=1, keepdims=True)), (8, 128))

    spread_start = None
    takes = clock["takes"]
    agenda.step(2.0, open_down)
    for s in range(4):
        agenda.step(takes["down"], functools.partial(down_slice, s))
    agenda.step(0.3, trade_up)
    for t in range(2):
        agenda.step(takes["gradient"], functools.partial(up_gradient, t))
    agenda.step(0.5, lambda: open_kind(1))
    for s in range(4):
        agenda.step(takes["matmul"], functools.partial(norm_two_slice, s))
    agenda.step(takes["norm"], back_second)
    agenda.step(takes["matmul"], back_attended)
    for head in range(HEADS):
        agenda.step(takes["head"], functools.partial(attend_back, head))
    agenda.step(1.0, leave_attention)
    agenda.step(takes["norm"], leave_block)
    for t in range(2):
        agenda.step(takes["gradient"], functools.partial(low_gradient, t))
    agenda.step(0.5, lambda: open_kind(0))
    for s in range(3):
        agenda.step(takes["matmul"], functools.partial(norm_one_slice, s))
    agenda.step(takes["norm"], back_first)
    agenda.step(0.5, start_spread)
    agenda.emit()
    answer()
    for kind in range(3):
        for copy in sent[kind]:
            copy.wait_send()
    for t in range(2):
        pairs[2 + t].wait_send()
    for done in finals:
        done()


BACK_CLOCK = {
    "spread": 4.0,
    "open": ((22.0, 4.0), (24.0, 5.5), (20.0, 5.0)),
    "takes": {"down": 4.2, "gradient": 4.2, "matmul": 2.1, "norm": 1.7, "head": 0.42},
}


def backward(weights, mod, bias_rows, down_sums, key_mask, row_mask, lift, mod_low, frames, cot, saved, rows, bits, pieces=PIECES, clock=BACK_CLOCK):
    a_all, b_all, c_all = weights
    width = a_all.shape[-1]
    count = 1 << bits
    hidden = c_all.shape[0]
    tall = hidden // count
    tokens = frames.shape[0]
    low, wide = jnp.bfloat16, jnp.float32

    def shaped(*sizes, dtype=low):
        return jax.ShapeDtypeStruct(sizes, dtype)

    anywhere = pl.BlockSpec(memory_space=pl.ANY)
    near = pl.BlockSpec(memory_space=pltpu.VMEM)
    dma = pltpu.SemaphoreType.DMA
    v = pltpu.VMEM
    kinds = len(pieces)
    scratch = [
        v((2, width, width), low), v((4, tokens, width), low),
        v((2, tokens, width), low), v((2, tokens, width), low),
        v((2, tokens, width), low), v((2, tokens, width), wide),
        v((tokens, width), low), v((tokens, width), low), v((tokens, width), low),
        v((tokens, width), low), v((tokens, width), low), v((tokens, width), low), v((tokens, width), low),
        v((tokens, width), wide), v((tokens, width), wide),
        v((tokens, width), wide), v((tokens, width), wide), v((tokens, width), wide),
        v((3, 2, width, tokens), low), v((tokens, 128), wide),
        v((2 * width, width), low), v((2 * width, width), low), v((2 * width, width), low),
        v((3, count // 2 - 1, 4 * rows, width), low), v((2, 4 * rows, width), wide), v((2, 4, rows, width), low),
        v((8, width), wide), v((8, width), wide), v((ROUND, width), low),
        v((ROUND, width), wide), v((count + 8, 128), wide), v((bits, count + 8, 128), wide),
        dma((2,)), dma((2, 2)), dma((13,)), dma((3,)), dma((kinds, count // 2)), dma((kinds, count // 2)),
        dma((4,)), dma((4,)), dma((2, 4)), dma((2, 4)), dma((2,)), dma((bits,)), dma((bits,)), dma, dma((bits,)), dma((bits,)),
    ]
    share = shaped(4, rows, width)
    return pl.pallas_call(
        functools.partial(backward_kernel, bits, rows, tall, pieces, clock),
        out_shape=(
            shaped(tokens, width), shaped(tokens, width), shaped(ROUND * count, width),
            share, share, shaped(tall, width, dtype=wide), shaped(count, 128, dtype=wide), shaped(8, 128, dtype=wide),
        ),
        in_specs=[anywhere] * 3 + [near] * 7 + [anywhere] * (2 + len(saved)),
        out_specs=[anywhere] * 6 + [near] * 2,
        scratch_shapes=scratch,
        compiler_params=pltpu.CompilerParams(collective_id=1, has_side_effects=True, vmem_limit_bytes=63 * 1024 * 1024),
        cost_estimate=pl.CostEstimate(flops=18_000_000_000, bytes_accessed=400_000_000, transcendentals=3_000_000),
        name="backward_reduce",
    )(a_all, b_all, c_all, mod, bias_rows, down_sums, key_mask, row_mask, lift, mod_low, frames, cot, *saved)


def update_kernel(count, a_in, b_in, c_in, spread_in, lift, norm, bias, bias_state, *rest):
    masters, states, rest = rest[:5], rest[5:10], rest[10:]
    grads, news, news_state, rest = rest[:5], rest[5:10], rest[10:15], rest[15:]
    (bias_grad, bias_new, bias_state_new), rest = rest[:3], rest[3:]
    w, st, g, rest = rest[:5], rest[5:10], rest[10:15], rest[15:]
    a_sum, b_sum, spread, sums, in_sem, load_sem, out_sem = rest
    wide = jnp.float32
    width = a_sum.shape[2]
    half = ROUND * count // 2
    inputs = [
        local(source, target, in_sem.at[index])
        for index, (source, target) in enumerate(
            (
                (spread_in.at[pl.ds(0, half)], spread.at[0]), (spread_in.at[pl.ds(half, half)], spread.at[1]),
                (a_in, a_sum), (b_in, b_sum), (c_in, g[4]),
            )
        )
    ]
    sequence = (0, 3, 4, 1, 2)
    loads = {
        k: (local(masters[k], w[k], load_sem.at[0, k]), local(states[k], st[k], load_sem.at[1, k])) for k in sequence
    }
    factor = jnp.minimum(1.0, CLIP / (norm[0:1, 0:1] + 1e-06))
    for copy in inputs:
        copy.wait()
    both = bias_sums(spread, count)
    sums[...] = jnp.zeros_like(sums)
    sums[0:6, :] = both[0:6, :]
    sums[6:14, :] = both[8:16, :]

    def adam(weight, first_moment, second_moment, average, raw):
        grad = raw * factor
        moved = FIRST_DECAY * first_moment + (1.0 - FIRST_DECAY) * grad
        around = SECOND_DECAY * second_moment + (1.0 - SECOND_DECAY) * grad * grad
        step = (moved / (1.0 - FIRST_DECAY**STEPS)) / (jnp.sqrt(around / (1.0 - SECOND_DECAY**STEPS)) + ADAM_EPS)
        fresh = weight - RATE * (step + WEIGHT_DECAY * weight)
        return grad, fresh, moved, around, AVERAGE_DECAY * average + (1.0 - AVERAGE_DECAY) * fresh

    share = bias.shape[1]
    first = (lax.axis_index("wide") * 2 + lax.axis_index("narrow")) * share
    top = quotient(first, width)
    pair = jnp.concatenate([sums[pl.ds(top, 1), :], sums[pl.ds(top + 1, 1), :]], axis=1)
    pair = jnp.broadcast_to(pair, (8, 2 * width))
    bias_raw = pltpu.roll(pair, 2 * width - (first - top * width), 1)[0:1, :share]
    results = adam(bias[...], bias_state[0:1, :], bias_state[1:2, :], bias_state[2:3, :], bias_raw)
    bias_grad[...], bias_new[...] = results[:2]
    for part in range(3):
        bias_state_new[part : part + 1, :] = results[2 + part]
    stores = []
    for k in sequence:
        for copy in loads[k]:
            copy.wait()
        tile = 128 if k == 4 else TILE
        for part in range(w[k].shape[1] // width):

            def body(t, k=k, tile=tile, part=part):
                inner = aligned(t * tile, tile, 128)
                where = aligned(part * width + t * tile, tile, 128)
                if k == 0:
                    raw = nn(lift[part, :, :half], spread[0, :, inner]) + nn(lift[part, :, half:], spread[1, :, inner])
                elif k == 4:
                    raw = g[4][:, where]
                else:
                    raw = (b_sum if k == 3 else a_sum)[3 if k == 2 else part, :, inner].astype(wide)
                results = adam(w[k][:, where], st[k][0, :, where], st[k][1, :, where], st[k][2, :, where], raw)
                g[k][:, where], w[k][:, where] = results[:2]
                for slot in range(3):
                    st[k][slot, :, where] = results[2 + slot]

            repeat(width // tile, body)
        for at, (source, target) in enumerate(((g[k], grads[k]), (w[k], news[k]), (st[k], news_state[k]))):
            stores.append(local(source, target, out_sem.at[at, k]))
    for copy in stores:
        copy.wait()


def update(sums, spread, lift, norm, masters, states):
    a_sum, b_sum, c_sum = sums
    count = spread.shape[0] // ROUND
    wide = jnp.float32
    anywhere = pl.BlockSpec(memory_space=pl.ANY)
    near = pl.BlockSpec(memory_space=pltpu.VMEM)
    dma = pltpu.SemaphoreType.DMA

    def like(member):
        return jax.ShapeDtypeStruct(member.shape, member.dtype)

    width = a_sum.shape[2]
    bias, bias_state = masters[5].reshape(1, -1), states[5]
    outs = [like(member) for member in masters[:5]] * 2 + [like(member) for member in states[:5]]
    outs += [like(bias), like(bias), like(bias_state)]
    buffers = [pltpu.VMEM(member.shape, wide) for member in tuple(masters[:5]) + tuple(states[:5]) + tuple(masters[:5])]
    results = pl.pallas_call(
        functools.partial(update_kernel, count),
        out_shape=tuple(outs),
        in_specs=[anywhere] * 4 + [near] * 4 + [anywhere] * 10,
        out_specs=tuple([anywhere] * 15 + [near] * 3),
        scratch_shapes=buffers + [
            pltpu.VMEM(a_sum.shape, a_sum.dtype), pltpu.VMEM(b_sum.shape, b_sum.dtype),
            pltpu.VMEM((2, spread.shape[0] // 2, width), spread.dtype), pltpu.VMEM((ROUND, width), wide),
            dma((5,)), dma((2, 5)), dma((3, 5)),
        ],
        compiler_params=pltpu.CompilerParams(vmem_limit_bytes=56 * 1024 * 1024),
        cost_estimate=pl.CostEstimate(flops=100_000_000, bytes_accessed=40_000_000, transcendentals=1_000_000),
        name="update",
    )(a_sum, b_sum, c_sum, spread, lift, norm, bias, bias_state, *masters[:5], *states[:5])
    grads, news, news_state = results[:5], results[5:10], results[10:15]
    bias_grad, bias_new, bias_state_new = results[15:]
    grads = tuple(grads) + (bias_grad.reshape(-1),)
    news = tuple(news) + (bias_new.reshape(-1),)
    return grads, news, tuple(news_state) + (bias_state_new,)


def masks(order, member):
    return sum(1 << bit for place, bit in enumerate(order) if member >> place & 1)


def me_index():
    return lax.axis_index("wide") * 2 + lax.axis_index("narrow")


def device(index):
    return (index // 2, lax.rem(index, 2))


def own_plane(me):
    return lax.rem(me // 2, 2)


def flip(index, mask):
    out = index
    bit = 0
    while mask >> bit:
        if mask >> bit & 1:
            value = lax.rem(out // (1 << bit), 2)
            out = out + (1 << bit) * (1 - 2 * value)
        bit += 1
    return out


def block_of(me, pair, member, bits):
    plane = own_plane(me)
    last = 1 << (bits - 1)
    if member & last:
        rest = member - last
        zero = flip(flip(me, 1 << CORE), masks(pair[1], rest))
        one = flip(flip(me, 1 << CORE), masks(pair[0], rest))
    else:
        zero = flip(me, masks(pair[0], member))
        one = flip(me, masks(pair[1], member))
    return jnp.where(plane == 0, zero, one)


def partner_of(me, pair, place):
    zero = flip(me, 1 << pair[0][place])
    if pair[0][place] == pair[1][place]:
        return zero
    return jnp.where(own_plane(me) == 0, zero, flip(me, 1 << pair[1][place]))


def greet(me, bits):
    barrier = pltpu.get_barrier_semaphore()
    partners = [flip(me, 1 << bit) for bit in range(bits)] + [flip(me, 3)]
    for partner in partners:
        pl.semaphore_signal(barrier, inc=1, device_id=device(partner), device_id_type=MESH)
    pl.semaphore_wait(barrier, len(partners))


def gather_kernel(bits, rows, lates, a_src, b_src, c_src, a_out, b_out, c_out,
                  stage, block, c_block, quad_send, quad_recv, own_sem, keep_sem, send_sem, recv_sem):
    count = 1 << bits
    me = me_index()
    quad, spot = lax.rem(me, 4), me // 4
    pairs = [orders(bits, late) for late in lates]
    outs = (a_out, b_out, c_out)

    def place(kind, index):
        q, j = lax.rem(index, 4), index // 4
        return outs[kind].at[q, j] if kind < 2 else outs[kind].at[j, q]

    def send(kind, member, step, source):
        target = member | 1 << step
        return pltpu.make_async_remote_copy(
            src_ref=source,
            dst_ref=place(kind, block_of(me, pairs[kind], member, bits)),
            send_sem=send_sem.at[kind, target],
            recv_sem=recv_sem.at[kind, target],
            device_id=device(partner_of(me, pairs[kind], step)),
            device_id_type=MESH,
        )

    own = []
    for kind, source in enumerate((a_src, b_src)):
        own.append(pltpu.make_async_copy(source.at[quad], stage.at[kind, quad], own_sem.at[kind]))
    own.append(pltpu.make_async_copy(c_src, c_block, own_sem.at[2]))
    for copy in own:
        copy.start()
    greet(me, bits)
    quads = []
    for kind, source in enumerate((a_src, b_src)):
        for other in (1, 2, 3):
            copy = pltpu.make_async_remote_copy(
                src_ref=source.at[flip(quad, other)],
                dst_ref=stage.at[kind, quad],
                send_sem=quad_send.at[kind, other],
                recv_sem=quad_recv.at[kind, other],
                device_id=device(flip(me, other)),
                device_id_type=MESH,
            )
            copy.start()
            quads.append(copy)
    sends = []
    keeps = []

    def launch(kind, member, source):
        for step in range(top_place(member) + 1, bits):
            copy = send(kind, member, step, source)
            copy.start()
            sends.append(copy)

    def keep(kind, source):
        copy = pltpu.make_async_copy(source, place(kind, me), keep_sem.at[kind])
        copy.start()
        keeps.append(copy)

    own[2].wait()
    launch(2, 0, c_block)
    keep(2, c_block)
    padded = block.shape[1]
    for kind in (0, 1):
        own[kind].wait()
        for copy in quads[3 * kind:3 * kind + 3]:
            copy.wait_recv()
        for lane in range(0, stage.shape[3], 128):
            parts = [stage[kind, q, :, lane:lane + 128].astype(jnp.float32) for q in range(4)]
            if padded > 4 * rows:
                parts.append(jnp.zeros((padded - 4 * rows, 128), jnp.float32))
            block[kind, :, lane:lane + 128] = jnp.concatenate(parts, axis=0).astype(jnp.bfloat16)
        launch(kind, 0, block.at[kind])
        keep(kind, block.at[kind])

    def arrived(kind, member):
        spot_ref = place(kind, block_of(me, pairs[kind], member, bits))
        pltpu.make_async_copy(spot_ref, spot_ref, recv_sem.at[kind, member]).wait()
        return spot_ref

    for member in range(1, count):
        for kind in (2, 0, 1):
            launch(kind, member, arrived(kind, member))
    for copy in sends + quads:
        copy.wait_send()
    for copy in keeps:
        copy.wait()


def gather(a_src, b_src, c_src, count, lates=(False, False, False)):
    bits = count.bit_length() - 1
    rows, columns = a_src.shape[1:]
    padded = -(-4 * rows // 16) * 16
    c_padded = -(-c_src.shape[0] // 16) * 16
    if c_padded != c_src.shape[0]:
        c_src = jnp.pad(c_src, ((0, c_padded - c_src.shape[0]), (0, 0)))
    kinds = 3
    anywhere = pl.BlockSpec(memory_space=pl.ANY)
    big = jax.ShapeDtypeStruct((4, count // 4, padded, columns), jnp.bfloat16)
    tall = jax.ShapeDtypeStruct((count // 4, 4, c_padded, columns), jnp.bfloat16)
    a_all, b_all, c_all = pl.pallas_call(
        functools.partial(gather_kernel, bits, rows, lates),
        out_shape=(big, big, tall),
        in_specs=[anywhere] * 3,
        out_specs=(anywhere,) * 3,
        scratch_shapes=[
            pltpu.VMEM((2, 4, rows, columns), jnp.bfloat16),
            pltpu.VMEM((2, padded, columns), jnp.bfloat16),
            pltpu.VMEM((c_padded, columns), jnp.bfloat16),
            pltpu.SemaphoreType.DMA((2, 4)),
            pltpu.SemaphoreType.DMA((2, 4)),
            pltpu.SemaphoreType.DMA((3,)),
            pltpu.SemaphoreType.DMA((3,)),
            pltpu.SemaphoreType.DMA((kinds, count)),
            pltpu.SemaphoreType.DMA((kinds, count)),
        ],
        compiler_params=pltpu.CompilerParams(collective_id=2, has_side_effects=True),
        cost_estimate=pl.CostEstimate(flops=0, bytes_accessed=400_000_000, transcendentals=0),
        name="gather_weights",
    )(a_src, b_src, c_src)
    return a_all, b_all, c_all


def reduce_kernel(bits, rows, lates, a_in, b_in, c_in, a_out, b_out, c_out,
                  own, recv, quad_block, total, own_sem, send_sem, recv_sem, quad_send, quad_recv, quad_own, total_sem):
    count = 1 << bits
    half = count // 2
    me = me_index()
    quad = lax.rem(me, 4)
    pairs = [orders(bits, late) for late in lates]
    ins = (a_in, b_in, c_in)
    kinds = (2, 1, 0)

    def place(kind, index):
        q, j = lax.rem(index, 4), index // 4
        return ins[kind].at[q, j] if kind < 2 else ins[kind].at[j, q]

    loads = {}
    for member in range(half - 1, -1, -1):
        for kind in kinds:
            loads[kind, member] = pltpu.make_async_copy(
                place(kind, block_of(me, pairs[kind], member, bits)), own.at[kind, member], own_sem.at[kind, member]
            )
    sends = []

    def send(kind, member, source):
        step = top_place(member)
        copy = pltpu.make_async_remote_copy(
            src_ref=source,
            dst_ref=recv.at[kind, member],
            send_sem=send_sem.at[kind, member],
            recv_sem=recv_sem.at[kind, member],
            device_id=device(partner_of(me, pairs[kind], step)),
            device_id_type=MESH,
        )
        copy.start()
        sends.append(copy)

    for kind in kinds:
        loads[kind, half - 1].start()
    greet(me, bits)
    for member in range(half - 1, -1, -1):
        for kind in kinds:
            send(kind, member + half, place(kind, block_of(me, pairs[kind], member + half, bits)))
            if member < half - 1:
                loads[kind, member].start()

    padded, columns = own.shape[2:]

    def ready(kind, member):
        loads[kind, member].wait()
        parts = [member | 1 << step for step in range(top_place(member) + 1, bits)]
        for part in parts:
            pltpu.make_async_copy(recv.at[kind, part], recv.at[kind, part], recv_sem.at[kind, part]).wait()
        return parts

    def summed(kind, member, parts, where):
        value = own[kind, member, where, :].astype(jnp.float32)
        for part in parts:
            value = value + recv[kind, part, where, :].astype(jnp.float32)
        return value

    for member in range(half - 1, 0, -1):
        for kind in kinds:
            parts = ready(kind, member)

            def strip(s, carry, kind=kind, member=member, parts=parts):
                where = pl.ds(pl.multiple_of(s * 16, 16), 16)
                own[kind, member, where, :] = summed(kind, member, parts, where).astype(jnp.bfloat16)
                return carry

            lax.fori_loop(0, padded // 16, strip, 0)
            send(kind, member, own.at[kind, member])

    copies = []
    for kind in kinds:
        parts = ready(kind, 0)

        def strip(s, carry, kind=kind, parts=parts):
            where = pl.ds(pl.multiple_of(s * 16, 16), 16)
            total[kind, where, :] = summed(kind, 0, parts, where)
            return carry

        lax.fori_loop(0, padded // 16, strip, 0)
        if kind == 2:
            copy = pltpu.make_async_copy(total.at[2], c_out, total_sem)
            copy.start()
            copies.append(copy)
            continue
        out = (a_out, b_out)[kind]
        for lane in range(0, columns, 128):
            for q in range(4):
                quad_block[kind, q, :, lane:lane + 128] = total[kind, q * rows:(q + 1) * rows, lane:lane + 128].astype(jnp.bfloat16)
        copy = pltpu.make_async_copy(quad_block.at[kind, quad], out.at[quad], quad_own.at[kind])
        copy.start()
        copies.append(copy)
        for other in (1, 2, 3):
            copy = pltpu.make_async_remote_copy(
                src_ref=quad_block.at[kind, flip(quad, other)],
                dst_ref=out.at[quad],
                send_sem=quad_send.at[kind, other],
                recv_sem=quad_recv.at[kind, other],
                device_id=device(flip(me, other)),
                device_id_type=MESH,
            )
            copy.start()
            copies.append(copy)
    for copy in copies:
        copy.wait()
    for copy in sends:
        copy.wait_send()


def reduce(a_in, b_in, c_in, rows, lates=(False, False, False)):
    count = a_in.shape[1] * 4
    bits = count.bit_length() - 1
    padded, columns = a_in.shape[2:]
    anywhere = pl.BlockSpec(memory_space=pl.ANY)
    share = jax.ShapeDtypeStruct((4, rows, columns), jnp.bfloat16)
    return pl.pallas_call(
        functools.partial(reduce_kernel, bits, rows, lates),
        out_shape=(share, share, jax.ShapeDtypeStruct((padded, columns), jnp.float32)),
        in_specs=[anywhere] * 3,
        out_specs=(anywhere,) * 3,
        scratch_shapes=[
            pltpu.VMEM((3, count // 2, padded, columns), jnp.bfloat16),
            pltpu.VMEM((3, count, padded, columns), jnp.bfloat16),
            pltpu.VMEM((2, 4, rows, columns), jnp.bfloat16),
            pltpu.VMEM((3, padded, columns), jnp.float32),
            pltpu.SemaphoreType.DMA((3, count // 2)),
            pltpu.SemaphoreType.DMA((3, count)),
            pltpu.SemaphoreType.DMA((3, count)),
            pltpu.SemaphoreType.DMA((2, 4)),
            pltpu.SemaphoreType.DMA((2, 4)),
            pltpu.SemaphoreType.DMA((2,)),
            pltpu.SemaphoreType.DMA,
        ],
        compiler_params=pltpu.CompilerParams(collective_id=3, has_side_effects=True, vmem_limit_bytes=62 * 1024 * 1024),
        cost_estimate=pl.CostEstimate(flops=0, bytes_accessed=400_000_000, transcendentals=0),
        name="reduce_gradients",
    )(a_in, b_in, c_in)


def layer_norm(values):
    centre = jnp.mean(values, axis=-1, keepdims=True)
    centred = values - centre
    spread = jnp.mean(centred * centred, axis=-1, keepdims=True)
    return centred * lax.rsqrt(spread + NORM_EPS)


def modulate(values, shift_part, scale_part):
    return layer_norm(values) * (1.0 + scale_part) + shift_part


def silu_act(values):
    return values * jax.nn.sigmoid(values)


def gelu_tanh(values):
    inner = 0.7978845608028654 * (values + 0.044715 * values * values * values)
    return 0.5 * values * (1.0 + jnp.tanh(inner))


def slot_mask(grid, frame_len):
    area = grid[:, 0] * grid[:, 1]
    return lax.broadcasted_iota(jnp.int32, (grid.shape[0], frame_len), 1) < area[:, None]


def split_biases(biases, model_width, hidden_width):
    edges = [
        6 * model_width,
        7 * model_width,
        8 * model_width,
        9 * model_width,
        9 * model_width + hidden_width,
    ]
    return jnp.split(biases, edges)


def adam_update(weight, state, grad):
    first = FIRST_DECAY * state[0] + (1.0 - FIRST_DECAY) * grad
    second = SECOND_DECAY * state[1] + (1.0 - SECOND_DECAY) * grad * grad
    first_hat = first / (1.0 - FIRST_DECAY**STEPS)
    second_hat = second / (1.0 - SECOND_DECAY**STEPS)
    new_weight = weight - RATE * (
        first_hat / (jnp.sqrt(second_hat) + ADAM_EPS) + WEIGHT_DECAY * weight
    )
    average = AVERAGE_DECAY * state[2] + (1.0 - AVERAGE_DECAY) * new_weight
    return (new_weight, jnp.stack([first, second, average]))


def attention_scores(query_heads, key_heads, valid_slots, score_scale):
    scores = (
        jnp.einsum("fqhs,fkhs->fhqk", query_heads, key_heads, preferred_element_type=jnp.float32)
        * score_scale
    )
    return jnp.where(valid_slots[:, None, None, :], scores, MASK_VALUE)


def token_sum(values):
    return jnp.sum(values, axis=(0, 1), dtype=jnp.float32)


def exchange(packets):
    return lax.all_to_all(packets, AXES, split_axis=0, concat_axis=0, tiled=True)


def plain_shards(
    frames_in,
    conditioning,
    grid,
    cotangent,
    mod_weight,
    qkv_weight,
    out_weight,
    up_weight,
    down_weight,
    biases,
    mod_state,
    qkv_state,
    out_state,
    up_state,
    down_state,
    bias_state,
):
    frame_count, frame_len, model_width = frames_in.shape
    hidden_width = up_weight.shape[1]
    head_size = model_width // HEADS
    score_scale = head_size ** (-0.5)
    head_shape = (frame_count, frame_len, HEADS, head_size)
    count = lax.axis_size("wide") * lax.axis_size("narrow")
    rows = mod_weight.shape[0]
    tall_rows = down_weight.shape[0]
    low = jnp.bfloat16

    def slices(member):
        return member.reshape(rows, 4, model_width).transpose(1, 0, 2)

    a_src = slices(jnp.concatenate([qkv_weight.astype(low), out_weight.astype(low)], axis=1))
    b_src = slices(up_weight.astype(low))
    a_all, b_all, c_all = gather(a_src, b_src, down_weight.astype(low), count, (False, False, True))
    a_all = a_all[:, :, : 4 * rows].reshape(4, model_width, model_width)
    up_low = b_all[:, :, : 4 * rows].reshape(4, model_width, model_width)
    down_low = c_all[:, :, :tall_rows].reshape(hidden_width, model_width)
    query_low, key_low, value_low, out_low = (a_all[index] for index in range(4))

    cond_f = conditioning.astype(jnp.float32)
    silu_low = silu_act(cond_f).astype(low)
    mod_low = mod_weight.astype(low)
    first = exchange(
        jnp.concatenate(
            [
                silu_low.reshape(count, rows),
                jnp.broadcast_to(biases.astype(low)[None], (count, biases.shape[0])),
            ],
            axis=1,
        )
    )
    silu_rows = first[:, :rows]
    bias_low = first[:, rows:].reshape(-1)
    mod_terms = exchange(jnp.dot(silu_rows, mod_low, preferred_element_type=jnp.float32))
    mod_bias, query_bias, value_bias, out_bias, up_bias, down_bias = split_biases(
        bias_low.astype(jnp.float32), model_width, hidden_width
    )
    modulation = jnp.sum(mod_terms, axis=0, keepdims=True) + mod_bias
    valid_slots = slot_mask(grid, frame_len)
    row_mask = valid_slots[:, :, None].astype(jnp.float32)
    frames_f = frames_in.astype(jnp.float32)
    shift_attn, scale_attn, gate_attn, shift_mlp, scale_mlp, gate_mlp = jnp.split(
        modulation[:, None, :], 6, axis=-1
    )
    norm_one = modulate(frames_f, shift_attn, scale_attn).astype(low)

    def project(values, weight):
        return jnp.einsum("fbd,de->fbe", values, weight, preferred_element_type=jnp.float32)

    query_heads = (project(norm_one, query_low) + query_bias).astype(low).reshape(head_shape)
    key_heads = project(norm_one, key_low).astype(low).reshape(head_shape)
    value_heads = (project(norm_one, value_low) + value_bias).astype(low).reshape(head_shape)
    scores = attention_scores(query_heads, key_heads, valid_slots, score_scale)
    row_max = jnp.max(scores, axis=-1, keepdims=True)
    exponent = jnp.exp(scores - row_max)
    row_total = jnp.sum(exponent, axis=-1, keepdims=True)
    log_total = row_max + jnp.log(row_total)
    attention = (exponent / row_total).astype(low)
    attended = jnp.einsum(
        "fhqk,fkhs->fqhs", attention, value_heads, preferred_element_type=jnp.float32
    )
    attended = attended.reshape(frame_count, frame_len, model_width).astype(low)
    branch = project(attended, out_low) + out_bias
    midway = frames_f + gate_attn * branch
    norm_two = modulate(midway, shift_mlp, scale_mlp).astype(low)
    up_values = (
        jnp.einsum("fbd,sde->fbse", norm_two, up_low, preferred_element_type=jnp.float32).reshape(
            frame_count, frame_len, hidden_width
        )
        + up_bias
    )
    activated = gelu_tanh(up_values).astype(low)
    down_values = project(activated, down_low) + down_bias
    block_out = ((midway + gate_mlp * down_values) * row_mask).astype(low)
    upstream = cotangent.astype(jnp.float32) * row_mask
    d_gate_mlp = jnp.sum(upstream * down_values, axis=1, keepdims=True)
    d_down = (upstream * gate_mlp).astype(low)
    grad_down = jnp.einsum("fbe,fbd->ed", activated, d_down, preferred_element_type=jnp.float32)
    grad_down_bias = token_sum(d_down)
    d_activated = jnp.einsum("fbd,ed->fbe", d_down, down_low, preferred_element_type=jnp.float32)
    gelu_pull = jax.vjp(gelu_tanh, up_values)[1]
    d_up = gelu_pull(d_activated)[0].astype(low)
    d_up_parts = d_up.reshape(frame_count, frame_len, 4, model_width)
    grad_up = jnp.einsum("fbd,fbse->sde", norm_two, d_up_parts, preferred_element_type=jnp.float32)
    grad_up_bias = token_sum(d_up)
    d_norm_two = jnp.einsum("fbse,sde->fbd", d_up_parts, up_low, preferred_element_type=jnp.float32)
    second_pull = jax.vjp(modulate, midway, shift_mlp, scale_mlp)[1]
    d_midway, d_shift_mlp, d_scale_mlp = second_pull(d_norm_two)
    d_midway = d_midway + upstream
    d_gate_attn = jnp.sum(d_midway * branch, axis=1, keepdims=True)
    d_branch = (d_midway * gate_attn).astype(low)
    grad_out = jnp.einsum("fbd,fbe->de", attended, d_branch, preferred_element_type=jnp.float32)
    grad_out_bias = token_sum(d_branch)
    d_attended = jnp.einsum("fbe,de->fbd", d_branch, out_low, preferred_element_type=jnp.float32)
    d_attended = d_attended.astype(low).reshape(head_shape)
    scores = attention_scores(query_heads, key_heads, valid_slots, score_scale)
    soft = jnp.exp(scores - log_total)
    d_soft = jnp.einsum(
        "fqhs,fkhs->fhqk", d_attended, value_heads, preferred_element_type=jnp.float32
    )
    d_value_heads = jnp.einsum(
        "fhqk,fqhs->fkhs", attention, d_attended, preferred_element_type=jnp.float32
    )
    d_scores = (soft * (d_soft - jnp.sum(soft * d_soft, axis=-1, keepdims=True))).astype(low)
    d_query_heads = (
        jnp.einsum("fhqk,fkhs->fqhs", d_scores, key_heads, preferred_element_type=jnp.float32)
        * score_scale
    )
    d_key_heads = (
        jnp.einsum("fhqk,fqhs->fkhs", d_scores, query_heads, preferred_element_type=jnp.float32)
        * score_scale
    )
    flat_shape = (frame_count, frame_len, model_width)
    d_query = d_query_heads.reshape(flat_shape).astype(low)
    d_key = d_key_heads.reshape(flat_shape).astype(low)
    d_value = d_value_heads.reshape(flat_shape).astype(low)
    grad_query, grad_key, grad_value = (
        jnp.einsum("fbd,fbe->de", norm_one, member, preferred_element_type=jnp.float32)
        for member in (d_query, d_key, d_value)
    )
    grad_query_bias = token_sum(d_query)
    grad_value_bias = token_sum(d_value)
    d_norm_one = sum(
        jnp.einsum("fbe,de->fbd", member, weight, preferred_element_type=jnp.float32)
        for member, weight in ((d_query, query_low), (d_key, key_low), (d_value, value_low))
    )
    first_pull = jax.vjp(modulate, frames_f, shift_attn, scale_attn)[1]
    d_frames, d_shift_attn, d_scale_attn = first_pull(d_norm_one)
    frames_grad = (d_frames + d_midway).astype(low)
    d_modulation = jnp.concatenate(
        [d_shift_attn, d_scale_attn, d_gate_attn, d_shift_mlp, d_scale_mlp, d_gate_mlp], axis=-1
    )[:, 0, :].astype(low)
    grad_mod_bias = d_modulation[0].astype(jnp.float32)
    grad_bias = jnp.concatenate(
        [
            grad_mod_bias,
            grad_query_bias,
            grad_value_bias,
            grad_out_bias,
            grad_up_bias,
            grad_down_bias,
        ]
    )
    terms = exchange(
        jnp.concatenate(
            [
                jnp.broadcast_to(d_modulation, (count, d_modulation.shape[1])),
                grad_bias.reshape(count, -1).astype(low),
            ],
            axis=1,
        )
    )
    d_mod_all, bias_terms = terms[:, : d_modulation.shape[1]], terms[:, d_modulation.shape[1] :]

    def grouped(member, group_rows):
        member = member.astype(low).reshape(4, count // 4, 4 * rows, model_width)
        return jnp.pad(member, ((0, 0), (0, 0), (0, group_rows - 4 * rows), (0, 0)))

    group_rows = -(-4 * rows // 16) * 16
    tall_group = -(-tall_rows // 16) * 16
    a_sum, b_sum, c_sum = reduce(
        grouped(jnp.stack([grad_query, grad_key, grad_value, grad_out]), group_rows),
        grouped(grad_up, group_rows),
        jnp.pad(
            grad_down.astype(low).reshape(count // 4, 4, tall_rows, model_width),
            ((0, 0), (0, 0), (0, tall_group - tall_rows), (0, 0)),
        ),
        rows,
        (True, False, False),
    )
    red_mod = lax.dot_general(
        silu_rows, d_mod_all, (((0,), (0,)), ((), ())), preferred_element_type=jnp.float32
    )
    a_sum = a_sum.astype(jnp.float32)
    red_qkv = a_sum[:3].transpose(1, 0, 2).reshape(rows, 3 * model_width)
    red_out = a_sum[3]
    red_up = b_sum.astype(jnp.float32).transpose(1, 0, 2).reshape(rows, hidden_width)
    red_down = c_sum[:tall_rows]
    red_bias = jnp.sum(bias_terms.astype(jnp.float32), axis=0)
    d_silu = lax.dot_general(
        d_mod_all, mod_low, (((1,), (1,)), ((), ())), preferred_element_type=jnp.float32
    )
    reduced = (red_mod, red_qkv, red_out, red_up, red_down, red_bias)
    partial_sq = sum((jnp.sum(member * member) for member in reduced))
    last = exchange(
        jnp.concatenate([d_silu, jnp.broadcast_to(partial_sq, (count, 1))], axis=1)
    )
    total_sq = jnp.sum(last[:, rows])
    silu_pull = jax.vjp(silu_act, cond_f)[1]
    cond_grad = silu_pull(last[:, :rows].reshape(1, model_width))[0]
    grad_norm = jnp.sqrt(total_sq)
    factor = jnp.minimum(1.0, CLIP / (grad_norm + 1e-06))
    clipped = tuple((member * factor for member in reduced))
    masters = (mod_weight, qkv_weight, out_weight, up_weight, down_weight, biases)
    states = (mod_state, qkv_state, out_state, up_state, down_state, bias_state)
    updated = [adam_update(masters[index], states[index], clipped[index]) for index in range(6)]
    return (
        (block_out, frames_grad, cond_grad, grad_norm)
        + clipped
        + tuple(pair[0] for pair in updated)
        + tuple(pair[1] for pair in updated)
    )


def fused_shards(
    frames_in,
    conditioning,
    grid,
    cotangent,
    mod_weight,
    qkv_weight,
    out_weight,
    up_weight,
    down_weight,
    biases,
    mod_state,
    qkv_state,
    out_state,
    up_state,
    down_state,
    bias_state,
):
    frame_count, frame_len, model_width = frames_in.shape
    hidden_width = up_weight.shape[1]
    count = lax.axis_size("wide") * lax.axis_size("narrow")
    rows = mod_weight.shape[0]
    tall_rows = down_weight.shape[0]
    low = jnp.bfloat16

    def slices(member):
        return member.reshape(rows, 4, model_width).transpose(1, 0, 2)

    a_src = slices(jnp.concatenate([qkv_weight.astype(low), out_weight.astype(low)], axis=1))
    b_src = slices(up_weight.astype(low))
    cond_f = conditioning.astype(jnp.float32)
    silu_low = silu_act(cond_f).astype(low)
    mod_low = mod_weight.astype(low)
    first = exchange(
        jnp.concatenate(
            [
                silu_low.reshape(count, rows),
                jnp.broadcast_to(biases.astype(low)[None], (count, biases.shape[0])),
            ],
            axis=1,
        )
    )
    silu_rows = first[:, :rows]
    bias_f = first[:, rows:].reshape(-1).astype(jnp.float32)
    bits = count.bit_length() - 1
    crossed = [CORE, 0] + list(range(2, bits))
    sorted_rows = silu_rows.reshape((2,) * bits + (rows,)).transpose(
        [bits - 1 - bit for bit in crossed] + [bits]
    )
    terms = jnp.dot(
        sorted_rows.reshape(count, rows), mod_low, preferred_element_type=jnp.float32
    ).reshape((2,) * bits + (6 * model_width // 128, 128))
    mod_bias = bias_f[: 6 * model_width].reshape(-1, 128)
    bias_rows = bias_f[6 * model_width :].reshape(-1, model_width)
    valid_slots = slot_mask(grid, frame_len)
    row_mask = valid_slots[:, :, None].astype(jnp.float32)
    key_mask = jnp.broadcast_to(valid_slots.astype(jnp.float32), (8, frame_len))
    forward_out = forward(
        a_src, b_src, down_weight.astype(low), terms, mod_bias, bias_rows, frames_in[0], cotangent[0], key_mask, row_mask[0],
    )
    weights, mod_parts, kept, down_sums = forward_out[:3], forward_out[3], forward_out[4:-1], forward_out[-1]
    me = lax.axis_index("wide") * 2 + lax.axis_index("narrow")
    near_rows = silu_rows.reshape((2,) * bits + (rows,))
    for bit in range(bits):
        axis = bits - 1 - bit
        near_rows = jnp.where(me // (1 << bit) % 2 == 1, jnp.flip(near_rows, axis), near_rows)
    near_rows = near_rows.transpose([bits - 1 - bit for bit in reversed(SPREAD(bits))] + [bits])
    near_rows = near_rows.reshape(count, rows).T
    lift = near_rows[None, :, :, None] * jnp.eye(6, 16, dtype=low)[:, None, None, :]
    lift = lift.reshape(6, rows, 16 * count)
    block_out, frames_grad, spread, *sums, ordered, norm = backward(
        weights, mod_parts, bias_rows, down_sums, key_mask, row_mask[0], lift, mod_low, frames_in[0], cotangent[0], kept,
        rows, bits,
    )
    grads, news, news_state = update(
        sums, spread, lift, norm,
        (mod_weight, qkv_weight, out_weight, up_weight, down_weight, biases),
        (mod_state, qkv_state, out_state, up_state, down_state, bias_state),
    )
    silu_pull = jax.vjp(silu_act, cond_f)[1]
    cond_grad = silu_pull(ordered[:, :rows].reshape(1, model_width))[0]
    return (block_out[None], frames_grad[None], cond_grad, norm[0, 0]) + grads + news + news_state


def shards(*arrays):
    rows, tall_rows = arrays[4].shape[0], arrays[8].shape[0]
    fits = 4 * rows % ROUND == 0 and tall_rows % ROUND == 0
    return (fused_shards if fits else plain_shards)(*arrays)


def solution(mesh):
    tokens = P(AXES, None, None)
    matrix = P(AXES, None)
    vector = P(AXES)
    state = P(None, AXES, None)
    weights = (matrix,) * 5 + (vector,)
    states = (state,) * 5 + (P(None, AXES),)
    return jax.shard_map(
        shards,
        mesh=mesh,
        in_specs=(tokens, matrix, matrix, tokens) + weights + states,
        out_specs=(tokens, tokens, matrix, P()) + weights + weights + states,
        check_vma=False,
    )
```

```python
import functools
import jax
import jax.numpy as jnp
from jax import lax
from jax.experimental import pallas as pl
from jax.experimental.pallas import tpu as pltpu
from jax.sharding import PartitionSpec as P

HEADS = 16
STEPS = 4
CLIP = 576
NORM_EPS = 1e-06
RATE = 0.04
FIRST_DECAY = 0.5
SECOND_DECAY = 0.5
WEIGHT_DECAY = 0.1
ADAM_EPS = 1e-08
AVERAGE_DECAY = 0.9999
MASK_VALUE = -1e30
AXES = ("wide", "narrow")

MESH = pl.DeviceIdType.MESH
CORE = 1
ROUND = 16


def orders(bits, late):
    high = list(range(bits - 1, 2, -1))
    if late:
        pair = (high[:-1] + [0, 2] + high[-1:], high[:-1] + [2, 0] + high[-1:])
    else:
        pair = (high + [2, 0], high + [0, 2])
    return tuple(order + [CORE] for order in pair)


def top_place(member):
    return member.bit_length() - 1


def quotient(value, by):
    return lax.div(value, jnp.int32(by))


def remainder(value, by):
    return lax.rem(value, jnp.int32(by))


class Spots:
    def __init__(self, bits):
        wide, narrow = lax.axis_index("wide"), lax.axis_index("narrow")
        self.bits = bits
        self.me = wide * 2 + narrow
        self.quad = remainder(self.me, 4)
        self.group = quotient(self.me, 4)
        self.digit = [remainder(quotient(self.me, 1 << bit), 2) for bit in range(bits)]
        self.core = self.digit[CORE]
        self.delta = [(1 << bit) * (1 - 2 * self.digit[bit]) for bit in range(bits)]
        self.device = [
            (wide, 1 - narrow) if bit == 0 else (wide + (1 << bit - 1) * (1 - 2 * self.digit[bit]), narrow)
            for bit in range(bits)
        ]
        self.steps = {}
        first = self.core == 0
        for late in (False, True):
            pair = orders(bits, late)
            own, other, devices = [], [], []
            for place in range(bits):
                zero, one = pair[0][place], pair[1][place]
                if zero == one:
                    own.append(self.delta[zero])
                    other.append(self.delta[zero])
                    devices.append(self.device[zero])
                else:
                    own.append(jnp.where(first, self.delta[zero], self.delta[one]))
                    other.append(jnp.where(first, self.delta[one], self.delta[zero]))
                    devices.append(
                        tuple(jnp.where(first, a, b) for a, b in zip(self.device[zero], self.device[one]))
                    )
            self.steps[late] = (own, other, devices)
        self.opposite = (self.device[CORE][0], self.device[0][1])

    def block(self, late, member):
        own, other, _ = self.steps[late]
        last = self.bits - 1
        table = other if member >> last & 1 else own
        index = self.me
        for place in range(self.bits):
            if member >> place & 1:
                index = index + table[place]
        return index

    def partner(self, late, place):
        return self.steps[late][2][place]

    def near(self, other):
        if other == 3:
            return self.opposite, 3 - self.quad
        bit = other - 1
        return self.device[bit], self.quad + self.delta[bit]

    def across(self, mask):
        wide, narrow = self.device[0][0], 1 - self.device[0][1]
        for bit in range(self.bits):
            if mask >> bit & 1:
                if bit == 0:
                    narrow = 1 - narrow
                else:
                    wide = wide + (1 << bit - 1) * (1 - 2 * self.digit[bit])
        return wide, narrow

    def greet(self, masks):
        barrier = pltpu.get_barrier_semaphore()
        for mask in masks:
            pl.semaphore_signal(barrier, inc=1, device_id=self.across(mask), device_id_type=MESH)
        pl.semaphore_wait(barrier, len(masks))


def remote(source, target, send_sem, recv_sem, device):
    copy = pltpu.make_async_remote_copy(
        src_ref=source, dst_ref=target, send_sem=send_sem, recv_sem=recv_sem, device_id=device, device_id_type=MESH
    )
    copy.start()
    return copy


def local(source, target, sem):
    copy = pltpu.make_async_copy(source, target, sem)
    copy.start()
    return copy


def await_bytes(spot, sem):
    pltpu.make_async_copy(spot, spot, sem).wait()


def aligned(start, size, by=16):
    return pl.ds(pl.multiple_of(start, by), size)


def repeat(times, body):
    def run(index, carry):
        body(index)
        return carry

    lax.fori_loop(0, times, run, 0)


class Agenda:
    def __init__(self):
        self.services = []
        self.steps = []
        self.now = 0.0

    def service(self, when, action):
        self.services.append((when, len(self.services), action))

    def step(self, takes, action, after=0.0):
        self.steps.append((takes, action, after))

    def emit(self):
        while self.services or self.steps:
            self.services.sort(key=lambda item: item[:2])
            due = self.services[0][0] if self.services else None
            after = self.steps[0][2] if self.steps else None
            if self.services and (not self.steps or due <= self.now or (after > self.now and due <= after)):
                when, _, action = self.services.pop(0)
                self.now = max(self.now, when) + 0.1
            else:
                takes, action, after = self.steps.pop(0)
                self.now = max(self.now, after) + takes
            action()


def nn(left, right):
    return jnp.dot(left, right, preferred_element_type=jnp.float32)


def nt(left, right):
    return lax.dot_general(left, right, (((1,), (1,)), ((), ())), preferred_element_type=jnp.float32)


def tn(left, right):
    return lax.dot_general(left, right, (((0,), (0,)), ((), ())), preferred_element_type=jnp.float32)


def gelu_parts(value):
    bend = jnp.tanh(0.7978845608028654 * (value + 0.044715 * value * value * value))
    slope = 0.7978845608028654 * (1.0 + 0.134145 * value * value)
    return 0.5 * value * (1.0 + bend), 0.5 * (1.0 + bend) + 0.5 * value * (1.0 - bend * bend) * slope


def normalized(value):
    centre = jnp.mean(value, axis=-1, keepdims=True)
    centred = value - centre
    spread = jnp.mean(centred * centred, axis=-1, keepdims=True)
    root = lax.rsqrt(spread + NORM_EPS)
    return centred * root, root


def head_window(head, size):
    first, last = head * size // 128, (head * size + size - 1) // 128
    return first * 128, (last + 1 - first) * 128, head * size - first * 128


def only_head(values, offset, size):
    lane = lax.broadcasted_iota(jnp.int32, values.shape, 1)
    return jnp.where(jnp.logical_and(lane >= offset, lane < offset + size), values, jnp.zeros((), values.dtype))


STRIP = 32
TILE = 384
WIDE_TILE = 1152


def forward_kernel(bits, rows, pieces, clock,
                   a_src, b_src, c_src, terms_in, mod_bias, bias_rows, frames, cot, key_mask, row_mask,
                   a_out, b_out, c_out, mod_out, query_out, key_out, value_out, total_out,
                   branch_out, midway_out, slope_out, active_out, change_out, turned_out, down_out, bias_out,
                   stage, block, c_block, terms, landed, x_ref, first, query, key, value, totals, joined, attended,
                   branch, midway, second, active, active_turned, other_turned, change, other_change, turned,
                   weight, slope_stage, down_stage,
                   quad_send, quad_recv, own_sem, keep_sem, send_sem, recv_sem, term_send, term_recv,
                   pair_send, pair_recv, load_sem, weight_sem, save_sem, slope_sem, down_sem):
    count = 1 << bits
    spots = Spots(bits)
    quad, core = spots.quad, spots.core
    sibling = spots.device[CORE]
    outs = (a_out, b_out, c_out)
    tall_rows = c_src.shape[0]
    tokens, width = first.shape
    size = width // HEADS
    scale = size ** (-0.5)
    low = jnp.bfloat16
    finals = []

    def save(source, target, index):
        finals.append(local(source, target, save_sem.at[index]).wait)

    def place(piece, index):
        kind, start, length, _ = pieces[piece]
        if kind == 2:
            return c_out.at[aligned(index * tall_rows + start, length)]
        return outs[kind].at[remainder(index, 4), aligned(quotient(index, 4) * (4 * rows) + start, length)]

    def of_kind(kind):
        return [piece for piece, entry in enumerate(pieces) if entry[0] == kind]

    own = [local(source.at[quad], stage.at[kind, quad], own_sem.at[kind]) for kind, source in enumerate((a_src, b_src))]
    own.append(local(c_src, c_block, own_sem.at[2]))
    loads = [local(terms_in, terms, load_sem.at[0]), local(frames, x_ref, load_sem.at[1])]
    spots.greet([1 << bit for bit in range(bits)] + [3])
    quads = []

    def start_quad(kind, source):
        for other in (1, 2, 3):
            device, spot = spots.near(other)
            copy = remote(source.at[spot], stage.at[kind, quad], quad_send.at[kind, other], quad_recv.at[kind, other], device)
            quads.append(copy)
            finals.append(copy.wait_send)

    keeps = {}

    def launch(piece, member, source):
        late = pieces[piece][3]
        spot = spots.block(late, member)
        for step in range(top_place(member) + 1, bits):
            target = member | 1 << step
            copy = remote(
                source, place(piece, spot), send_sem.at[piece, target], recv_sem.at[piece, target], spots.partner(late, step)
            )
            finals.append(copy.wait_send)

    def open_pieces(kind, source):
        for piece in of_kind(kind):
            _, start, length, _ = pieces[piece]
            part = source.at[pl.ds(start, length)]
            launch(piece, 0, part)
            keeps[piece] = local(part, place(piece, spots.me), keep_sem.at[piece])

    def arrived(piece, member):
        spot = place(piece, spots.block(pieces[piece][3], member))
        await_bytes(spot, recv_sem.at[piece, member])
        return spot

    def open_quad(kind):
        own[kind].wait()
        for copy in quads[3 * kind : 3 * kind + 3]:
            copy.wait_recv()
        for lane in range(0, width, 128):
            parts = [stage[kind, q, :, lane : lane + 128].astype(jnp.float32) for q in range(4)]
            block[kind, :, lane : lane + 128] = jnp.concatenate(parts, axis=0).astype(low)
        open_pieces(kind, block.at[kind])

    crossed = [CORE, 0] + list(range(2, bits))
    term_copies = []

    def start_term(step):
        given = tuple(spots.digit[bit] for bit in crossed[:step]) + (1 - spots.digit[crossed[step]],)
        copy = remote(terms.at[given], landed[step], term_send.at[step], term_recv.at[step], spots.device[crossed[step]])
        term_copies.append(copy)
        finals.append(copy.wait_send)

    def end_term(step):
        kept = tuple(spots.digit[bit] for bit in crossed[: step + 1])
        term_copies[step].wait_recv()
        terms[kept] = terms[kept] + landed[step][...]
        if step + 1 < bits:
            start_term(step + 1)
            return
        parts = terms[kept] + mod_bias[...]
        per = width // 128
        for at in range(6 * per):
            part, lane = at // per, at % per * 128
            mod_out[part : part + 1, lane : lane + 128] = parts[at : at + 1, :]

    start_quad(0, a_src)
    loads[0].wait()
    start_term(0)
    own[2].wait()
    open_pieces(2, c_block)
    open_quad(0)
    start_quad(1, b_src)
    open_quad(1)
    agenda = Agenda()
    for step in range(bits):
        agenda.service(clock["terms"][0] + clock["terms"][1] * step, functools.partial(end_term, step))
    full = [0.0] * 3
    for piece, (kind, _, _, _) in enumerate(pieces):
        begin, pace = clock["pieces"][piece]
        for member in range(1, count // 2):
            agenda.service(
                begin + pace * member,
                lambda piece=piece, member=member: launch(piece, member, arrived(piece, member)),
            )
        full[kind] = max(full[kind], begin + pace * (count // 2) + clock["settle"])

    def finish(kind):
        for piece in of_kind(kind):
            for member in range(count // 2, count):
                arrived(piece, member)
            keeps[piece].wait()

    def load_weight(kind, q, slot):
        return local(outs[kind].at[q], weight.at[slot], weight_sem.at[slot])

    def over_strips(body):
        repeat(tokens // STRIP, lambda s: body(aligned(s * STRIP, STRIP, STRIP)))

    def over_tiles(body):
        repeat(width // WIDE_TILE, lambda t: body(aligned(t * WIDE_TILE, WIDE_TILE, 128)))

    pairs = {}

    def trade(index, source, target):
        pairs[index] = remote(source, target, pair_send.at[index], pair_recv.at[index], sibling)
        finals.append(pairs[index].wait_send)

    def turn(source, index):
        repeat(
            width // 128,
            lambda t: turned.__setitem__(
                (index, aligned(t * 128, 128, 128)), source[:, aligned(t * 128, 128, 128)].T
            ),
        )
        save(turned.at[index], turned_out.at[index, 0], 8 + index)
        trade(index, turned.at[index], turned_out.at[index, 1])
        finals.append(pairs[index].wait_recv)

    def norm_first():
        loads[1].wait()

        def body(where):
            unit, _ = normalized(x_ref[where, :].astype(jnp.float32))
            first[where, :] = (unit * (1.0 + mod_out[1:2, :]) + mod_out[0:1, :]).astype(low)
            upstream = cot[where, :].astype(jnp.float32) * row_mask[where, :]
            change[where, :] = (mod_out[5:6, :] * upstream).astype(low)

        over_strips(body)
        save(change, change_out, 0)
        trade(3, change, other_change)
        bias_out[...] = jnp.zeros_like(bias_out)
        bias_out[0:1, :] = jnp.sum(change[...].astype(jnp.float32), axis=0, keepdims=True)

    weight_loads = {}

    def begin_first():
        finish(0)
        for s in range(2):
            weight_loads[s] = load_weight(0, s, s)

    def project(s, target, bias):
        slot = s % 2
        weight_loads[s].wait()

        def body(where):
            result = nn(first[...], weight[slot, :, where])
            if bias is not None:
                result = result + bias_rows[bias : bias + 1, where]
            target[:, where] = result.astype(low)

        over_tiles(body)
        if s + 2 < 4:
            weight_loads[s + 2] = load_weight(0, s + 2, slot)
        save(target, (query_out, key_out, value_out)[s], 1 + s)

    def clear():
        joined[...] = jnp.zeros_like(joined)
        totals[...] = jnp.zeros_like(totals)

    def attend(head):
        start, span, offset = head_window(head, size)
        where = slice(start, start + span)
        scores = nt(only_head(query[:, where], offset, size), key[:, where])
        scores = jnp.where(key_mask[0:1, :] > 0, scores * scale, MASK_VALUE)
        peak = jnp.max(scores, axis=-1, keepdims=True)
        power = jnp.exp(scores - peak)
        total = jnp.sum(power, axis=-1, keepdims=True)
        attention = (power / total).astype(low)
        joined[:, where] = joined[:, where] + nn(attention, only_head(value[:, where], offset, size))
        lane = lax.broadcasted_iota(jnp.int32, (tokens, 128), 1)
        totals[...] = jnp.where(lane == head, peak + jnp.log(total), totals[...])

    def leave_attention():
        attended[...] = joined[...].astype(low)
        save(totals, total_out, 4)
        weight_loads[3].wait()

        def body(where):
            result = nn(attended[...], weight[1, :, where]) + bias_rows[2:3, where]
            branch[:, where] = result
            midway[:, where] = x_ref[:, where].astype(jnp.float32) + mod_out[2:3, where] * result

        over_tiles(body)
        save(branch, branch_out, 5)
        save(midway, midway_out, 6)

    def norm_second():
        def body(where):
            unit, _ = normalized(midway[where, :])
            second[where, :] = (unit * (1.0 + mod_out[4:5, :]) + mod_out[3:4, :]).astype(low)

        over_strips(body)

    up_loads = {}
    slope_copies = {}

    def begin_up():
        finish(1)
        for s in range(2):
            up_loads[s] = load_weight(1, s, s)

    def raise_up(s):
        slot = s % 2
        up_loads[s].wait()
        if s >= 2:
            slope_copies[s - 2].wait()

        def body(t):
            where = aligned(t * TILE, TILE, 128)
            wide = aligned(s * width + t * TILE, TILE, 128)
            bent, slope = gelu_parts(nn(second[...], weight[slot, :, where]) + bias_rows[aligned(3 + s, 1, 1), where])
            active[:, wide] = bent.astype(low)
            active_turned[wide, :] = bent.astype(low).T
            slope_stage[slot, :, where] = slope

        repeat(width // TILE, body)
        if s + 2 < 4:
            up_loads[s + 2] = load_weight(1, s + 2, slot)
        slope_copies[s] = local(
            slope_stage.at[slot], slope_out.at[:, pl.ds(s * width, width)], slope_sem.at[slot]
        )

    span = 2 * tall_rows

    def plane_rows(j, plane):
        return aligned((2 * j + plane) * span, span)

    def trade_active():
        save(active, active_out, 7)
        for j in range(count // 4):
            trade(4 + j, active_turned.at[plane_rows(j, 1 - core)], other_turned.at[pl.ds(j * span, span)])

    def down_gradients(first_piece):
        if first_piece == 0:
            pairs[3].wait_recv()
        for j in range(first_piece, first_piece + 4):
            pairs[4 + j].wait_recv()

        def piece(at):
            j = first_piece + at
            slot = remainder(j, 2)
            target = down_out.at[aligned(j * span, span)]
            if first_piece:
                await_bytes(target, down_sem.at[slot])
            else:
                pl.when(at >= 2)(lambda: await_bytes(target, down_sem.at[slot]))

            def body(where):
                result = nn(active_turned[plane_rows(j, core), :], change[:, where])
                result = result + nn(other_turned[aligned(j * span, span), :], other_change[:, where])
                down_stage[slot, :, where] = result.astype(low)

            repeat(width // TILE, lambda t: body(aligned(t * TILE, TILE, 128)))
            local(down_stage.at[slot], target, down_sem.at[slot])

        repeat(4, piece)

    takes = clock["takes"]
    agenda.step(takes["norm"], norm_first, clock["terms"][0] + clock["terms"][1] * bits)
    agenda.step(takes["turn"], lambda: turn(first, 0))
    agenda.step(0.3, begin_first, full[0])
    for s, (target, bias) in enumerate(((query, 0), (key, None), (value, 1))):
        agenda.step(takes["matmul"], functools.partial(project, s, target, bias))
    agenda.step(0.3, clear)
    for head in range(HEADS):
        agenda.step(takes["head"], functools.partial(attend, head))
    agenda.step(takes["matmul"], leave_attention)
    agenda.step(takes["norm"], norm_second)
    agenda.step(0.3, begin_up, full[1])
    for s in range(4):
        agenda.step(takes["up"], functools.partial(raise_up, s))
    agenda.step(0.3, trade_active)
    agenda.step(takes["turn"], lambda: turn(attended, 1))
    agenda.step(takes["turn"], lambda: turn(second, 2))
    for j in range(0, count // 4, 4):
        agenda.step(4 * takes["down"], functools.partial(down_gradients, j))
    agenda.emit()
    finish(2)
    for done in finals:
        done()
    for index in (2, 3):
        slope_copies[index].wait()
    for slot in range(2):
        await_bytes(down_out.at[pl.ds(slot * span, span)], down_sem.at[slot])


PIECES = ((0, 0, 96, False), (0, 96, 48, True), (1, 0, 96, False), (1, 96, 48, True), (2, 0, 96, False), (2, 96, 48, True))
CLOCK = {
    "terms": (12.0, 5.0),
    "pieces": ((8.0, 1.44), (8.0, 1.44), (16.0, 4.6), (16.0, 4.6), (24.0, 6.6), (24.0, 6.6)),
    "settle": 10.0,
    "takes": {"norm": 2.0, "turn": 0.6, "matmul": 1.8, "head": 0.42, "up": 3.0, "down": 1.0},
}


def forward(a_src, b_src, c_src, terms, mod_bias, bias_rows, frames, cot, key_mask, row_mask, pieces=PIECES, clock=CLOCK):
    rows, width = a_src.shape[1:]
    tall = c_src.shape[0]
    bits = terms.ndim - 2
    count = 1 << bits
    tokens = frames.shape[0]
    hidden = tall * count
    low, wide = jnp.bfloat16, jnp.float32

    def shaped(*sizes, dtype=low):
        return jax.ShapeDtypeStruct(sizes, dtype)

    anywhere = pl.BlockSpec(memory_space=pl.ANY)
    near = pl.BlockSpec(memory_space=pltpu.VMEM)
    token = shaped(tokens, width)
    token_wide = shaped(tokens, width, dtype=wide)
    outs = (
        shaped(4, width, width), shaped(4, width, width), shaped(hidden, width),
        shaped(8, width, dtype=wide),
        token, token, token, shaped(tokens, 128, dtype=wide),
        token_wide, token_wide,
        shaped(tokens, hidden, dtype=wide), shaped(tokens, hidden), token,
        shaped(3, 2, width, tokens),
        shaped(hidden // 2, width), shaped(8, width, dtype=wide),
    )
    out_specs = [anywhere] * len(outs)
    out_specs[3] = near
    out_specs[-1] = near
    dma = pltpu.SemaphoreType.DMA
    v = pltpu.VMEM
    scratch = [
        v((2, 4, rows, width), low), v((2, 4 * rows, width), low), v((tall, width), low),
        v(terms.shape, wide), tuple(v(terms.shape[step + 1 :], wide) for step in range(bits)),
        v((tokens, width), low), v((tokens, width), low),
        v((tokens, width), low), v((tokens, width), low), v((tokens, width), low),
        v((tokens, 128), wide), v((tokens, width), wide), v((tokens, width), low),
        v((tokens, width), wide), v((tokens, width), wide), v((tokens, width), low),
        v((tokens, hidden), low), v((hidden, tokens), low), v((hidden // 2, tokens), low),
        v((tokens, width), low), v((tokens, width), low), v((3, width, tokens), low),
        v((2, width, width), low), v((2, tokens, width), wide), v((2, 2 * tall, width), low),
        dma((2, 4)), dma((2, 4)), dma((3,)), dma((len(pieces),)), dma((len(pieces), count)), dma((len(pieces), count)),
        dma((bits,)), dma((bits,)), dma((4 + count // 4,)), dma((4 + count // 4,)),
        dma((2,)), dma((2,)), dma((16,)), dma((2,)), dma((2,)),
    ]
    return pl.pallas_call(
        functools.partial(forward_kernel, bits, rows, pieces, clock),
        out_shape=outs,
        in_specs=[anywhere] * 4 + [near] * 2 + [anywhere] + [near] * 3,
        out_specs=out_specs,
        scratch_shapes=scratch,
        compiler_params=pltpu.CompilerParams(collective_id=0, has_side_effects=True, vmem_limit_bytes=56 * 1024 * 1024),
        cost_estimate=pl.CostEstimate(flops=10_000_000_000, bytes_accessed=400_000_000, transcendentals=3_000_000),
        name="forward_gather",
    )(a_src, b_src, c_src, terms, mod_bias, bias_rows, frames, cot, key_mask, row_mask)


def SPREAD(bits):
    return list(range(bits - 1, 1, -1)) + [0, CORE]


def folded_rows(values):
    whole = values.shape[0] // 8 * 8
    result = sum(values[at : at + 8, :] for at in range(0, whole, 8))
    if whole < values.shape[0]:
        rest = values[whole:, :]
        result = result + jnp.concatenate([rest, jnp.zeros((8 - rest.shape[0], rest.shape[1]), rest.dtype)], axis=0)
    return result


def bias_sums(halves, count):
    shape = (ROUND, ROUND * count // 2)
    pick = jnp.where(
        remainder(lax.broadcasted_iota(jnp.int32, shape, 1), ROUND) == lax.broadcasted_iota(jnp.int32, shape, 0), 1.0, 0.0
    ).astype(jnp.bfloat16)
    return nn(pick, halves[0]) + nn(pick, halves[1])


def lifted(lift, part, halves, count):
    half = ROUND * count // 2
    return nn(lift[part, :, :half], halves[0]) + nn(lift[part, :, half:], halves[1])


def backward_kernel(bits, rows, tall_rows, pieces, clock,
                    a_all, b_all, c_all, mod, bias_rows, down_sums, key_mask, row_mask, lift, mod_low, frames, cot_in, query_in, key_in, value_in,
                    total_in, branch_in, midway_in, slope_in, active_in, change_in, turned_in, down_in,
                    block_out, frames_out, spread_out, a_out, b_out, c_out, ordered, norm_out,
                    weight, slabs, other_up, other_low, active, slope, query, key, value, x_ref, cot, change, d_attended,
                    midway, branch, down_acc, d_norm, d_midway, turned, totals, first_grads, second_grads, third_grads, recv, total,
                    quad_block, dmod, bias_out, spread, squares, table, answers, mine, partials,
                    weight_sem, stream_sem, load_sem, save_sem, send_sem, recv_sem, pair_send, pair_recv,
                    quad_send, quad_recv, quad_own, spread_send, spread_recv, spread_own,
                    answer_send, answer_recv, norm_send, norm_recv):
    count = 1 << bits
    spots = Spots(bits)
    core = spots.core
    sibling = spots.device[CORE]
    tokens, width = x_ref.shape
    size = width // HEADS
    scale = size ** (-0.5)
    low, wide = jnp.bfloat16, jnp.float32
    span = 2 * tall_rows
    finals = []

    grads_load = local(down_in, first_grads, load_sem.at[0])
    order = [(c_all, s, True) for s in range(4)] + [(b_all, s, False) for s in range(4)]
    order += [(a_all, 3, False), (a_all, 0, False), (a_all, 1, False), (a_all, 2, False)]
    weights = {}

    def load_weight(index):
        if index < len(order):
            source, s, flat = order[index]
            part = source.at[pl.ds(s * width, width)] if flat else source.at[s]
            weights[index] = local(part, weight.at[index % 2], weight_sem.at[index % 2])

    streams = {}

    def load_stream(s):
        if s < 4:
            where = pl.ds(s * width, width)
            streams[s] = (
                local(slope_in.at[:, where], slope.at[s % 2], stream_sem.at[0, s % 2]),
                local(active_in.at[:, where], active.at[s % 2], stream_sem.at[1, s % 2]),
            )

    change_load = local(change_in, change, load_sem.at[1])
    load_weight(0)
    load_stream(0)
    load_weight(1)
    load_stream(1)
    loads = {
        name: local(source, target, load_sem.at[2 + index])
        for index, (name, source, target) in enumerate(
            (
                ("second", turned_in.at[2], turned.at[2]), ("midway", midway_in, midway), ("cot", cot_in, cot),
                ("branch", branch_in, branch), ("value", value_in, value), ("query", query_in, query), ("key", key_in, key),
                ("totals", total_in, totals), ("first", turned_in.at[0], turned.at[0]),
                ("attended", turned_in.at[1], turned.at[1]), ("x", frames, x_ref),
            )
        )
    }
    spots.greet([distance for distance in range(1, 8)] + [distance << 3 for distance in range(1, count // 8)])
    dmod[...] = jnp.zeros_like(dmod)
    bias_out[...] = jnp.zeros_like(bias_out)
    squares[...] = jnp.zeros_like(squares)

    grads = (third_grads, second_grads, first_grads)
    sums_at = (0, 1, 0)
    block_stage, frames_stage = change, d_attended
    down_copies = []

    def own(piece, member):
        kind, start, length, late = pieces[piece]
        index = spots.block(late, member)
        row = remainder(index, 2) * (tall_rows if kind == 2 else width)
        row = row + quotient(index, 4) * (span if kind == 2 else 4 * rows)
        return grads[kind].at[aligned(row + start, length)]

    def landed(piece, member):
        kind, start, length, _ = pieces[piece]
        return recv.at[kind, member - 1, pl.ds(start, length)]

    sent = {kind: [] for kind in range(3)}

    def pass_on(piece, member):
        kind, _, _, late = pieces[piece]
        place = top_place(member)
        sent[kind].append(
            remote(
                own(piece, member), landed(piece, member), send_sem.at[piece, member], recv_sem.at[piece, member],
                spots.partner(late, place),
            )
        )

    def summed(piece, member, body):
        parts = [member | 1 << place for place in range(top_place(member) + 1, bits - 1)]
        for part in parts:
            await_bytes(landed(piece, part), recv_sem.at[piece, part])
        kind, start, length, _ = pieces[piece]
        mine = own(piece, member)

        def strip(s):
            where = aligned(s * ROUND, ROUND)
            value = mine[where, :].astype(wide)
            for part in parts:
                value = value + recv[kind, part - 1, aligned(start + s * ROUND, ROUND), :].astype(wide)
            body(mine, where, s, value)

        repeat(length // ROUND, strip)

    def relay(piece, member):
        def body(mine, where, s, value):
            mine[where, :] = value.astype(low)

        summed(piece, member, body)
        pass_on(piece, member)

    left = {kind: len([1 for entry in pieces if entry[0] == kind]) for kind in range(3)}

    def settle(piece):
        kind, start, length, _ = pieces[piece]

        def body(mine, where, s, value):
            total[sums_at[kind], aligned(start + s * ROUND, ROUND), :] = value
            squares[...] = squares[...] + value * value

        if kind == 0:
            while down_copies:
                down_copies.pop().wait()
        summed(piece, 0, body)
        left[kind] -= 1
        if left[kind]:
            return
        if kind == 2:
            down_copies.append(local(total.at[0], c_out, save_sem.at[0]))
            return
        for lane in range(0, width, 128):
            for q in range(4):
                part = total[sums_at[kind], q * rows : (q + 1) * rows, lane : lane + 128]
                quad_block[kind, q, :, lane : lane + 128] = part.astype(low)
        out = (a_out, b_out)[kind]
        finals.append(local(quad_block.at[kind, spots.quad], out.at[spots.quad], quad_own.at[kind]).wait)
        for other in (1, 2, 3):
            device, spot = spots.near(other)
            copy = remote(
                quad_block.at[kind, spot], out.at[spots.quad], quad_send.at[kind, other], quad_recv.at[kind, other], device
            )
            finals.append(copy.wait)

    agenda = Agenda()

    def open_kind(kind):
        half = count // 2
        for member in range(half - 1, half // 2 - 1, -1):
            for piece, entry in enumerate(pieces):
                if entry[0] == kind:
                    pass_on(piece, member)
        begin, pace = clock["open"][kind]
        for piece, entry in enumerate(pieces):
            if entry[0] == kind:
                for at, member in enumerate(range(half // 2 - 1, 0, -1)):
                    agenda.service(agenda.now + begin + pace * at, functools.partial(relay, piece, member))
                agenda.service(agenda.now + begin + pace * (half // 2 - 1), functools.partial(settle, piece))

    def open_down():
        grads_load.wait()
        open_kind(2)

    pairs = {}

    def trade(index, source, target):
        pairs[index] = remote(source, target, pair_send.at[index], pair_recv.at[index], sibling)

    def over_strips(body):
        repeat(tokens // STRIP, lambda s: body(aligned(s * STRIP, STRIP, STRIP)))

    def over_tiles(body):
        repeat(width // TILE, lambda t: body(aligned(t * TILE, TILE, 128)))

    def add_row(ref, row, where, values):
        ref[row : row + 1, where] = ref[row : row + 1, where] + jnp.sum(values, axis=0, keepdims=True)

    everything = slice(None)

    def down_slice(s):
        slot = s % 2
        if s == 0:
            change_load.wait()
        weights[s].wait()
        for copy in streams[s]:
            copy.wait()

        def body(where):
            d_up = (nt(change[...], weight[slot, where, :]) * slope[slot, :, where]).astype(low)
            slabs[s, :, where] = d_up
            add_row(bias_out, 3 + s, where, d_up.astype(wide))
            part = nn(active[slot], weight[slot, :, where])
            down_acc[:, where] = part if s == 0 else down_acc[:, where] + part

        over_tiles(body)
        load_weight(s + 2)
        load_stream(s + 2)

    def trade_up():
        for t in range(2):
            trade(t, slabs.at[2 * (1 - core) + t], other_up.at[t])

    def up_gradient(t):
        if t == 0:
            loads["second"].wait()
        pairs[t].wait_recv()

        def body(where):
            def strip(m):
                down = aligned(m * 288, 288)
                result = nn(turned[2, 0, down, :], slabs[2 * core + t, :, where])
                result = result + nn(turned[2, 1, down, :], other_up[t, :, where])
                second_grads[aligned(t * width + m * 288, 288), where] = result.astype(low)

            repeat(width // 288, strip)

        over_tiles(body)

    def norm_two_slice(s):
        weights[4 + s].wait()

        def body(where):
            part = nt(slabs[s], weight[s % 2, where, :])
            d_norm[:, where] = part if s == 0 else d_norm[:, where] + part

        over_tiles(body)
        load_weight(6 + s)

    def upstream_of(where):
        return cot[where, :].astype(wide) * row_mask[where, :]

    def norm_back(values, gradient, gain):
        unit, root = normalized(values)
        spread = gain * gradient
        back = root * (
            spread
            - jnp.mean(spread, axis=-1, keepdims=True)
            - unit * jnp.mean(spread * unit, axis=-1, keepdims=True)
        )
        return unit, back

    def back_second():
        for name in ("midway", "cot", "branch"):
            loads[name].wait()
        for t in range(2):
            pairs[t].wait_send()

        def body(where):
            gradient = d_norm[where, :]
            unit, back = norm_back(midway[where, :], gradient, 1.0 + mod[4:5, :])
            middle = upstream_of(where) + back
            d_midway[where, :] = middle
            d_branch = (mod[2:3, :] * middle).astype(low)
            slabs[3, where, :] = d_branch
            add_row(dmod, 3, everything, gradient)
            add_row(dmod, 4, everything, gradient * unit)
            add_row(dmod, 2, everything, middle * branch[where, :])
            add_row(bias_out, 2, everything, d_branch.astype(wide))

        over_strips(body)

    def back_attended():
        weights[8].wait()

        def body(where):
            d_attended[:, where] = nt(slabs[3], weight[0, where, :]).astype(low)

        over_tiles(body)
        load_weight(10)
        for name in ("value", "query", "key", "totals"):
            loads[name].wait()
        slope[...] = jnp.zeros_like(slope)
        branch[...] = jnp.zeros_like(branch)

    def attend_back(head):
        start, reach, offset = head_window(head, size)
        where = slice(start, start + reach)
        chosen = only_head(query[:, where], offset, size)
        scores = nt(chosen, key[:, where])
        scores = jnp.where(key_mask[0:1, :] > 0, scores * scale, MASK_VALUE)
        soft = jnp.exp(scores - totals[:, head : head + 1])
        given = only_head(d_attended[:, where], offset, size)
        d_soft = nt(given, value[:, where])
        d_scores = (soft * (d_soft - jnp.sum(soft * d_soft, axis=-1, keepdims=True))).astype(low)
        slope[0, :, where] = slope[0, :, where] + nn(d_scores, only_head(key[:, where], offset, size))
        slope[1, :, where] = slope[1, :, where] + tn(d_scores, chosen)
        branch[:, where] = branch[:, where] + tn(soft.astype(low), given)

    def leave_attention():
        slabs[0] = (slope[0] * scale).astype(low)
        slabs[1] = (slope[1] * scale).astype(low)
        slabs[2] = branch[...].astype(low)
        for t in range(2):
            trade(2 + t, slabs.at[2 * (1 - core) + t], other_low.at[t])
        bias_out[0:1, :] = jnp.sum(slabs[0].astype(wide), axis=0, keepdims=True)
        bias_out[1:2, :] = jnp.sum(slabs[2].astype(wide), axis=0, keepdims=True)

    def leave_block():
        def body(where):
            down = down_acc[where, :] + bias_rows[7:8, :]
            add_row(dmod, 5, everything, upstream_of(where) * down)
            block_stage[where, :] = ((midway[where, :] + mod[5:6, :] * down) * row_mask[where, :]).astype(low)

        over_strips(body)
        finals.append(local(block_stage, block_out, save_sem.at[1]).wait)

    def low_gradient(t):
        if t == 0:
            loads["first"].wait()
            loads["attended"].wait()
        pairs[2 + t].wait_recv()
        at = 2 * core + t
        which = quotient(at, 3)

        def body(where):
            def strip(m):
                down = aligned(m * 288, 288)
                result = nn(turned[which, 0, down, :], slabs[at, :, where])
                result = result + nn(turned[which, 1, down, :], other_low[t, :, where])
                third_grads[aligned(t * width + m * 288, 288), where] = result.astype(low)

            repeat(width // 288, strip)

        over_tiles(body)

    def norm_one_slice(s):
        weights[9 + s].wait()

        def body(where):
            part = nt(slabs[s], weight[(9 + s) % 2, where, :])
            d_norm[:, where] = part if s == 0 else d_norm[:, where] + part

        over_tiles(body)
        load_weight(11 + s)

    def back_first():
        loads["x"].wait()

        def body(where):
            gradient = d_norm[where, :]
            unit, back = norm_back(x_ref[where, :].astype(wide), gradient, 1.0 + mod[1:2, :])
            add_row(dmod, 0, everything, gradient)
            add_row(dmod, 1, everything, gradient * unit)
            frames_stage[where, :] = (back + d_midway[where, :]).astype(low)

        over_strips(body)
        finals.append(local(frames_stage, frames_out, save_sem.at[2]).wait)

    spread_copies = []

    def spread_step(step):
        if step == 0:
            spread_start.wait()
        else:
            spread_copies[step - 1].wait_recv()
        if step == bits:
            use_spread()
            return
        held = pl.ds(0, ROUND << step)
        copy = remote(
            spread_out.at[held], spread_out.at[pl.ds(ROUND << step, ROUND << step)], spread_send.at[step],
            spread_recv.at[step], spots.device[SPREAD(bits)[step]],
        )
        spread_copies.append(copy)
        finals.append(copy.wait_send)
        agenda.service(agenda.now + clock["spread"], functools.partial(spread_step, step + 1))

    def start_spread():
        nonlocal spread_start
        bias_out[7:8, :] = down_sums[0:1, :]
        spread[...] = jnp.concatenate([dmod[...], bias_out[...]], axis=0).astype(low)
        spread_start = local(spread, spread_out.at[pl.ds(0, ROUND)], spread_own)
        agenda.service(agenda.now + 1.0, functools.partial(spread_step, 0))

    def use_spread():
        half = ROUND * count // 2
        copies = [local(spread_out.at[pl.ds(t * half, half)], active.at[t], stream_sem.at[1, t]) for t in range(2)]
        for copy in copies:
            copy.wait()
        both = bias_sums(active, count)
        squares[...] = squares[...] + both * both * (1.0 / count)
        member = remainder(lax.broadcasted_iota(jnp.int32, (half, rows), 0), ROUND)
        partial = [jnp.zeros((half, rows), wide) for _ in range(2)]
        for part in range(6):
            where = slice(part * width, (part + 1) * width)
            value = lifted(lift, part, active, count)
            squares[0:8, :] = squares[0:8, :] + folded_rows(value * value)
            for t in range(2):
                partial[t] = partial[t] + jnp.where(member == part, nt(active[t], mod_low[:, where]), 0.0)
        table[...] = jnp.zeros_like(table)
        shape = (count // 2, half)
        gathers = jnp.where(
            quotient(lax.broadcasted_iota(jnp.int32, shape, 1), ROUND) == lax.broadcasted_iota(jnp.int32, shape, 0), 1.0, 0.0
        )
        for t in range(2):
            table[t * count // 2 : (t + 1) * count // 2, 0:rows] = jnp.dot(
                gathers, partial[t], preferred_element_type=wide, precision=lax.Precision.HIGHEST
            )
        agenda.service(agenda.now + 0.1, functools.partial(answer_step, 0))

    answer_copies = []

    def answer_step(step):
        if step:
            slot = lax.broadcasted_iota(jnp.int32, (count, 128), 0)
            answer_copies[step - 1].wait()
            took = remainder(quotient(slot, 1 << step - 1), 2) == 1
            table[...] = jnp.where(took, answers[step - 1], table[...])
        if step < bits:
            answer_copies.append(
                remote(
                    table, answers.at[step], answer_send.at[step], answer_recv.at[step], spots.device[SPREAD(bits)[step]]
                )
            )
            agenda.service(agenda.now + clock["spread"], functools.partial(answer_step, step + 1))
            return
        for member in range(count):
            index = spots.me
            for place, bit in enumerate(SPREAD(bits)):
                if member >> place & 1:
                    index = index + spots.delta[bit]
            ordered[pl.ds(index, 1), :] = table[member : member + 1, :]

    def norm_round(first, amount, column):
        slot = sum((1 << at) * spots.digit[first + at] for at in range(amount))
        partials[column, slot] = mine[...]
        copies = []
        for distance in range(1, 1 << amount):
            copies.append(
                remote(
                    mine, partials.at[column, slot], norm_send.at[column, distance], norm_recv.at[column, distance],
                    spots.across(distance << first),
                )
            )
        for copy in copies:
            copy.wait()
        return sum(partials[column, at] for at in range(1 << amount))

    def answer():
        total_square = jnp.sum(squares[...], axis=0, keepdims=True)
        folded = sum(total_square[:, at : at + 128] for at in range(0, width, 128))
        mine[...] = jnp.broadcast_to(folded, (8, 128))
        mine[...] = norm_round(0, 3, 0)
        whole = norm_round(3, bits - 3, 1)
        norm_out[...] = jnp.broadcast_to(jnp.sqrt(jnp.sum(whole, axis=1, keepdims=True)), (8, 128))

    spread_start = None
    takes = clock["takes"]
    agenda.step(2.0, open_down)
    for s in range(4):
        agenda.step(takes["down"], functools.partial(down_slice, s))
    agenda.step(0.3, trade_up)
    for t in range(2):
        agenda.step(takes["gradient"], functools.partial(up_gradient, t))
    agenda.step(0.5, lambda: open_kind(1))
    for s in range(4):
        agenda.step(takes["matmul"], functools.partial(norm_two_slice, s))
    agenda.step(takes["norm"], back_second)
    agenda.step(takes["matmul"], back_attended)
    for head in range(HEADS):
        agenda.step(takes["head"], functools.partial(attend_back, head))
    agenda.step(1.0, leave_attention)
    agenda.step(takes["norm"], leave_block)
    for t in range(2):
        agenda.step(takes["gradient"], functools.partial(low_gradient, t))
    agenda.step(0.5, lambda: open_kind(0))
    for s in range(3):
        agenda.step(takes["matmul"], functools.partial(norm_one_slice, s))
    agenda.step(takes["norm"], back_first)
    agenda.step(0.5, start_spread)
    agenda.emit()
    answer()
    for kind in range(3):
        for copy in sent[kind]:
            copy.wait_send()
    for t in range(2):
        pairs[2 + t].wait_send()
    for done in finals:
        done()


BACK_CLOCK = {
    "spread": 4.0,
    "open": ((22.0, 4.0), (24.0, 5.5), (20.0, 5.0)),
    "takes": {"down": 4.2, "gradient": 4.2, "matmul": 2.1, "norm": 1.7, "head": 0.42},
}


def backward(weights, mod, bias_rows, down_sums, key_mask, row_mask, lift, mod_low, frames, cot, saved, rows, bits, pieces=PIECES, clock=BACK_CLOCK):
    a_all, b_all, c_all = weights
    width = a_all.shape[-1]
    count = 1 << bits
    hidden = c_all.shape[0]
    tall = hidden // count
    tokens = frames.shape[0]
    low, wide = jnp.bfloat16, jnp.float32

    def shaped(*sizes, dtype=low):
        return jax.ShapeDtypeStruct(sizes, dtype)

    anywhere = pl.BlockSpec(memory_space=pl.ANY)
    near = pl.BlockSpec(memory_space=pltpu.VMEM)
    dma = pltpu.SemaphoreType.DMA
    v = pltpu.VMEM
    kinds = len(pieces)
    scratch = [
        v((2, width, width), low), v((4, tokens, width), low),
        v((2, tokens, width), low), v((2, tokens, width), low),
        v((2, tokens, width), low), v((2, tokens, width), wide),
        v((tokens, width), low), v((tokens, width), low), v((tokens, width), low),
        v((tokens, width), low), v((tokens, width), low), v((tokens, width), low), v((tokens, width), low),
        v((tokens, width), wide), v((tokens, width), wide),
        v((tokens, width), wide), v((tokens, width), wide), v((tokens, width), wide),
        v((3, 2, width, tokens), low), v((tokens, 128), wide),
        v((2 * width, width), low), v((2 * width, width), low), v((2 * width, width), low),
        v((3, count // 2 - 1, 4 * rows, width), low), v((2, 4 * rows, width), wide), v((2, 4, rows, width), low),
        v((8, width), wide), v((8, width), wide), v((ROUND, width), low),
        v((ROUND, width), wide), v((count, 128), wide), v((bits, count, 128), wide),
        v((8, 128), wide), v((2, 8, 8, 128), wide),
        dma((2,)), dma((2, 2)), dma((13,)), dma((3,)), dma((kinds, count // 2)), dma((kinds, count // 2)),
        dma((4,)), dma((4,)), dma((2, 4)), dma((2, 4)), dma((2,)), dma((bits,)), dma((bits,)), dma, dma((bits,)), dma((bits,)), dma((2, 8)), dma((2, 8)),
    ]
    share = shaped(4, rows, width)
    return pl.pallas_call(
        functools.partial(backward_kernel, bits, rows, tall, pieces, clock),
        out_shape=(
            shaped(tokens, width), shaped(tokens, width), shaped(ROUND * count, width),
            share, share, shaped(tall, width, dtype=wide), shaped(count, 128, dtype=wide), shaped(8, 128, dtype=wide),
        ),
        in_specs=[anywhere] * 3 + [near] * 7 + [anywhere] * (2 + len(saved)),
        out_specs=[anywhere] * 6 + [near] * 2,
        scratch_shapes=scratch,
        compiler_params=pltpu.CompilerParams(collective_id=1, has_side_effects=True, vmem_limit_bytes=63 * 1024 * 1024),
        cost_estimate=pl.CostEstimate(flops=18_000_000_000, bytes_accessed=400_000_000, transcendentals=3_000_000),
        name="backward_reduce",
    )(a_all, b_all, c_all, mod, bias_rows, down_sums, key_mask, row_mask, lift, mod_low, frames, cot, *saved)


def update_kernel(count, a_in, b_in, c_in, spread_in, lift, norm, bias, bias_state, *rest):
    masters, states, rest = rest[:5], rest[5:10], rest[10:]
    grads, news, news_state, rest = rest[:5], rest[5:10], rest[10:15], rest[15:]
    (bias_grad, bias_new, bias_state_new), rest = rest[:3], rest[3:]
    w, st, g, rest = rest[:5], rest[5:10], rest[10:15], rest[15:]
    a_sum, b_sum, spread, sums, in_sem, load_sem, out_sem = rest
    wide = jnp.float32
    width = a_sum.shape[2]
    half = ROUND * count // 2
    inputs = [
        local(source, target, in_sem.at[index])
        for index, (source, target) in enumerate(
            (
                (spread_in.at[pl.ds(0, half)], spread.at[0]), (spread_in.at[pl.ds(half, half)], spread.at[1]),
                (a_in, a_sum), (b_in, b_sum), (c_in, g[4]),
            )
        )
    ]
    sequence = (0, 3, 4, 1, 2)
    loads = {
        k: (local(masters[k], w[k], load_sem.at[0, k]), local(states[k], st[k], load_sem.at[1, k])) for k in sequence
    }
    factor = jnp.minimum(1.0, CLIP / (norm[0:1, 0:1] + 1e-06))
    for copy in inputs:
        copy.wait()
    both = bias_sums(spread, count)
    sums[...] = jnp.zeros_like(sums)
    sums[0:6, :] = both[0:6, :]
    sums[6:14, :] = both[8:16, :]

    def adam(weight, first_moment, second_moment, average, raw):
        grad = raw * factor
        moved = FIRST_DECAY * first_moment + (1.0 - FIRST_DECAY) * grad
        around = SECOND_DECAY * second_moment + (1.0 - SECOND_DECAY) * grad * grad
        step = (moved / (1.0 - FIRST_DECAY**STEPS)) / (jnp.sqrt(around / (1.0 - SECOND_DECAY**STEPS)) + ADAM_EPS)
        fresh = weight - RATE * (step + WEIGHT_DECAY * weight)
        return grad, fresh, moved, around, AVERAGE_DECAY * average + (1.0 - AVERAGE_DECAY) * fresh

    share = bias.shape[1]
    first = (lax.axis_index("wide") * 2 + lax.axis_index("narrow")) * share
    top = quotient(first, width)
    pair = jnp.concatenate([sums[pl.ds(top, 1), :], sums[pl.ds(top + 1, 1), :]], axis=1)
    pair = jnp.broadcast_to(pair, (8, 2 * width))
    bias_raw = pltpu.roll(pair, 2 * width - (first - top * width), 1)[0:1, :share]
    results = adam(bias[...], bias_state[0:1, :], bias_state[1:2, :], bias_state[2:3, :], bias_raw)
    bias_grad[...], bias_new[...] = results[:2]
    for part in range(3):
        bias_state_new[part : part + 1, :] = results[2 + part]
    stores = []
    for k in sequence:
        for copy in loads[k]:
            copy.wait()
        tile = 128 if k == 4 else WIDE_TILE
        pieces = width // tile

        def body(index, k=k, tile=tile, pieces=pieces):
            part = quotient(index, pieces)
            inner = aligned(remainder(index, pieces) * tile, tile, 128)
            where = aligned(index * tile, tile, 128)
            if k == 0:
                raw = nn(lift[part, :, :half], spread[0, :, inner]) + nn(lift[part, :, half:], spread[1, :, inner])
            elif k == 4:
                raw = g[4][:, where]
            else:
                raw = (b_sum if k == 3 else a_sum)[3 if k == 2 else part, :, inner].astype(wide)
            results = adam(w[k][:, where], st[k][0, :, where], st[k][1, :, where], st[k][2, :, where], raw)
            g[k][:, where], w[k][:, where] = results[:2]
            for slot in range(3):
                st[k][slot, :, where] = results[2 + slot]

        repeat(w[k].shape[1] // tile, body)
        for at, (source, target) in enumerate(((g[k], grads[k]), (w[k], news[k]), (st[k], news_state[k]))):
            stores.append(local(source, target, out_sem.at[at, k]))
    for copy in stores:
        copy.wait()


def update(sums, spread, lift, norm, masters, states):
    a_sum, b_sum, c_sum = sums
    count = spread.shape[0] // ROUND
    wide = jnp.float32
    anywhere = pl.BlockSpec(memory_space=pl.ANY)
    near = pl.BlockSpec(memory_space=pltpu.VMEM)
    dma = pltpu.SemaphoreType.DMA

    def like(member):
        return jax.ShapeDtypeStruct(member.shape, member.dtype)

    width = a_sum.shape[2]
    bias, bias_state = masters[5].reshape(1, -1), states[5]
    outs = [like(member) for member in masters[:5]] * 2 + [like(member) for member in states[:5]]
    outs += [like(bias), like(bias), like(bias_state)]
    buffers = [pltpu.VMEM(member.shape, wide) for member in tuple(masters[:5]) + tuple(states[:5]) + tuple(masters[:5])]
    results = pl.pallas_call(
        functools.partial(update_kernel, count),
        out_shape=tuple(outs),
        in_specs=[anywhere] * 4 + [near] * 4 + [anywhere] * 10,
        out_specs=tuple([anywhere] * 15 + [near] * 3),
        scratch_shapes=buffers + [
            pltpu.VMEM(a_sum.shape, a_sum.dtype), pltpu.VMEM(b_sum.shape, b_sum.dtype),
            pltpu.VMEM((2, spread.shape[0] // 2, width), spread.dtype), pltpu.VMEM((ROUND, width), wide),
            dma((5,)), dma((2, 5)), dma((3, 5)),
        ],
        compiler_params=pltpu.CompilerParams(vmem_limit_bytes=56 * 1024 * 1024),
        cost_estimate=pl.CostEstimate(flops=100_000_000, bytes_accessed=40_000_000, transcendentals=1_000_000),
        name="update",
    )(a_sum, b_sum, c_sum, spread, lift, norm, bias, bias_state, *masters[:5], *states[:5])
    grads, news, news_state = results[:5], results[5:10], results[10:15]
    bias_grad, bias_new, bias_state_new = results[15:]
    grads = tuple(grads) + (bias_grad.reshape(-1),)
    news = tuple(news) + (bias_new.reshape(-1),)
    return grads, news, tuple(news_state) + (bias_state_new,)


def masks(order, member):
    return sum(1 << bit for place, bit in enumerate(order) if member >> place & 1)


def me_index():
    return lax.axis_index("wide") * 2 + lax.axis_index("narrow")


def device(index):
    return (index // 2, lax.rem(index, 2))


def own_plane(me):
    return lax.rem(me // 2, 2)


def flip(index, mask):
    out = index
    bit = 0
    while mask >> bit:
        if mask >> bit & 1:
            value = lax.rem(out // (1 << bit), 2)
            out = out + (1 << bit) * (1 - 2 * value)
        bit += 1
    return out


def block_of(me, pair, member, bits):
    plane = own_plane(me)
    last = 1 << (bits - 1)
    if member & last:
        rest = member - last
        zero = flip(flip(me, 1 << CORE), masks(pair[1], rest))
        one = flip(flip(me, 1 << CORE), masks(pair[0], rest))
    else:
        zero = flip(me, masks(pair[0], member))
        one = flip(me, masks(pair[1], member))
    return jnp.where(plane == 0, zero, one)


def partner_of(me, pair, place):
    zero = flip(me, 1 << pair[0][place])
    if pair[0][place] == pair[1][place]:
        return zero
    return jnp.where(own_plane(me) == 0, zero, flip(me, 1 << pair[1][place]))


def greet(me, bits):
    barrier = pltpu.get_barrier_semaphore()
    partners = [flip(me, 1 << bit) for bit in range(bits)] + [flip(me, 3)]
    for partner in partners:
        pl.semaphore_signal(barrier, inc=1, device_id=device(partner), device_id_type=MESH)
    pl.semaphore_wait(barrier, len(partners))


def gather_kernel(bits, rows, lates, a_src, b_src, c_src, a_out, b_out, c_out,
                  stage, block, c_block, quad_send, quad_recv, own_sem, keep_sem, send_sem, recv_sem):
    count = 1 << bits
    me = me_index()
    quad, spot = lax.rem(me, 4), me // 4
    pairs = [orders(bits, late) for late in lates]
    outs = (a_out, b_out, c_out)

    def place(kind, index):
        q, j = lax.rem(index, 4), index // 4
        return outs[kind].at[q, j] if kind < 2 else outs[kind].at[j, q]

    def send(kind, member, step, source):
        target = member | 1 << step
        return pltpu.make_async_remote_copy(
            src_ref=source,
            dst_ref=place(kind, block_of(me, pairs[kind], member, bits)),
            send_sem=send_sem.at[kind, target],
            recv_sem=recv_sem.at[kind, target],
            device_id=device(partner_of(me, pairs[kind], step)),
            device_id_type=MESH,
        )

    own = []
    for kind, source in enumerate((a_src, b_src)):
        own.append(pltpu.make_async_copy(source.at[quad], stage.at[kind, quad], own_sem.at[kind]))
    own.append(pltpu.make_async_copy(c_src, c_block, own_sem.at[2]))
    for copy in own:
        copy.start()
    greet(me, bits)
    quads = []
    for kind, source in enumerate((a_src, b_src)):
        for other in (1, 2, 3):
            copy = pltpu.make_async_remote_copy(
                src_ref=source.at[flip(quad, other)],
                dst_ref=stage.at[kind, quad],
                send_sem=quad_send.at[kind, other],
                recv_sem=quad_recv.at[kind, other],
                device_id=device(flip(me, other)),
                device_id_type=MESH,
            )
            copy.start()
            quads.append(copy)
    sends = []
    keeps = []

    def launch(kind, member, source):
        for step in range(top_place(member) + 1, bits):
            copy = send(kind, member, step, source)
            copy.start()
            sends.append(copy)

    def keep(kind, source):
        copy = pltpu.make_async_copy(source, place(kind, me), keep_sem.at[kind])
        copy.start()
        keeps.append(copy)

    own[2].wait()
    launch(2, 0, c_block)
    keep(2, c_block)
    padded = block.shape[1]
    for kind in (0, 1):
        own[kind].wait()
        for copy in quads[3 * kind:3 * kind + 3]:
            copy.wait_recv()
        for lane in range(0, stage.shape[3], 128):
            parts = [stage[kind, q, :, lane:lane + 128].astype(jnp.float32) for q in range(4)]
            if padded > 4 * rows:
                parts.append(jnp.zeros((padded - 4 * rows, 128), jnp.float32))
            block[kind, :, lane:lane + 128] = jnp.concatenate(parts, axis=0).astype(jnp.bfloat16)
        launch(kind, 0, block.at[kind])
        keep(kind, block.at[kind])

    def arrived(kind, member):
        spot_ref = place(kind, block_of(me, pairs[kind], member, bits))
        pltpu.make_async_copy(spot_ref, spot_ref, recv_sem.at[kind, member]).wait()
        return spot_ref

    for member in range(1, count):
        for kind in (2, 0, 1):
            launch(kind, member, arrived(kind, member))
    for copy in sends + quads:
        copy.wait_send()
    for copy in keeps:
        copy.wait()


def gather(a_src, b_src, c_src, count, lates=(False, False, False)):
    bits = count.bit_length() - 1
    rows, columns = a_src.shape[1:]
    padded = -(-4 * rows // 16) * 16
    c_padded = -(-c_src.shape[0] // 16) * 16
    if c_padded != c_src.shape[0]:
        c_src = jnp.pad(c_src, ((0, c_padded - c_src.shape[0]), (0, 0)))
    kinds = 3
    anywhere = pl.BlockSpec(memory_space=pl.ANY)
    big = jax.ShapeDtypeStruct((4, count // 4, padded, columns), jnp.bfloat16)
    tall = jax.ShapeDtypeStruct((count // 4, 4, c_padded, columns), jnp.bfloat16)
    a_all, b_all, c_all = pl.pallas_call(
        functools.partial(gather_kernel, bits, rows, lates),
        out_shape=(big, big, tall),
        in_specs=[anywhere] * 3,
        out_specs=(anywhere,) * 3,
        scratch_shapes=[
            pltpu.VMEM((2, 4, rows, columns), jnp.bfloat16),
            pltpu.VMEM((2, padded, columns), jnp.bfloat16),
            pltpu.VMEM((c_padded, columns), jnp.bfloat16),
            pltpu.SemaphoreType.DMA((2, 4)),
            pltpu.SemaphoreType.DMA((2, 4)),
            pltpu.SemaphoreType.DMA((3,)),
            pltpu.SemaphoreType.DMA((3,)),
            pltpu.SemaphoreType.DMA((kinds, count)),
            pltpu.SemaphoreType.DMA((kinds, count)),
        ],
        compiler_params=pltpu.CompilerParams(collective_id=2, has_side_effects=True),
        cost_estimate=pl.CostEstimate(flops=0, bytes_accessed=400_000_000, transcendentals=0),
        name="gather_weights",
    )(a_src, b_src, c_src)
    return a_all, b_all, c_all


def reduce_kernel(bits, rows, lates, a_in, b_in, c_in, a_out, b_out, c_out,
                  own, recv, quad_block, total, own_sem, send_sem, recv_sem, quad_send, quad_recv, quad_own, total_sem):
    count = 1 << bits
    half = count // 2
    me = me_index()
    quad = lax.rem(me, 4)
    pairs = [orders(bits, late) for late in lates]
    ins = (a_in, b_in, c_in)
    kinds = (2, 1, 0)

    def place(kind, index):
        q, j = lax.rem(index, 4), index // 4
        return ins[kind].at[q, j] if kind < 2 else ins[kind].at[j, q]

    loads = {}
    for member in range(half - 1, -1, -1):
        for kind in kinds:
            loads[kind, member] = pltpu.make_async_copy(
                place(kind, block_of(me, pairs[kind], member, bits)), own.at[kind, member], own_sem.at[kind, member]
            )
    sends = []

    def send(kind, member, source):
        step = top_place(member)
        copy = pltpu.make_async_remote_copy(
            src_ref=source,
            dst_ref=recv.at[kind, member],
            send_sem=send_sem.at[kind, member],
            recv_sem=recv_sem.at[kind, member],
            device_id=device(partner_of(me, pairs[kind], step)),
            device_id_type=MESH,
        )
        copy.start()
        sends.append(copy)

    for kind in kinds:
        loads[kind, half - 1].start()
    greet(me, bits)
    for member in range(half - 1, -1, -1):
        for kind in kinds:
            send(kind, member + half, place(kind, block_of(me, pairs[kind], member + half, bits)))
            if member < half - 1:
                loads[kind, member].start()

    padded, columns = own.shape[2:]

    def ready(kind, member):
        loads[kind, member].wait()
        parts = [member | 1 << step for step in range(top_place(member) + 1, bits)]
        for part in parts:
            pltpu.make_async_copy(recv.at[kind, part], recv.at[kind, part], recv_sem.at[kind, part]).wait()
        return parts

    def summed(kind, member, parts, where):
        value = own[kind, member, where, :].astype(jnp.float32)
        for part in parts:
            value = value + recv[kind, part, where, :].astype(jnp.float32)
        return value

    for member in range(half - 1, 0, -1):
        for kind in kinds:
            parts = ready(kind, member)

            def strip(s, carry, kind=kind, member=member, parts=parts):
                where = pl.ds(pl.multiple_of(s * 16, 16), 16)
                own[kind, member, where, :] = summed(kind, member, parts, where).astype(jnp.bfloat16)
                return carry

            lax.fori_loop(0, padded // 16, strip, 0)
            send(kind, member, own.at[kind, member])

    copies = []
    for kind in kinds:
        parts = ready(kind, 0)

        def strip(s, carry, kind=kind, parts=parts):
            where = pl.ds(pl.multiple_of(s * 16, 16), 16)
            total[kind, where, :] = summed(kind, 0, parts, where)
            return carry

        lax.fori_loop(0, padded // 16, strip, 0)
        if kind == 2:
            copy = pltpu.make_async_copy(total.at[2], c_out, total_sem)
            copy.start()
            copies.append(copy)
            continue
        out = (a_out, b_out)[kind]
        for lane in range(0, columns, 128):
            for q in range(4):
                quad_block[kind, q, :, lane:lane + 128] = total[kind, q * rows:(q + 1) * rows, lane:lane + 128].astype(jnp.bfloat16)
        copy = pltpu.make_async_copy(quad_block.at[kind, quad], out.at[quad], quad_own.at[kind])
        copy.start()
        copies.append(copy)
        for other in (1, 2, 3):
            copy = pltpu.make_async_remote_copy(
                src_ref=quad_block.at[kind, flip(quad, other)],
                dst_ref=out.at[quad],
                send_sem=quad_send.at[kind, other],
                recv_sem=quad_recv.at[kind, other],
                device_id=device(flip(me, other)),
                device_id_type=MESH,
            )
            copy.start()
            copies.append(copy)
    for copy in copies:
        copy.wait()
    for copy in sends:
        copy.wait_send()


def reduce(a_in, b_in, c_in, rows, lates=(False, False, False)):
    count = a_in.shape[1] * 4
    bits = count.bit_length() - 1
    padded, columns = a_in.shape[2:]
    anywhere = pl.BlockSpec(memory_space=pl.ANY)
    share = jax.ShapeDtypeStruct((4, rows, columns), jnp.bfloat16)
    return pl.pallas_call(
        functools.partial(reduce_kernel, bits, rows, lates),
        out_shape=(share, share, jax.ShapeDtypeStruct((padded, columns), jnp.float32)),
        in_specs=[anywhere] * 3,
        out_specs=(anywhere,) * 3,
        scratch_shapes=[
            pltpu.VMEM((3, count // 2, padded, columns), jnp.bfloat16),
            pltpu.VMEM((3, count, padded, columns), jnp.bfloat16),
            pltpu.VMEM((2, 4, rows, columns), jnp.bfloat16),
            pltpu.VMEM((3, padded, columns), jnp.float32),
            pltpu.SemaphoreType.DMA((3, count // 2)),
            pltpu.SemaphoreType.DMA((3, count)),
            pltpu.SemaphoreType.DMA((3, count)),
            pltpu.SemaphoreType.DMA((2, 4)),
            pltpu.SemaphoreType.DMA((2, 4)),
            pltpu.SemaphoreType.DMA((2,)),
            pltpu.SemaphoreType.DMA,
        ],
        compiler_params=pltpu.CompilerParams(collective_id=3, has_side_effects=True, vmem_limit_bytes=62 * 1024 * 1024),
        cost_estimate=pl.CostEstimate(flops=0, bytes_accessed=400_000_000, transcendentals=0),
        name="reduce_gradients",
    )(a_in, b_in, c_in)


def layer_norm(values):
    centre = jnp.mean(values, axis=-1, keepdims=True)
    centred = values - centre
    spread = jnp.mean(centred * centred, axis=-1, keepdims=True)
    return centred * lax.rsqrt(spread + NORM_EPS)


def modulate(values, shift_part, scale_part):
    return layer_norm(values) * (1.0 + scale_part) + shift_part


def silu_act(values):
    return values * jax.nn.sigmoid(values)


def gelu_tanh(values):
    inner = 0.7978845608028654 * (values + 0.044715 * values * values * values)
    return 0.5 * values * (1.0 + jnp.tanh(inner))


def slot_mask(grid, frame_len):
    area = grid[:, 0] * grid[:, 1]
    return lax.broadcasted_iota(jnp.int32, (grid.shape[0], frame_len), 1) < area[:, None]


def split_biases(biases, model_width, hidden_width):
    edges = [
        6 * model_width,
        7 * model_width,
        8 * model_width,
        9 * model_width,
        9 * model_width + hidden_width,
    ]
    return jnp.split(biases, edges)


def adam_update(weight, state, grad):
    first = FIRST_DECAY * state[0] + (1.0 - FIRST_DECAY) * grad
    second = SECOND_DECAY * state[1] + (1.0 - SECOND_DECAY) * grad * grad
    first_hat = first / (1.0 - FIRST_DECAY**STEPS)
    second_hat = second / (1.0 - SECOND_DECAY**STEPS)
    new_weight = weight - RATE * (
        first_hat / (jnp.sqrt(second_hat) + ADAM_EPS) + WEIGHT_DECAY * weight
    )
    average = AVERAGE_DECAY * state[2] + (1.0 - AVERAGE_DECAY) * new_weight
    return (new_weight, jnp.stack([first, second, average]))


def attention_scores(query_heads, key_heads, valid_slots, score_scale):
    scores = (
        jnp.einsum("fqhs,fkhs->fhqk", query_heads, key_heads, preferred_element_type=jnp.float32)
        * score_scale
    )
    return jnp.where(valid_slots[:, None, None, :], scores, MASK_VALUE)


def token_sum(values):
    return jnp.sum(values, axis=(0, 1), dtype=jnp.float32)


def exchange(packets):
    return lax.all_to_all(packets, AXES, split_axis=0, concat_axis=0, tiled=True)


def plain_shards(
    frames_in,
    conditioning,
    grid,
    cotangent,
    mod_weight,
    qkv_weight,
    out_weight,
    up_weight,
    down_weight,
    biases,
    mod_state,
    qkv_state,
    out_state,
    up_state,
    down_state,
    bias_state,
):
    frame_count, frame_len, model_width = frames_in.shape
    hidden_width = up_weight.shape[1]
    head_size = model_width // HEADS
    score_scale = head_size ** (-0.5)
    head_shape = (frame_count, frame_len, HEADS, head_size)
    count = lax.axis_size("wide") * lax.axis_size("narrow")
    rows = mod_weight.shape[0]
    tall_rows = down_weight.shape[0]
    low = jnp.bfloat16

    def slices(member):
        return member.reshape(rows, 4, model_width).transpose(1, 0, 2)

    a_src = slices(jnp.concatenate([qkv_weight.astype(low), out_weight.astype(low)], axis=1))
    b_src = slices(up_weight.astype(low))
    a_all, b_all, c_all = gather(a_src, b_src, down_weight.astype(low), count, (False, False, True))
    a_all = a_all[:, :, : 4 * rows].reshape(4, model_width, model_width)
    up_low = b_all[:, :, : 4 * rows].reshape(4, model_width, model_width)
    down_low = c_all[:, :, :tall_rows].reshape(hidden_width, model_width)
    query_low, key_low, value_low, out_low = (a_all[index] for index in range(4))

    cond_f = conditioning.astype(jnp.float32)
    silu_low = silu_act(cond_f).astype(low)
    mod_low = mod_weight.astype(low)
    first = exchange(
        jnp.concatenate(
            [
                silu_low.reshape(count, rows),
                jnp.broadcast_to(biases.astype(low)[None], (count, biases.shape[0])),
            ],
            axis=1,
        )
    )
    silu_rows = first[:, :rows]
    bias_low = first[:, rows:].reshape(-1)
    mod_terms = exchange(jnp.dot(silu_rows, mod_low, preferred_element_type=jnp.float32))
    mod_bias, query_bias, value_bias, out_bias, up_bias, down_bias = split_biases(
        bias_low.astype(jnp.float32), model_width, hidden_width
    )
    modulation = jnp.sum(mod_terms, axis=0, keepdims=True) + mod_bias
    valid_slots = slot_mask(grid, frame_len)
    row_mask = valid_slots[:, :, None].astype(jnp.float32)
    frames_f = frames_in.astype(jnp.float32)
    shift_attn, scale_attn, gate_attn, shift_mlp, scale_mlp, gate_mlp = jnp.split(
        modulation[:, None, :], 6, axis=-1
    )
    norm_one = modulate(frames_f, shift_attn, scale_attn).astype(low)

    def project(values, weight):
        return jnp.einsum("fbd,de->fbe", values, weight, preferred_element_type=jnp.float32)

    query_heads = (project(norm_one, query_low) + query_bias).astype(low).reshape(head_shape)
    key_heads = project(norm_one, key_low).astype(low).reshape(head_shape)
    value_heads = (project(norm_one, value_low) + value_bias).astype(low).reshape(head_shape)
    scores = attention_scores(query_heads, key_heads, valid_slots, score_scale)
    row_max = jnp.max(scores, axis=-1, keepdims=True)
    exponent = jnp.exp(scores - row_max)
    row_total = jnp.sum(exponent, axis=-1, keepdims=True)
    log_total = row_max + jnp.log(row_total)
    attention = (exponent / row_total).astype(low)
    attended = jnp.einsum(
        "fhqk,fkhs->fqhs", attention, value_heads, preferred_element_type=jnp.float32
    )
    attended = attended.reshape(frame_count, frame_len, model_width).astype(low)
    branch = project(attended, out_low) + out_bias
    midway = frames_f + gate_attn * branch
    norm_two = modulate(midway, shift_mlp, scale_mlp).astype(low)
    up_values = (
        jnp.einsum("fbd,sde->fbse", norm_two, up_low, preferred_element_type=jnp.float32).reshape(
            frame_count, frame_len, hidden_width
        )
        + up_bias
    )
    activated = gelu_tanh(up_values).astype(low)
    down_values = project(activated, down_low) + down_bias
    block_out = ((midway + gate_mlp * down_values) * row_mask).astype(low)
    upstream = cotangent.astype(jnp.float32) * row_mask
    d_gate_mlp = jnp.sum(upstream * down_values, axis=1, keepdims=True)
    d_down = (upstream * gate_mlp).astype(low)
    grad_down = jnp.einsum("fbe,fbd->ed", activated, d_down, preferred_element_type=jnp.float32)
    grad_down_bias = token_sum(d_down)
    d_activated = jnp.einsum("fbd,ed->fbe", d_down, down_low, preferred_element_type=jnp.float32)
    gelu_pull = jax.vjp(gelu_tanh, up_values)[1]
    d_up = gelu_pull(d_activated)[0].astype(low)
    d_up_parts = d_up.reshape(frame_count, frame_len, 4, model_width)
    grad_up = jnp.einsum("fbd,fbse->sde", norm_two, d_up_parts, preferred_element_type=jnp.float32)
    grad_up_bias = token_sum(d_up)
    d_norm_two = jnp.einsum("fbse,sde->fbd", d_up_parts, up_low, preferred_element_type=jnp.float32)
    second_pull = jax.vjp(modulate, midway, shift_mlp, scale_mlp)[1]
    d_midway, d_shift_mlp, d_scale_mlp = second_pull(d_norm_two)
    d_midway = d_midway + upstream
    d_gate_attn = jnp.sum(d_midway * branch, axis=1, keepdims=True)
    d_branch = (d_midway * gate_attn).astype(low)
    grad_out = jnp.einsum("fbd,fbe->de", attended, d_branch, preferred_element_type=jnp.float32)
    grad_out_bias = token_sum(d_branch)
    d_attended = jnp.einsum("fbe,de->fbd", d_branch, out_low, preferred_element_type=jnp.float32)
    d_attended = d_attended.astype(low).reshape(head_shape)
    scores = attention_scores(query_heads, key_heads, valid_slots, score_scale)
    soft = jnp.exp(scores - log_total)
    d_soft = jnp.einsum(
        "fqhs,fkhs->fhqk", d_attended, value_heads, preferred_element_type=jnp.float32
    )
    d_value_heads = jnp.einsum(
        "fhqk,fqhs->fkhs", attention, d_attended, preferred_element_type=jnp.float32
    )
    d_scores = (soft * (d_soft - jnp.sum(soft * d_soft, axis=-1, keepdims=True))).astype(low)
    d_query_heads = (
        jnp.einsum("fhqk,fkhs->fqhs", d_scores, key_heads, preferred_element_type=jnp.float32)
        * score_scale
    )
    d_key_heads = (
        jnp.einsum("fhqk,fqhs->fkhs", d_scores, query_heads, preferred_element_type=jnp.float32)
        * score_scale
    )
    flat_shape = (frame_count, frame_len, model_width)
    d_query = d_query_heads.reshape(flat_shape).astype(low)
    d_key = d_key_heads.reshape(flat_shape).astype(low)
    d_value = d_value_heads.reshape(flat_shape).astype(low)
    grad_query, grad_key, grad_value = (
        jnp.einsum("fbd,fbe->de", norm_one, member, preferred_element_type=jnp.float32)
        for member in (d_query, d_key, d_value)
    )
    grad_query_bias = token_sum(d_query)
    grad_value_bias = token_sum(d_value)
    d_norm_one = sum(
        jnp.einsum("fbe,de->fbd", member, weight, preferred_element_type=jnp.float32)
        for member, weight in ((d_query, query_low), (d_key, key_low), (d_value, value_low))
    )
    first_pull = jax.vjp(modulate, frames_f, shift_attn, scale_attn)[1]
    d_frames, d_shift_attn, d_scale_attn = first_pull(d_norm_one)
    frames_grad = (d_frames + d_midway).astype(low)
    d_modulation = jnp.concatenate(
        [d_shift_attn, d_scale_attn, d_gate_attn, d_shift_mlp, d_scale_mlp, d_gate_mlp], axis=-1
    )[:, 0, :].astype(low)
    grad_mod_bias = d_modulation[0].astype(jnp.float32)
    grad_bias = jnp.concatenate(
        [
            grad_mod_bias,
            grad_query_bias,
            grad_value_bias,
            grad_out_bias,
            grad_up_bias,
            grad_down_bias,
        ]
    )
    terms = exchange(
        jnp.concatenate(
            [
                jnp.broadcast_to(d_modulation, (count, d_modulation.shape[1])),
                grad_bias.reshape(count, -1).astype(low),
            ],
            axis=1,
        )
    )
    d_mod_all, bias_terms = terms[:, : d_modulation.shape[1]], terms[:, d_modulation.shape[1] :]

    def grouped(member, group_rows):
        member = member.astype(low).reshape(4, count // 4, 4 * rows, model_width)
        return jnp.pad(member, ((0, 0), (0, 0), (0, group_rows - 4 * rows), (0, 0)))

    group_rows = -(-4 * rows // 16) * 16
    tall_group = -(-tall_rows // 16) * 16
    a_sum, b_sum, c_sum = reduce(
        grouped(jnp.stack([grad_query, grad_key, grad_value, grad_out]), group_rows),
        grouped(grad_up, group_rows),
        jnp.pad(
            grad_down.astype(low).reshape(count // 4, 4, tall_rows, model_width),
            ((0, 0), (0, 0), (0, tall_group - tall_rows), (0, 0)),
        ),
        rows,
        (True, False, False),
    )
    red_mod = lax.dot_general(
        silu_rows, d_mod_all, (((0,), (0,)), ((), ())), preferred_element_type=jnp.float32
    )
    a_sum = a_sum.astype(jnp.float32)
    red_qkv = a_sum[:3].transpose(1, 0, 2).reshape(rows, 3 * model_width)
    red_out = a_sum[3]
    red_up = b_sum.astype(jnp.float32).transpose(1, 0, 2).reshape(rows, hidden_width)
    red_down = c_sum[:tall_rows]
    red_bias = jnp.sum(bias_terms.astype(jnp.float32), axis=0)
    d_silu = lax.dot_general(
        d_mod_all, mod_low, (((1,), (1,)), ((), ())), preferred_element_type=jnp.float32
    )
    reduced = (red_mod, red_qkv, red_out, red_up, red_down, red_bias)
    partial_sq = sum((jnp.sum(member * member) for member in reduced))
    last = exchange(
        jnp.concatenate([d_silu, jnp.broadcast_to(partial_sq, (count, 1))], axis=1)
    )
    total_sq = jnp.sum(last[:, rows])
    silu_pull = jax.vjp(silu_act, cond_f)[1]
    cond_grad = silu_pull(last[:, :rows].reshape(1, model_width))[0]
    grad_norm = jnp.sqrt(total_sq)
    factor = jnp.minimum(1.0, CLIP / (grad_norm + 1e-06))
    clipped = tuple((member * factor for member in reduced))
    masters = (mod_weight, qkv_weight, out_weight, up_weight, down_weight, biases)
    states = (mod_state, qkv_state, out_state, up_state, down_state, bias_state)
    updated = [adam_update(masters[index], states[index], clipped[index]) for index in range(6)]
    return (
        (block_out, frames_grad, cond_grad, grad_norm)
        + clipped
        + tuple(pair[0] for pair in updated)
        + tuple(pair[1] for pair in updated)
    )


def fused_shards(
    frames_in,
    conditioning,
    grid,
    cotangent,
    mod_weight,
    qkv_weight,
    out_weight,
    up_weight,
    down_weight,
    biases,
    mod_state,
    qkv_state,
    out_state,
    up_state,
    down_state,
    bias_state,
):
    frame_count, frame_len, model_width = frames_in.shape
    hidden_width = up_weight.shape[1]
    count = lax.axis_size("wide") * lax.axis_size("narrow")
    rows = mod_weight.shape[0]
    tall_rows = down_weight.shape[0]
    low = jnp.bfloat16

    def slices(member):
        return member.reshape(rows, 4, model_width).transpose(1, 0, 2)

    a_src = slices(jnp.concatenate([qkv_weight.astype(low), out_weight.astype(low)], axis=1))
    b_src = slices(up_weight.astype(low))
    cond_f = conditioning.astype(jnp.float32)
    silu_low = silu_act(cond_f).astype(low)
    mod_low = mod_weight.astype(low)
    first = exchange(
        jnp.concatenate(
            [
                silu_low.reshape(count, rows),
                jnp.broadcast_to(biases.astype(low)[None], (count, biases.shape[0])),
            ],
            axis=1,
        )
    )
    silu_rows = first[:, :rows]
    bias_f = first[:, rows:].reshape(-1).astype(jnp.float32)
    bits = count.bit_length() - 1
    crossed = [CORE, 0] + list(range(2, bits))
    sorted_rows = silu_rows.reshape((2,) * bits + (rows,)).transpose(
        [bits - 1 - bit for bit in crossed] + [bits]
    )
    terms = jnp.dot(
        sorted_rows.reshape(count, rows), mod_low, preferred_element_type=jnp.float32
    ).reshape((2,) * bits + (6 * model_width // 128, 128))
    mod_bias = bias_f[: 6 * model_width].reshape(-1, 128)
    bias_rows = bias_f[6 * model_width :].reshape(-1, model_width)
    valid_slots = slot_mask(grid, frame_len)
    row_mask = valid_slots[:, :, None].astype(jnp.float32)
    key_mask = jnp.broadcast_to(valid_slots.astype(jnp.float32), (8, frame_len))
    forward_out = forward(
        a_src, b_src, down_weight.astype(low), terms, mod_bias, bias_rows, frames_in[0], cotangent[0], key_mask, row_mask[0],
    )
    weights, mod_parts, kept, down_sums = forward_out[:3], forward_out[3], forward_out[4:-1], forward_out[-1]
    me = lax.axis_index("wide") * 2 + lax.axis_index("narrow")
    near_rows = silu_rows.reshape((2,) * bits + (rows,))
    for bit in range(bits):
        axis = bits - 1 - bit
        near_rows = jnp.where(me // (1 << bit) % 2 == 1, jnp.flip(near_rows, axis), near_rows)
    near_rows = near_rows.transpose([bits - 1 - bit for bit in reversed(SPREAD(bits))] + [bits])
    near_rows = near_rows.reshape(count, rows).T
    lift = near_rows[None, :, :, None] * jnp.eye(6, 16, dtype=low)[:, None, None, :]
    lift = lift.reshape(6, rows, 16 * count)
    block_out, frames_grad, spread, *sums, ordered, norm = backward(
        weights, mod_parts, bias_rows, down_sums, key_mask, row_mask[0], lift, mod_low, frames_in[0], cotangent[0], kept,
        rows, bits,
    )
    grads, news, news_state = update(
        sums, spread, lift, norm,
        (mod_weight, qkv_weight, out_weight, up_weight, down_weight, biases),
        (mod_state, qkv_state, out_state, up_state, down_state, bias_state),
    )
    silu_pull = jax.vjp(silu_act, cond_f)[1]
    cond_grad = silu_pull(ordered[:, :rows].reshape(1, model_width))[0]
    return (block_out[None], frames_grad[None], cond_grad, norm[0, 0]) + grads + news + news_state


def shards(*arrays):
    rows, tall_rows = arrays[4].shape[0], arrays[8].shape[0]
    fits = 4 * rows % ROUND == 0 and tall_rows % ROUND == 0
    return (fused_shards if fits else plain_shards)(*arrays)


def solution(mesh):
    tokens = P(AXES, None, None)
    matrix = P(AXES, None)
    vector = P(AXES)
    state = P(None, AXES, None)
    weights = (matrix,) * 5 + (vector,)
    states = (state,) * 5 + (P(None, AXES),)
    return jax.shard_map(
        shards,
        mesh=mesh,
        in_specs=(tokens, matrix, matrix, tokens) + weights + states,
        out_specs=(tokens, tokens, matrix, P()) + weights + weights + states,
        check_vma=False,
    )
```

```python
import functools
import jax
import jax.numpy as jnp
from jax import lax
from jax.experimental import pallas as pl
from jax.experimental.pallas import tpu as pltpu
from jax.sharding import PartitionSpec as P

HEADS = 16
STEPS = 4
CLIP = 576
NORM_EPS = 1e-06
RATE = 0.04
FIRST_DECAY = 0.5
SECOND_DECAY = 0.5
WEIGHT_DECAY = 0.1
ADAM_EPS = 1e-08
AVERAGE_DECAY = 0.9999
MASK_VALUE = -1e30
AXES = ("wide", "narrow")

MESH = pl.DeviceIdType.MESH
CORE = 1
ROUND = 16


def orders(bits, late):
    high = list(range(bits - 1, 2, -1))
    if late:
        pair = (high[:-1] + [0, 2] + high[-1:], high[:-1] + [2, 0] + high[-1:])
    else:
        pair = (high + [2, 0], high + [0, 2])
    return tuple(order + [CORE] for order in pair)


def top_place(member):
    return member.bit_length() - 1


def quotient(value, by):
    return lax.div(value, jnp.int32(by))


def remainder(value, by):
    return lax.rem(value, jnp.int32(by))


class Spots:
    def __init__(self, bits):
        wide, narrow = lax.axis_index("wide"), lax.axis_index("narrow")
        self.bits = bits
        self.me = wide * 2 + narrow
        self.quad = remainder(self.me, 4)
        self.group = quotient(self.me, 4)
        self.digit = [remainder(quotient(self.me, 1 << bit), 2) for bit in range(bits)]
        self.core = self.digit[CORE]
        self.delta = [(1 << bit) * (1 - 2 * self.digit[bit]) for bit in range(bits)]
        self.device = [
            (wide, 1 - narrow) if bit == 0 else (wide + (1 << bit - 1) * (1 - 2 * self.digit[bit]), narrow)
            for bit in range(bits)
        ]
        self.steps = {}
        first = self.core == 0
        for late in (False, True):
            pair = orders(bits, late)
            own, other, devices = [], [], []
            for place in range(bits):
                zero, one = pair[0][place], pair[1][place]
                if zero == one:
                    own.append(self.delta[zero])
                    other.append(self.delta[zero])
                    devices.append(self.device[zero])
                else:
                    own.append(jnp.where(first, self.delta[zero], self.delta[one]))
                    other.append(jnp.where(first, self.delta[one], self.delta[zero]))
                    devices.append(
                        tuple(jnp.where(first, a, b) for a, b in zip(self.device[zero], self.device[one]))
                    )
            self.steps[late] = (own, other, devices)
        self.opposite = (self.device[CORE][0], self.device[0][1])

    def block(self, late, member):
        own, other, _ = self.steps[late]
        last = self.bits - 1
        table = other if member >> last & 1 else own
        index = self.me
        for place in range(self.bits):
            if member >> place & 1:
                index = index + table[place]
        return index

    def partner(self, late, place):
        return self.steps[late][2][place]

    def near(self, other):
        if other == 3:
            return self.opposite, 3 - self.quad
        bit = other - 1
        return self.device[bit], self.quad + self.delta[bit]

    def across(self, mask):
        wide, narrow = self.device[0][0], 1 - self.device[0][1]
        for bit in range(self.bits):
            if mask >> bit & 1:
                if bit == 0:
                    narrow = 1 - narrow
                else:
                    wide = wide + (1 << bit - 1) * (1 - 2 * self.digit[bit])
        return wide, narrow

    def greet(self, masks):
        barrier = pltpu.get_barrier_semaphore()
        for mask in masks:
            pl.semaphore_signal(barrier, inc=1, device_id=self.across(mask), device_id_type=MESH)
        pl.semaphore_wait(barrier, len(masks))


def remote(source, target, send_sem, recv_sem, device):
    copy = pltpu.make_async_remote_copy(
        src_ref=source, dst_ref=target, send_sem=send_sem, recv_sem=recv_sem, device_id=device, device_id_type=MESH
    )
    copy.start()
    return copy


def local(source, target, sem):
    copy = pltpu.make_async_copy(source, target, sem)
    copy.start()
    return copy


def await_bytes(spot, sem):
    pltpu.make_async_copy(spot, spot, sem).wait()


def aligned(start, size, by=16):
    return pl.ds(pl.multiple_of(start, by), size)


def repeat(times, body):
    def run(index, carry):
        body(index)
        return carry

    lax.fori_loop(0, times, run, 0)


class Agenda:
    def __init__(self):
        self.services = []
        self.steps = []
        self.now = 0.0

    def service(self, when, action):
        self.services.append((when, len(self.services), action))

    def step(self, takes, action, after=0.0):
        self.steps.append((takes, action, after))

    def emit(self):
        while self.services or self.steps:
            self.services.sort(key=lambda item: item[:2])
            due = self.services[0][0] if self.services else None
            after = self.steps[0][2] if self.steps else None
            if self.services and (not self.steps or due <= self.now or (after > self.now and due <= after)):
                when, _, action = self.services.pop(0)
                self.now = max(self.now, when) + 0.1
            else:
                takes, action, after = self.steps.pop(0)
                self.now = max(self.now, after) + takes
            action()


def nn(left, right):
    return jnp.dot(left, right, preferred_element_type=jnp.float32)


def nt(left, right):
    return lax.dot_general(left, right, (((1,), (1,)), ((), ())), preferred_element_type=jnp.float32)


def tn(left, right):
    return lax.dot_general(left, right, (((0,), (0,)), ((), ())), preferred_element_type=jnp.float32)


def gelu_parts(value):
    bend = jnp.tanh(0.7978845608028654 * (value + 0.044715 * value * value * value))
    slope = 0.7978845608028654 * (1.0 + 0.134145 * value * value)
    return 0.5 * value * (1.0 + bend), 0.5 * (1.0 + bend) + 0.5 * value * (1.0 - bend * bend) * slope


def normalized(value):
    centre = jnp.mean(value, axis=-1, keepdims=True)
    centred = value - centre
    spread = jnp.mean(centred * centred, axis=-1, keepdims=True)
    root = lax.rsqrt(spread + NORM_EPS)
    return centred * root, root


def head_window(head, size):
    first, last = head * size // 128, (head * size + size - 1) // 128
    return first * 128, (last + 1 - first) * 128, head * size - first * 128


def only_head(values, offset, size):
    lane = lax.broadcasted_iota(jnp.int32, values.shape, 1)
    return jnp.where(jnp.logical_and(lane >= offset, lane < offset + size), values, jnp.zeros((), values.dtype))


STRIP = 32
TILE = 384
WIDE_TILE = 1152


def forward_kernel(bits, rows, pieces, clock,
                   a_src, b_src, c_src, terms_in, mod_bias, bias_rows, frames, cot, key_mask, row_mask,
                   a_out, b_out, c_out, mod_out, query_out, key_out, value_out, total_out,
                   branch_out, midway_out, slope_out, active_out, change_out, turned_out, down_out, bias_out,
                   stage, block, c_block, terms, landed, x_ref, first, query, key, value, totals, joined, attended,
                   branch, midway, second, active, active_turned, other_turned, change, other_change, turned,
                   weight, slope_stage, down_stage,
                   quad_send, quad_recv, own_sem, keep_sem, send_sem, recv_sem, term_send, term_recv,
                   pair_send, pair_recv, load_sem, weight_sem, save_sem, slope_sem, down_sem):
    count = 1 << bits
    spots = Spots(bits)
    quad, core = spots.quad, spots.core
    sibling = spots.device[CORE]
    outs = (a_out, b_out, c_out)
    tall_rows = c_src.shape[0]
    tokens, width = first.shape
    size = width // HEADS
    scale = size ** (-0.5)
    low = jnp.bfloat16
    finals = []

    def save(source, target, index):
        finals.append(local(source, target, save_sem.at[index]).wait)

    def place(piece, index):
        kind, start, length, _ = pieces[piece]
        if kind == 2:
            return c_out.at[aligned(index * tall_rows + start, length)]
        return outs[kind].at[remainder(index, 4), aligned(quotient(index, 4) * (4 * rows) + start, length)]

    def of_kind(kind):
        return [piece for piece, entry in enumerate(pieces) if entry[0] == kind]

    own = [local(source.at[quad], stage.at[kind, quad], own_sem.at[kind]) for kind, source in enumerate((a_src, b_src))]
    own.append(local(c_src, c_block, own_sem.at[2]))
    loads = [local(terms_in, terms, load_sem.at[0]), local(frames, x_ref, load_sem.at[1])]
    spots.greet([1 << bit for bit in range(bits)] + [3])
    quads = []

    def start_quad(kind, source):
        for other in (1, 2, 3):
            device, spot = spots.near(other)
            copy = remote(source.at[spot], stage.at[kind, quad], quad_send.at[kind, other], quad_recv.at[kind, other], device)
            quads.append(copy)
            finals.append(copy.wait_send)

    keeps = {}

    def launch(piece, member, source):
        late = pieces[piece][3]
        spot = spots.block(late, member)
        for step in range(top_place(member) + 1, bits):
            target = member | 1 << step
            copy = remote(
                source, place(piece, spot), send_sem.at[piece, target], recv_sem.at[piece, target], spots.partner(late, step)
            )
            finals.append(copy.wait_send)

    def open_pieces(kind, source):
        for piece in of_kind(kind):
            _, start, length, _ = pieces[piece]
            part = source.at[pl.ds(start, length)]
            launch(piece, 0, part)
            keeps[piece] = local(part, place(piece, spots.me), keep_sem.at[piece])

    def arrived(piece, member):
        spot = place(piece, spots.block(pieces[piece][3], member))
        await_bytes(spot, recv_sem.at[piece, member])
        return spot

    def open_quad(kind):
        own[kind].wait()
        for copy in quads[3 * kind : 3 * kind + 3]:
            copy.wait_recv()
        for lane in range(0, width, 128):
            parts = [stage[kind, q, :, lane : lane + 128].astype(jnp.float32) for q in range(4)]
            block[kind, :, lane : lane + 128] = jnp.concatenate(parts, axis=0).astype(low)
        open_pieces(kind, block.at[kind])

    crossed = [CORE, 0] + list(range(2, bits))
    term_copies = []

    def start_term(step):
        given = tuple(spots.digit[bit] for bit in crossed[:step]) + (1 - spots.digit[crossed[step]],)
        copy = remote(terms.at[given], landed[step], term_send.at[step], term_recv.at[step], spots.device[crossed[step]])
        term_copies.append(copy)
        finals.append(copy.wait_send)

    def end_term(step):
        kept = tuple(spots.digit[bit] for bit in crossed[: step + 1])
        term_copies[step].wait_recv()
        terms[kept] = terms[kept] + landed[step][...]
        if step + 1 < bits:
            start_term(step + 1)
            return
        parts = terms[kept] + mod_bias[...]
        per = width // 128
        for at in range(6 * per):
            part, lane = at // per, at % per * 128
            mod_out[part : part + 1, lane : lane + 128] = parts[at : at + 1, :]

    start_quad(0, a_src)
    loads[0].wait()
    start_term(0)
    own[2].wait()
    open_pieces(2, c_block)
    open_quad(0)
    start_quad(1, b_src)
    open_quad(1)
    agenda = Agenda()
    for step in range(bits):
        agenda.service(clock["terms"][0] + clock["terms"][1] * step, functools.partial(end_term, step))
    full = [0.0] * 3
    for piece, (kind, _, _, _) in enumerate(pieces):
        begin, pace = clock["pieces"][piece]
        for member in range(1, count // 2):
            agenda.service(
                begin + pace * member,
                lambda piece=piece, member=member: launch(piece, member, arrived(piece, member)),
            )
        full[kind] = max(full[kind], begin + pace * (count // 2) + clock["settle"])

    def finish(kind):
        for piece in of_kind(kind):
            for member in range(count // 2, count):
                arrived(piece, member)
            keeps[piece].wait()

    def load_weight(kind, q, slot):
        return local(outs[kind].at[q], weight.at[slot], weight_sem.at[slot])

    def over_strips(body):
        repeat(tokens // STRIP, lambda s: body(aligned(s * STRIP, STRIP, STRIP)))

    def over_tiles(body):
        repeat(width // WIDE_TILE, lambda t: body(aligned(t * WIDE_TILE, WIDE_TILE, 128)))

    pairs = {}

    def trade(index, source, target):
        pairs[index] = remote(source, target, pair_send.at[index], pair_recv.at[index], sibling)
        finals.append(pairs[index].wait_send)

    def turn(source, index):
        repeat(
            width // 128,
            lambda t: turned.__setitem__(
                (index, aligned(t * 128, 128, 128)), source[:, aligned(t * 128, 128, 128)].T
            ),
        )
        save(turned.at[index], turned_out.at[index, 0], 8 + index)
        trade(index, turned.at[index], turned_out.at[index, 1])
        finals.append(pairs[index].wait_recv)

    def norm_first():
        loads[1].wait()

        def body(where):
            unit, _ = normalized(x_ref[where, :].astype(jnp.float32))
            first[where, :] = (unit * (1.0 + mod_out[1:2, :]) + mod_out[0:1, :]).astype(low)
            upstream = cot[where, :].astype(jnp.float32) * row_mask[where, :]
            change[where, :] = (mod_out[5:6, :] * upstream).astype(low)

        over_strips(body)
        save(change, change_out, 0)
        trade(3, change, other_change)
        bias_out[...] = jnp.zeros_like(bias_out)
        bias_out[0:1, :] = jnp.sum(change[...].astype(jnp.float32), axis=0, keepdims=True)

    weight_loads = {}

    def begin_first():
        finish(0)
        for s in range(2):
            weight_loads[s] = load_weight(0, s, s)

    def project(s, target, bias):
        slot = s % 2
        weight_loads[s].wait()

        def body(where):
            result = nn(first[...], weight[slot, :, where])
            if bias is not None:
                result = result + bias_rows[bias : bias + 1, where]
            target[:, where] = result.astype(low)

        over_tiles(body)
        if s + 2 < 4:
            weight_loads[s + 2] = load_weight(0, s + 2, slot)
        save(target, (query_out, key_out, value_out)[s], 1 + s)

    def clear():
        joined[...] = jnp.zeros_like(joined)
        totals[...] = jnp.zeros_like(totals)

    def attend(head):
        start, span, offset = head_window(head, size)
        where = slice(start, start + span)
        scores = nt(only_head(query[:, where], offset, size), key[:, where])
        scores = jnp.where(key_mask[0:1, :] > 0, scores * scale, MASK_VALUE)
        peak = jnp.max(scores, axis=-1, keepdims=True)
        power = jnp.exp(scores - peak)
        total = jnp.sum(power, axis=-1, keepdims=True)
        attention = (power / total).astype(low)
        joined[:, where] = joined[:, where] + nn(attention, only_head(value[:, where], offset, size))
        lane = lax.broadcasted_iota(jnp.int32, (tokens, 128), 1)
        totals[...] = jnp.where(lane == head, peak + jnp.log(total), totals[...])

    def leave_attention():
        attended[...] = joined[...].astype(low)
        save(totals, total_out, 4)
        weight_loads[3].wait()

        def body(where):
            result = nn(attended[...], weight[1, :, where]) + bias_rows[2:3, where]
            branch[:, where] = result
            midway[:, where] = x_ref[:, where].astype(jnp.float32) + mod_out[2:3, where] * result

        over_tiles(body)
        save(branch, branch_out, 5)
        save(midway, midway_out, 6)

    def norm_second():
        def body(where):
            unit, _ = normalized(midway[where, :])
            second[where, :] = (unit * (1.0 + mod_out[4:5, :]) + mod_out[3:4, :]).astype(low)

        over_strips(body)

    up_loads = {}
    slope_copies = {}

    def begin_up():
        finish(1)
        for s in range(2):
            up_loads[s] = load_weight(1, s, s)

    def raise_up(s):
        slot = s % 2
        up_loads[s].wait()
        if s >= 2:
            slope_copies[s - 2].wait()

        def body(t):
            where = aligned(t * TILE, TILE, 128)
            wide = aligned(s * width + t * TILE, TILE, 128)
            bent, slope = gelu_parts(nn(second[...], weight[slot, :, where]) + bias_rows[aligned(3 + s, 1, 1), where])
            active[:, wide] = bent.astype(low)
            active_turned[wide, :] = bent.astype(low).T
            slope_stage[slot, :, where] = slope

        repeat(width // TILE, body)
        if s + 2 < 4:
            up_loads[s + 2] = load_weight(1, s + 2, slot)
        slope_copies[s] = local(
            slope_stage.at[slot], slope_out.at[:, pl.ds(s * width, width)], slope_sem.at[slot]
        )

    span = 2 * tall_rows

    def plane_rows(j, plane):
        return aligned((2 * j + plane) * span, span)

    def trade_active():
        save(active, active_out, 7)
        for j in range(count // 4):
            trade(4 + j, active_turned.at[plane_rows(j, 1 - core)], other_turned.at[pl.ds(j * span, span)])

    def down_gradients(first_piece):
        if first_piece == 0:
            pairs[3].wait_recv()
        for j in range(first_piece, first_piece + 4):
            pairs[4 + j].wait_recv()

        def piece(at):
            j = first_piece + at
            slot = remainder(j, 2)
            target = down_out.at[aligned(j * span, span)]
            if first_piece:
                await_bytes(target, down_sem.at[slot])
            else:
                pl.when(at >= 2)(lambda: await_bytes(target, down_sem.at[slot]))

            def body(where):
                result = nn(active_turned[plane_rows(j, core), :], change[:, where])
                result = result + nn(other_turned[aligned(j * span, span), :], other_change[:, where])
                down_stage[slot, :, where] = result.astype(low)

            over_tiles(body)
            local(down_stage.at[slot], target, down_sem.at[slot])

        repeat(4, piece)

    takes = clock["takes"]
    agenda.step(takes["norm"], norm_first, clock["terms"][0] + clock["terms"][1] * bits)
    agenda.step(takes["turn"], lambda: turn(first, 0))
    agenda.step(0.3, begin_first, full[0])
    for s, (target, bias) in enumerate(((query, 0), (key, None), (value, 1))):
        agenda.step(takes["matmul"], functools.partial(project, s, target, bias))
    agenda.step(0.3, clear)
    for head in range(HEADS):
        agenda.step(takes["head"], functools.partial(attend, head))
    agenda.step(takes["matmul"], leave_attention)
    agenda.step(takes["norm"], norm_second)
    agenda.step(0.3, begin_up, full[1])
    for s in range(4):
        agenda.step(takes["up"], functools.partial(raise_up, s))
    agenda.step(0.3, trade_active)
    agenda.step(takes["turn"], lambda: turn(attended, 1))
    agenda.step(takes["turn"], lambda: turn(second, 2))
    for j in range(0, count // 4, 4):
        agenda.step(4 * takes["down"], functools.partial(down_gradients, j))
    agenda.emit()
    finish(2)
    for done in finals:
        done()
    for index in (2, 3):
        slope_copies[index].wait()
    for slot in range(2):
        await_bytes(down_out.at[pl.ds(slot * span, span)], down_sem.at[slot])


PIECES = ((0, 0, 96, False), (0, 96, 48, True), (1, 0, 96, False), (1, 96, 48, True), (2, 0, 96, False), (2, 96, 48, True))
CLOCK = {
    "terms": (12.0, 5.0),
    "pieces": ((8.0, 1.44), (8.0, 1.44), (16.0, 4.6), (16.0, 4.6), (24.0, 6.6), (24.0, 6.6)),
    "settle": 10.0,
    "takes": {"norm": 2.0, "turn": 0.6, "matmul": 1.8, "head": 0.42, "up": 3.0, "down": 1.0},
}


def forward(a_src, b_src, c_src, terms, mod_bias, bias_rows, frames, cot, key_mask, row_mask, pieces=PIECES, clock=CLOCK):
    rows, width = a_src.shape[1:]
    tall = c_src.shape[0]
    bits = terms.ndim - 2
    count = 1 << bits
    tokens = frames.shape[0]
    hidden = tall * count
    low, wide = jnp.bfloat16, jnp.float32

    def shaped(*sizes, dtype=low):
        return jax.ShapeDtypeStruct(sizes, dtype)

    anywhere = pl.BlockSpec(memory_space=pl.ANY)
    near = pl.BlockSpec(memory_space=pltpu.VMEM)
    token = shaped(tokens, width)
    token_wide = shaped(tokens, width, dtype=wide)
    outs = (
        shaped(4, width, width), shaped(4, width, width), shaped(hidden, width),
        shaped(8, width, dtype=wide),
        token, token, token, shaped(tokens, 128, dtype=wide),
        token_wide, token_wide,
        shaped(tokens, hidden, dtype=wide), shaped(tokens, hidden), token,
        shaped(3, 2, width, tokens),
        shaped(hidden // 2, width), shaped(8, width, dtype=wide),
    )
    out_specs = [anywhere] * len(outs)
    out_specs[3] = near
    out_specs[-1] = near
    dma = pltpu.SemaphoreType.DMA
    v = pltpu.VMEM
    scratch = [
        v((2, 4, rows, width), low), v((2, 4 * rows, width), low), v((tall, width), low),
        v(terms.shape, wide), tuple(v(terms.shape[step + 1 :], wide) for step in range(bits)),
        v((tokens, width), low), v((tokens, width), low),
        v((tokens, width), low), v((tokens, width), low), v((tokens, width), low),
        v((tokens, 128), wide), v((tokens, width), wide), v((tokens, width), low),
        v((tokens, width), wide), v((tokens, width), wide), v((tokens, width), low),
        v((tokens, hidden), low), v((hidden, tokens), low), v((hidden // 2, tokens), low),
        v((tokens, width), low), v((tokens, width), low), v((3, width, tokens), low),
        v((2, width, width), low), v((2, tokens, width), wide), v((2, 2 * tall, width), low),
        dma((2, 4)), dma((2, 4)), dma((3,)), dma((len(pieces),)), dma((len(pieces), count)), dma((len(pieces), count)),
        dma((bits,)), dma((bits,)), dma((4 + count // 4,)), dma((4 + count // 4,)),
        dma((2,)), dma((2,)), dma((16,)), dma((2,)), dma((2,)),
    ]
    return pl.pallas_call(
        functools.partial(forward_kernel, bits, rows, pieces, clock),
        out_shape=outs,
        in_specs=[anywhere] * 4 + [near] * 2 + [anywhere] + [near] * 3,
        out_specs=out_specs,
        scratch_shapes=scratch,
        compiler_params=pltpu.CompilerParams(collective_id=0, has_side_effects=True, vmem_limit_bytes=56 * 1024 * 1024),
        cost_estimate=pl.CostEstimate(flops=10_000_000_000, bytes_accessed=400_000_000, transcendentals=3_000_000),
        name="forward_gather",
    )(a_src, b_src, c_src, terms, mod_bias, bias_rows, frames, cot, key_mask, row_mask)


def SPREAD(bits):
    return list(range(bits - 1, 1, -1)) + [0, CORE]


def folded_rows(values):
    whole = values.shape[0] // 8 * 8
    result = sum(values[at : at + 8, :] for at in range(0, whole, 8))
    if whole < values.shape[0]:
        rest = values[whole:, :]
        result = result + jnp.concatenate([rest, jnp.zeros((8 - rest.shape[0], rest.shape[1]), rest.dtype)], axis=0)
    return result


def bias_sums(halves, count):
    shape = (ROUND, ROUND * count // 2)
    pick = jnp.where(
        remainder(lax.broadcasted_iota(jnp.int32, shape, 1), ROUND) == lax.broadcasted_iota(jnp.int32, shape, 0), 1.0, 0.0
    ).astype(jnp.bfloat16)
    return nn(pick, halves[0]) + nn(pick, halves[1])


def lifted(lift, part, halves, count):
    half = ROUND * count // 2
    return nn(lift[part, :, :half], halves[0]) + nn(lift[part, :, half:], halves[1])


def backward_kernel(bits, rows, tall_rows, pieces, clock,
                    a_all, b_all, c_all, mod, bias_rows, down_sums, key_mask, row_mask, lift, mod_low, frames, cot_in, query_in, key_in, value_in,
                    total_in, branch_in, midway_in, slope_in, active_in, change_in, turned_in, down_in,
                    block_out, frames_out, spread_out, a_out, b_out, c_out, ordered, norm_out,
                    weight, slabs, other_up, other_low, active, slope, query, key, value, x_ref, cot, change, d_attended,
                    midway, branch, down_acc, d_norm, d_midway, turned, totals, first_grads, second_grads, third_grads, recv, total,
                    quad_block, dmod, bias_out, spread, squares, table, answers, mine, partials,
                    weight_sem, stream_sem, load_sem, save_sem, send_sem, recv_sem, pair_send, pair_recv,
                    quad_send, quad_recv, quad_own, spread_send, spread_recv, spread_own,
                    answer_send, answer_recv, norm_send, norm_recv):
    count = 1 << bits
    spots = Spots(bits)
    core = spots.core
    sibling = spots.device[CORE]
    tokens, width = x_ref.shape
    size = width // HEADS
    scale = size ** (-0.5)
    low, wide = jnp.bfloat16, jnp.float32
    span = 2 * tall_rows
    finals = []

    grads_load = local(down_in, first_grads, load_sem.at[0])
    order = [(c_all, s, True) for s in range(4)] + [(b_all, s, False) for s in range(4)]
    order += [(a_all, 3, False), (a_all, 0, False), (a_all, 1, False), (a_all, 2, False)]
    weights = {}

    def load_weight(index):
        if index < len(order):
            source, s, flat = order[index]
            part = source.at[pl.ds(s * width, width)] if flat else source.at[s]
            weights[index] = local(part, weight.at[index % 2], weight_sem.at[index % 2])

    streams = {}

    def load_stream(s):
        if s < 4:
            where = pl.ds(s * width, width)
            streams[s] = (
                local(slope_in.at[:, where], slope.at[s % 2], stream_sem.at[0, s % 2]),
                local(active_in.at[:, where], active.at[s % 2], stream_sem.at[1, s % 2]),
            )

    change_load = local(change_in, change, load_sem.at[1])
    load_weight(0)
    load_stream(0)
    load_weight(1)
    load_stream(1)
    loads = {
        name: local(source, target, load_sem.at[2 + index])
        for index, (name, source, target) in enumerate(
            (
                ("second", turned_in.at[2], turned.at[2]), ("midway", midway_in, midway), ("cot", cot_in, cot),
                ("branch", branch_in, branch), ("value", value_in, value), ("query", query_in, query), ("key", key_in, key),
                ("totals", total_in, totals), ("first", turned_in.at[0], turned.at[0]),
                ("attended", turned_in.at[1], turned.at[1]), ("x", frames, x_ref),
            )
        )
    }
    spots.greet([distance for distance in range(1, 8)] + [distance << 3 for distance in range(1, count // 8)])
    dmod[...] = jnp.zeros_like(dmod)
    bias_out[...] = jnp.zeros_like(bias_out)
    squares[...] = jnp.zeros_like(squares)

    grads = (third_grads, second_grads, first_grads)
    sums_at = (0, 1, 0)
    block_stage, frames_stage = change, d_attended
    down_copies = []

    def own(piece, member):
        kind, start, length, late = pieces[piece]
        index = spots.block(late, member)
        row = remainder(index, 2) * (tall_rows if kind == 2 else width)
        row = row + quotient(index, 4) * (span if kind == 2 else 4 * rows)
        return grads[kind].at[aligned(row + start, length)]

    def landed(piece, member):
        kind, start, length, _ = pieces[piece]
        return recv.at[kind, member - 1, pl.ds(start, length)]

    sent = {kind: [] for kind in range(3)}

    def pass_on(piece, member):
        kind, _, _, late = pieces[piece]
        place = top_place(member)
        sent[kind].append(
            remote(
                own(piece, member), landed(piece, member), send_sem.at[piece, member], recv_sem.at[piece, member],
                spots.partner(late, place),
            )
        )

    def summed(piece, member, body):
        parts = [member | 1 << place for place in range(top_place(member) + 1, bits - 1)]
        for part in parts:
            await_bytes(landed(piece, part), recv_sem.at[piece, part])
        kind, start, length, _ = pieces[piece]
        mine = own(piece, member)

        def strip(s):
            where = aligned(s * ROUND, ROUND)
            value = mine[where, :].astype(wide)
            for part in parts:
                value = value + recv[kind, part - 1, aligned(start + s * ROUND, ROUND), :].astype(wide)
            body(mine, where, s, value)

        repeat(length // ROUND, strip)

    def relay(piece, member):
        def body(mine, where, s, value):
            mine[where, :] = value.astype(low)

        summed(piece, member, body)
        pass_on(piece, member)

    left = {kind: len([1 for entry in pieces if entry[0] == kind]) for kind in range(3)}

    def settle(piece):
        kind, start, length, _ = pieces[piece]

        def body(mine, where, s, value):
            total[sums_at[kind], aligned(start + s * ROUND, ROUND), :] = value
            squares[...] = squares[...] + value * value

        if kind == 0:
            while down_copies:
                down_copies.pop().wait()
        summed(piece, 0, body)
        left[kind] -= 1
        if left[kind]:
            return
        if kind == 2:
            down_copies.append(local(total.at[0], c_out, save_sem.at[0]))
            return
        for lane in range(0, width, 128):
            for q in range(4):
                part = total[sums_at[kind], q * rows : (q + 1) * rows, lane : lane + 128]
                quad_block[kind, q, :, lane : lane + 128] = part.astype(low)
        out = (a_out, b_out)[kind]
        finals.append(local(quad_block.at[kind, spots.quad], out.at[spots.quad], quad_own.at[kind]).wait)
        for other in (1, 2, 3):
            device, spot = spots.near(other)
            copy = remote(
                quad_block.at[kind, spot], out.at[spots.quad], quad_send.at[kind, other], quad_recv.at[kind, other], device
            )
            finals.append(copy.wait)

    agenda = Agenda()

    def open_kind(kind):
        half = count // 2
        for member in range(half - 1, half // 2 - 1, -1):
            for piece, entry in enumerate(pieces):
                if entry[0] == kind:
                    pass_on(piece, member)
        begin, pace = clock["open"][kind]
        for piece, entry in enumerate(pieces):
            if entry[0] == kind:
                for at, member in enumerate(range(half // 2 - 1, 0, -1)):
                    agenda.service(agenda.now + begin + pace * at, functools.partial(relay, piece, member))
                agenda.service(agenda.now + begin + pace * (half // 2 - 1), functools.partial(settle, piece))

    def open_down():
        grads_load.wait()
        open_kind(2)

    pairs = {}

    def trade(index, source, target):
        pairs[index] = remote(source, target, pair_send.at[index], pair_recv.at[index], sibling)

    def over_strips(body):
        repeat(tokens // STRIP, lambda s: body(aligned(s * STRIP, STRIP, STRIP)))

    def over_tiles(body):
        repeat(width // TILE, lambda t: body(aligned(t * TILE, TILE, 128)))

    def add_row(ref, row, where, values):
        ref[row : row + 1, where] = ref[row : row + 1, where] + jnp.sum(values, axis=0, keepdims=True)

    everything = slice(None)

    def down_slice(s):
        slot = s % 2
        if s == 0:
            change_load.wait()
        weights[s].wait()
        for copy in streams[s]:
            copy.wait()

        def body(where):
            d_up = (nt(change[...], weight[slot, where, :]) * slope[slot, :, where]).astype(low)
            slabs[s, :, where] = d_up
            add_row(bias_out, 3 + s, where, d_up.astype(wide))
            part = nn(active[slot], weight[slot, :, where])
            down_acc[:, where] = part if s == 0 else down_acc[:, where] + part

        over_tiles(body)
        load_weight(s + 2)
        load_stream(s + 2)

    def trade_up():
        for t in range(2):
            trade(t, slabs.at[2 * (1 - core) + t], other_up.at[t])

    def up_gradient(t):
        if t == 0:
            loads["second"].wait()
        pairs[t].wait_recv()

        def body(where):
            def strip(m):
                down = aligned(m * 288, 288)
                result = nn(turned[2, 0, down, :], slabs[2 * core + t, :, where])
                result = result + nn(turned[2, 1, down, :], other_up[t, :, where])
                second_grads[aligned(t * width + m * 288, 288), where] = result.astype(low)

            repeat(width // 288, strip)

        over_tiles(body)

    def norm_two_slice(s):
        weights[4 + s].wait()

        def body(where):
            part = nt(slabs[s], weight[s % 2, where, :])
            d_norm[:, where] = part if s == 0 else d_norm[:, where] + part

        over_tiles(body)
        load_weight(6 + s)

    def upstream_of(where):
        return cot[where, :].astype(wide) * row_mask[where, :]

    def norm_back(values, gradient, gain):
        unit, root = normalized(values)
        spread = gain * gradient
        back = root * (
            spread
            - jnp.mean(spread, axis=-1, keepdims=True)
            - unit * jnp.mean(spread * unit, axis=-1, keepdims=True)
        )
        return unit, back

    def back_second():
        for name in ("midway", "cot", "branch"):
            loads[name].wait()
        for t in range(2):
            pairs[t].wait_send()

        def body(where):
            gradient = d_norm[where, :]
            unit, back = norm_back(midway[where, :], gradient, 1.0 + mod[4:5, :])
            middle = upstream_of(where) + back
            d_midway[where, :] = middle
            d_branch = (mod[2:3, :] * middle).astype(low)
            slabs[3, where, :] = d_branch
            add_row(dmod, 3, everything, gradient)
            add_row(dmod, 4, everything, gradient * unit)
            add_row(dmod, 2, everything, middle * branch[where, :])
            add_row(bias_out, 2, everything, d_branch.astype(wide))

        over_strips(body)

    def back_attended():
        weights[8].wait()

        def body(where):
            d_attended[:, where] = nt(slabs[3], weight[0, where, :]).astype(low)

        over_tiles(body)
        load_weight(10)
        for name in ("value", "query", "key", "totals"):
            loads[name].wait()
        slope[...] = jnp.zeros_like(slope)
        branch[...] = jnp.zeros_like(branch)

    def attend_back(head):
        start, reach, offset = head_window(head, size)
        where = slice(start, start + reach)
        chosen = only_head(query[:, where], offset, size)
        scores = nt(chosen, key[:, where])
        scores = jnp.where(key_mask[0:1, :] > 0, scores * scale, MASK_VALUE)
        soft = jnp.exp(scores - totals[:, head : head + 1])
        given = only_head(d_attended[:, where], offset, size)
        d_soft = nt(given, value[:, where])
        d_scores = (soft * (d_soft - jnp.sum(soft * d_soft, axis=-1, keepdims=True))).astype(low)
        slope[0, :, where] = slope[0, :, where] + nn(d_scores, only_head(key[:, where], offset, size))
        slope[1, :, where] = slope[1, :, where] + tn(d_scores, chosen)
        branch[:, where] = branch[:, where] + tn(soft.astype(low), given)

    def leave_attention():
        slabs[0] = (slope[0] * scale).astype(low)
        slabs[1] = (slope[1] * scale).astype(low)
        slabs[2] = branch[...].astype(low)
        for t in range(2):
            trade(2 + t, slabs.at[2 * (1 - core) + t], other_low.at[t])
        bias_out[0:1, :] = jnp.sum(slabs[0].astype(wide), axis=0, keepdims=True)
        bias_out[1:2, :] = jnp.sum(slabs[2].astype(wide), axis=0, keepdims=True)

    def leave_block():
        def body(where):
            down = down_acc[where, :] + bias_rows[7:8, :]
            add_row(dmod, 5, everything, upstream_of(where) * down)
            block_stage[where, :] = ((midway[where, :] + mod[5:6, :] * down) * row_mask[where, :]).astype(low)

        over_strips(body)
        finals.append(local(block_stage, block_out, save_sem.at[1]).wait)

    def low_gradient(t):
        if t == 0:
            loads["first"].wait()
            loads["attended"].wait()
        pairs[2 + t].wait_recv()
        at = 2 * core + t
        which = quotient(at, 3)

        def body(where):
            def strip(m):
                down = aligned(m * 288, 288)
                result = nn(turned[which, 0, down, :], slabs[at, :, where])
                result = result + nn(turned[which, 1, down, :], other_low[t, :, where])
                third_grads[aligned(t * width + m * 288, 288), where] = result.astype(low)

            repeat(width // 288, strip)

        over_tiles(body)

    def norm_one_slice(s):
        weights[9 + s].wait()

        def body(where):
            part = nt(slabs[s], weight[(9 + s) % 2, where, :])
            d_norm[:, where] = part if s == 0 else d_norm[:, where] + part

        over_tiles(body)
        load_weight(11 + s)

    def back_first():
        loads["x"].wait()

        def body(where):
            gradient = d_norm[where, :]
            unit, back = norm_back(x_ref[where, :].astype(wide), gradient, 1.0 + mod[1:2, :])
            add_row(dmod, 0, everything, gradient)
            add_row(dmod, 1, everything, gradient * unit)
            frames_stage[where, :] = (back + d_midway[where, :]).astype(low)

        over_strips(body)
        finals.append(local(frames_stage, frames_out, save_sem.at[2]).wait)

    spread_copies = []

    def spread_step(step):
        if step == 0:
            spread_start.wait()
        else:
            spread_copies[step - 1].wait_recv()
        if step == bits:
            use_spread()
            return
        held = pl.ds(0, ROUND << step)
        copy = remote(
            spread_out.at[held], spread_out.at[pl.ds(ROUND << step, ROUND << step)], spread_send.at[step],
            spread_recv.at[step], spots.device[SPREAD(bits)[step]],
        )
        spread_copies.append(copy)
        finals.append(copy.wait_send)
        agenda.service(agenda.now + clock["spread"], functools.partial(spread_step, step + 1))

    def start_spread():
        nonlocal spread_start
        bias_out[7:8, :] = down_sums[0:1, :]
        spread[...] = jnp.concatenate([dmod[...], bias_out[...]], axis=0).astype(low)
        spread_start = local(spread, spread_out.at[pl.ds(0, ROUND)], spread_own)
        agenda.service(agenda.now + 1.0, functools.partial(spread_step, 0))

    def use_spread():
        half = ROUND * count // 2
        copies = [local(spread_out.at[pl.ds(t * half, half)], active.at[t], stream_sem.at[1, t]) for t in range(2)]
        for copy in copies:
            copy.wait()
        both = bias_sums(active, count)
        squares[...] = squares[...] + both * both * (1.0 / count)
        member = remainder(lax.broadcasted_iota(jnp.int32, (half, rows), 0), ROUND)
        partial = [jnp.zeros((half, rows), wide) for _ in range(2)]
        for part in range(6):
            where = slice(part * width, (part + 1) * width)
            value = lifted(lift, part, active, count)
            squares[0:8, :] = squares[0:8, :] + folded_rows(value * value)
            for t in range(2):
                partial[t] = partial[t] + jnp.where(member == part, nt(active[t], mod_low[:, where]), 0.0)
        table[...] = jnp.zeros_like(table)
        shape = (count // 2, half)
        gathers = jnp.where(
            quotient(lax.broadcasted_iota(jnp.int32, shape, 1), ROUND) == lax.broadcasted_iota(jnp.int32, shape, 0), 1.0, 0.0
        )
        for t in range(2):
            table[t * count // 2 : (t + 1) * count // 2, 0:rows] = jnp.dot(
                gathers, partial[t], preferred_element_type=wide, precision=lax.Precision.HIGHEST
            )
        agenda.service(agenda.now + 0.1, functools.partial(answer_step, 0))

    answer_copies = []

    def answer_step(step):
        if step:
            slot = lax.broadcasted_iota(jnp.int32, (count, 128), 0)
            answer_copies[step - 1].wait()
            took = remainder(quotient(slot, 1 << step - 1), 2) == 1
            table[...] = jnp.where(took, answers[step - 1], table[...])
        if step < bits:
            answer_copies.append(
                remote(
                    table, answers.at[step], answer_send.at[step], answer_recv.at[step], spots.device[SPREAD(bits)[step]]
                )
            )
            agenda.service(agenda.now + clock["spread"], functools.partial(answer_step, step + 1))
            return
        for member in range(count):
            index = spots.me
            for place, bit in enumerate(SPREAD(bits)):
                if member >> place & 1:
                    index = index + spots.delta[bit]
            ordered[pl.ds(index, 1), :] = table[member : member + 1, :]

    def norm_round(first, amount, column):
        slot = sum((1 << at) * spots.digit[first + at] for at in range(amount))
        partials[column, slot] = mine[...]
        copies = []
        for distance in range(1, 1 << amount):
            copies.append(
                remote(
                    mine, partials.at[column, slot], norm_send.at[column, distance], norm_recv.at[column, distance],
                    spots.across(distance << first),
                )
            )
        for copy in copies:
            copy.wait()
        return sum(partials[column, at] for at in range(1 << amount))

    def answer():
        total_square = jnp.sum(squares[...], axis=0, keepdims=True)
        folded = sum(total_square[:, at : at + 128] for at in range(0, width, 128))
        mine[...] = jnp.broadcast_to(folded, (8, 128))
        mine[...] = norm_round(0, 3, 0)
        whole = norm_round(3, bits - 3, 1)
        norm_out[...] = jnp.broadcast_to(jnp.sqrt(jnp.sum(whole, axis=1, keepdims=True)), (8, 128))

    spread_start = None
    takes = clock["takes"]
    agenda.step(2.0, open_down)
    for s in range(4):
        agenda.step(takes["down"], functools.partial(down_slice, s))
    agenda.step(0.3, trade_up)
    for t in range(2):
        agenda.step(takes["gradient"], functools.partial(up_gradient, t))
    agenda.step(0.5, lambda: open_kind(1))
    for s in range(4):
        agenda.step(takes["matmul"], functools.partial(norm_two_slice, s))
    agenda.step(takes["norm"], back_second)
    agenda.step(takes["matmul"], back_attended)
    for head in range(HEADS):
        agenda.step(takes["head"], functools.partial(attend_back, head))
    agenda.step(1.0, leave_attention)
    agenda.step(takes["norm"], leave_block)
    for t in range(2):
        agenda.step(takes["gradient"], functools.partial(low_gradient, t))
    agenda.step(0.5, lambda: open_kind(0))
    for s in range(3):
        agenda.step(takes["matmul"], functools.partial(norm_one_slice, s))
    agenda.step(takes["norm"], back_first)
    agenda.step(0.5, start_spread)
    agenda.emit()
    answer()
    for kind in range(3):
        for copy in sent[kind]:
            copy.wait_send()
    for t in range(2):
        pairs[2 + t].wait_send()
    for done in finals:
        done()


BACK_CLOCK = {
    "spread": 4.0,
    "open": ((22.0, 4.0), (24.0, 5.5), (20.0, 5.0)),
    "takes": {"down": 4.2, "gradient": 4.2, "matmul": 2.1, "norm": 1.7, "head": 0.42},
}


def backward(weights, mod, bias_rows, down_sums, key_mask, row_mask, lift, mod_low, frames, cot, saved, rows, bits, pieces=PIECES, clock=BACK_CLOCK):
    a_all, b_all, c_all = weights
    width = a_all.shape[-1]
    count = 1 << bits
    hidden = c_all.shape[0]
    tall = hidden // count
    tokens = frames.shape[0]
    low, wide = jnp.bfloat16, jnp.float32

    def shaped(*sizes, dtype=low):
        return jax.ShapeDtypeStruct(sizes, dtype)

    anywhere = pl.BlockSpec(memory_space=pl.ANY)
    near = pl.BlockSpec(memory_space=pltpu.VMEM)
    dma = pltpu.SemaphoreType.DMA
    v = pltpu.VMEM
    kinds = len(pieces)
    scratch = [
        v((2, width, width), low), v((4, tokens, width), low),
        v((2, tokens, width), low), v((2, tokens, width), low),
        v((2, tokens, width), low), v((2, tokens, width), wide),
        v((tokens, width), low), v((tokens, width), low), v((tokens, width), low),
        v((tokens, width), low), v((tokens, width), low), v((tokens, width), low), v((tokens, width), low),
        v((tokens, width), wide), v((tokens, width), wide),
        v((tokens, width), wide), v((tokens, width), wide), v((tokens, width), wide),
        v((3, 2, width, tokens), low), v((tokens, 128), wide),
        v((2 * width, width), low), v((2 * width, width), low), v((2 * width, width), low),
        v((3, count // 2 - 1, 4 * rows, width), low), v((2, 4 * rows, width), wide), v((2, 4, rows, width), low),
        v((8, width), wide), v((8, width), wide), v((ROUND, width), low),
        v((ROUND, width), wide), v((count, 128), wide), v((bits, count, 128), wide),
        v((8, 128), wide), v((2, 8, 8, 128), wide),
        dma((2,)), dma((2, 2)), dma((13,)), dma((3,)), dma((kinds, count // 2)), dma((kinds, count // 2)),
        dma((4,)), dma((4,)), dma((2, 4)), dma((2, 4)), dma((2,)), dma((bits,)), dma((bits,)), dma, dma((bits,)), dma((bits,)), dma((2, 8)), dma((2, 8)),
    ]
    share = shaped(4, rows, width)
    return pl.pallas_call(
        functools.partial(backward_kernel, bits, rows, tall, pieces, clock),
        out_shape=(
            shaped(tokens, width), shaped(tokens, width), shaped(ROUND * count, width),
            share, share, shaped(tall, width, dtype=wide), shaped(count, 128, dtype=wide), shaped(8, 128, dtype=wide),
        ),
        in_specs=[anywhere] * 3 + [near] * 7 + [anywhere] * (2 + len(saved)),
        out_specs=[anywhere] * 6 + [near] * 2,
        scratch_shapes=scratch,
        compiler_params=pltpu.CompilerParams(collective_id=1, has_side_effects=True, vmem_limit_bytes=63 * 1024 * 1024),
        cost_estimate=pl.CostEstimate(flops=18_000_000_000, bytes_accessed=400_000_000, transcendentals=3_000_000),
        name="backward_reduce",
    )(a_all, b_all, c_all, mod, bias_rows, down_sums, key_mask, row_mask, lift, mod_low, frames, cot, *saved)


def update_kernel(count, a_in, b_in, c_in, spread_in, lift, norm, bias, bias_state, *rest):
    masters, states, rest = rest[:5], rest[5:10], rest[10:]
    grads, news, news_state, rest = rest[:5], rest[5:10], rest[10:15], rest[15:]
    (bias_grad, bias_new, bias_state_new), rest = rest[:3], rest[3:]
    w, st, g, rest = rest[:5], rest[5:10], rest[10:15], rest[15:]
    a_sum, b_sum, spread, sums, in_sem, load_sem, out_sem = rest
    wide = jnp.float32
    width = a_sum.shape[2]
    half = ROUND * count // 2
    inputs = [
        local(source, target, in_sem.at[index])
        for index, (source, target) in enumerate(
            (
                (spread_in.at[pl.ds(0, half)], spread.at[0]), (spread_in.at[pl.ds(half, half)], spread.at[1]),
                (a_in, a_sum), (b_in, b_sum), (c_in, g[4]),
            )
        )
    ]
    sequence = (0, 3, 4, 1, 2)
    loads = {
        k: (local(masters[k], w[k], load_sem.at[0, k]), local(states[k], st[k], load_sem.at[1, k])) for k in sequence
    }
    factor = jnp.minimum(1.0, CLIP / (norm[0:1, 0:1] + 1e-06))
    for copy in inputs:
        copy.wait()
    both = bias_sums(spread, count)
    sums[...] = jnp.zeros_like(sums)
    sums[0:6, :] = both[0:6, :]
    sums[6:14, :] = both[8:16, :]

    def adam(weight, first_moment, second_moment, average, raw):
        grad = raw * factor
        moved = FIRST_DECAY * first_moment + (1.0 - FIRST_DECAY) * grad
        around = SECOND_DECAY * second_moment + (1.0 - SECOND_DECAY) * grad * grad
        step = (moved / (1.0 - FIRST_DECAY**STEPS)) / (jnp.sqrt(around / (1.0 - SECOND_DECAY**STEPS)) + ADAM_EPS)
        fresh = weight - RATE * (step + WEIGHT_DECAY * weight)
        return grad, fresh, moved, around, AVERAGE_DECAY * average + (1.0 - AVERAGE_DECAY) * fresh

    share = bias.shape[1]
    first = (lax.axis_index("wide") * 2 + lax.axis_index("narrow")) * share
    top = quotient(first, width)
    pair = jnp.concatenate([sums[pl.ds(top, 1), :], sums[pl.ds(top + 1, 1), :]], axis=1)
    pair = jnp.broadcast_to(pair, (8, 2 * width))
    bias_raw = pltpu.roll(pair, 2 * width - (first - top * width), 1)[0:1, :share]
    results = adam(bias[...], bias_state[0:1, :], bias_state[1:2, :], bias_state[2:3, :], bias_raw)
    bias_grad[...], bias_new[...] = results[:2]
    for part in range(3):
        bias_state_new[part : part + 1, :] = results[2 + part]
    stores = []
    for k in sequence:
        for copy in loads[k]:
            copy.wait()
        tile = 128 if k == 4 else WIDE_TILE
        pieces = width // tile

        def body(index, k=k, tile=tile, pieces=pieces):
            part = quotient(index, pieces)
            inner = aligned(remainder(index, pieces) * tile, tile, 128)
            where = aligned(index * tile, tile, 128)
            if k == 0:
                raw = nn(lift[part, :, :half], spread[0, :, inner]) + nn(lift[part, :, half:], spread[1, :, inner])
            elif k == 4:
                raw = g[4][:, where]
            else:
                raw = (b_sum if k == 3 else a_sum)[3 if k == 2 else part, :, inner].astype(wide)
            results = adam(w[k][:, where], st[k][0, :, where], st[k][1, :, where], st[k][2, :, where], raw)
            g[k][:, where], w[k][:, where] = results[:2]
            for slot in range(3):
                st[k][slot, :, where] = results[2 + slot]

        repeat(w[k].shape[1] // tile, body)
        for at, (source, target) in enumerate(((g[k], grads[k]), (w[k], news[k]), (st[k], news_state[k]))):
            stores.append(local(source, target, out_sem.at[at, k]))
    for copy in stores:
        copy.wait()


def update(sums, spread, lift, norm, masters, states):
    a_sum, b_sum, c_sum = sums
    count = spread.shape[0] // ROUND
    wide = jnp.float32
    anywhere = pl.BlockSpec(memory_space=pl.ANY)
    near = pl.BlockSpec(memory_space=pltpu.VMEM)
    dma = pltpu.SemaphoreType.DMA

    def like(member):
        return jax.ShapeDtypeStruct(member.shape, member.dtype)

    width = a_sum.shape[2]
    bias, bias_state = masters[5].reshape(1, -1), states[5]
    outs = [like(member) for member in masters[:5]] * 2 + [like(member) for member in states[:5]]
    outs += [like(bias), like(bias), like(bias_state)]
    buffers = [pltpu.VMEM(member.shape, wide) for member in tuple(masters[:5]) + tuple(states[:5]) + tuple(masters[:5])]
    results = pl.pallas_call(
        functools.partial(update_kernel, count),
        out_shape=tuple(outs),
        in_specs=[anywhere] * 4 + [near] * 4 + [anywhere] * 10,
        out_specs=tuple([anywhere] * 15 + [near] * 3),
        scratch_shapes=buffers + [
            pltpu.VMEM(a_sum.shape, a_sum.dtype), pltpu.VMEM(b_sum.shape, b_sum.dtype),
            pltpu.VMEM((2, spread.shape[0] // 2, width), spread.dtype), pltpu.VMEM((ROUND, width), wide),
            dma((5,)), dma((2, 5)), dma((3, 5)),
        ],
        compiler_params=pltpu.CompilerParams(vmem_limit_bytes=56 * 1024 * 1024),
        cost_estimate=pl.CostEstimate(flops=100_000_000, bytes_accessed=40_000_000, transcendentals=1_000_000),
        name="update",
    )(a_sum, b_sum, c_sum, spread, lift, norm, bias, bias_state, *masters[:5], *states[:5])
    grads, news, news_state = results[:5], results[5:10], results[10:15]
    bias_grad, bias_new, bias_state_new = results[15:]
    grads = tuple(grads) + (bias_grad.reshape(-1),)
    news = tuple(news) + (bias_new.reshape(-1),)
    return grads, news, tuple(news_state) + (bias_state_new,)


def masks(order, member):
    return sum(1 << bit for place, bit in enumerate(order) if member >> place & 1)


def me_index():
    return lax.axis_index("wide") * 2 + lax.axis_index("narrow")


def device(index):
    return (index // 2, lax.rem(index, 2))


def own_plane(me):
    return lax.rem(me // 2, 2)


def flip(index, mask):
    out = index
    bit = 0
    while mask >> bit:
        if mask >> bit & 1:
            value = lax.rem(out // (1 << bit), 2)
            out = out + (1 << bit) * (1 - 2 * value)
        bit += 1
    return out


def block_of(me, pair, member, bits):
    plane = own_plane(me)
    last = 1 << (bits - 1)
    if member & last:
        rest = member - last
        zero = flip(flip(me, 1 << CORE), masks(pair[1], rest))
        one = flip(flip(me, 1 << CORE), masks(pair[0], rest))
    else:
        zero = flip(me, masks(pair[0], member))
        one = flip(me, masks(pair[1], member))
    return jnp.where(plane == 0, zero, one)


def partner_of(me, pair, place):
    zero = flip(me, 1 << pair[0][place])
    if pair[0][place] == pair[1][place]:
        return zero
    return jnp.where(own_plane(me) == 0, zero, flip(me, 1 << pair[1][place]))


def greet(me, bits):
    barrier = pltpu.get_barrier_semaphore()
    partners = [flip(me, 1 << bit) for bit in range(bits)] + [flip(me, 3)]
    for partner in partners:
        pl.semaphore_signal(barrier, inc=1, device_id=device(partner), device_id_type=MESH)
    pl.semaphore_wait(barrier, len(partners))


def gather_kernel(bits, rows, lates, a_src, b_src, c_src, a_out, b_out, c_out,
                  stage, block, c_block, quad_send, quad_recv, own_sem, keep_sem, send_sem, recv_sem):
    count = 1 << bits
    me = me_index()
    quad, spot = lax.rem(me, 4), me // 4
    pairs = [orders(bits, late) for late in lates]
    outs = (a_out, b_out, c_out)

    def place(kind, index):
        q, j = lax.rem(index, 4), index // 4
        return outs[kind].at[q, j] if kind < 2 else outs[kind].at[j, q]

    def send(kind, member, step, source):
        target = member | 1 << step
        return pltpu.make_async_remote_copy(
            src_ref=source,
            dst_ref=place(kind, block_of(me, pairs[kind], member, bits)),
            send_sem=send_sem.at[kind, target],
            recv_sem=recv_sem.at[kind, target],
            device_id=device(partner_of(me, pairs[kind], step)),
            device_id_type=MESH,
        )

    own = []
    for kind, source in enumerate((a_src, b_src)):
        own.append(pltpu.make_async_copy(source.at[quad], stage.at[kind, quad], own_sem.at[kind]))
    own.append(pltpu.make_async_copy(c_src, c_block, own_sem.at[2]))
    for copy in own:
        copy.start()
    greet(me, bits)
    quads = []
    for kind, source in enumerate((a_src, b_src)):
        for other in (1, 2, 3):
            copy = pltpu.make_async_remote_copy(
                src_ref=source.at[flip(quad, other)],
                dst_ref=stage.at[kind, quad],
                send_sem=quad_send.at[kind, other],
                recv_sem=quad_recv.at[kind, other],
                device_id=device(flip(me, other)),
                device_id_type=MESH,
            )
            copy.start()
            quads.append(copy)
    sends = []
    keeps = []

    def launch(kind, member, source):
        for step in range(top_place(member) + 1, bits):
            copy = send(kind, member, step, source)
            copy.start()
            sends.append(copy)

    def keep(kind, source):
        copy = pltpu.make_async_copy(source, place(kind, me), keep_sem.at[kind])
        copy.start()
        keeps.append(copy)

    own[2].wait()
    launch(2, 0, c_block)
    keep(2, c_block)
    padded = block.shape[1]
    for kind in (0, 1):
        own[kind].wait()
        for copy in quads[3 * kind:3 * kind + 3]:
            copy.wait_recv()
        for lane in range(0, stage.shape[3], 128):
            parts = [stage[kind, q, :, lane:lane + 128].astype(jnp.float32) for q in range(4)]
            if padded > 4 * rows:
                parts.append(jnp.zeros((padded - 4 * rows, 128), jnp.float32))
            block[kind, :, lane:lane + 128] = jnp.concatenate(parts, axis=0).astype(jnp.bfloat16)
        launch(kind, 0, block.at[kind])
        keep(kind, block.at[kind])

    def arrived(kind, member):
        spot_ref = place(kind, block_of(me, pairs[kind], member, bits))
        pltpu.make_async_copy(spot_ref, spot_ref, recv_sem.at[kind, member]).wait()
        return spot_ref

    for member in range(1, count):
        for kind in (2, 0, 1):
            launch(kind, member, arrived(kind, member))
    for copy in sends + quads:
        copy.wait_send()
    for copy in keeps:
        copy.wait()


def gather(a_src, b_src, c_src, count, lates=(False, False, False)):
    bits = count.bit_length() - 1
    rows, columns = a_src.shape[1:]
    padded = -(-4 * rows // 16) * 16
    c_padded = -(-c_src.shape[0] // 16) * 16
    if c_padded != c_src.shape[0]:
        c_src = jnp.pad(c_src, ((0, c_padded - c_src.shape[0]), (0, 0)))
    kinds = 3
    anywhere = pl.BlockSpec(memory_space=pl.ANY)
    big = jax.ShapeDtypeStruct((4, count // 4, padded, columns), jnp.bfloat16)
    tall = jax.ShapeDtypeStruct((count // 4, 4, c_padded, columns), jnp.bfloat16)
    a_all, b_all, c_all = pl.pallas_call(
        functools.partial(gather_kernel, bits, rows, lates),
        out_shape=(big, big, tall),
        in_specs=[anywhere] * 3,
        out_specs=(anywhere,) * 3,
        scratch_shapes=[
            pltpu.VMEM((2, 4, rows, columns), jnp.bfloat16),
            pltpu.VMEM((2, padded, columns), jnp.bfloat16),
            pltpu.VMEM((c_padded, columns), jnp.bfloat16),
            pltpu.SemaphoreType.DMA((2, 4)),
            pltpu.SemaphoreType.DMA((2, 4)),
            pltpu.SemaphoreType.DMA((3,)),
            pltpu.SemaphoreType.DMA((3,)),
            pltpu.SemaphoreType.DMA((kinds, count)),
            pltpu.SemaphoreType.DMA((kinds, count)),
        ],
        compiler_params=pltpu.CompilerParams(collective_id=2, has_side_effects=True),
        cost_estimate=pl.CostEstimate(flops=0, bytes_accessed=400_000_000, transcendentals=0),
        name="gather_weights",
    )(a_src, b_src, c_src)
    return a_all, b_all, c_all


def reduce_kernel(bits, rows, lates, a_in, b_in, c_in, a_out, b_out, c_out,
                  own, recv, quad_block, total, own_sem, send_sem, recv_sem, quad_send, quad_recv, quad_own, total_sem):
    count = 1 << bits
    half = count // 2
    me = me_index()
    quad = lax.rem(me, 4)
    pairs = [orders(bits, late) for late in lates]
    ins = (a_in, b_in, c_in)
    kinds = (2, 1, 0)

    def place(kind, index):
        q, j = lax.rem(index, 4), index // 4
        return ins[kind].at[q, j] if kind < 2 else ins[kind].at[j, q]

    loads = {}
    for member in range(half - 1, -1, -1):
        for kind in kinds:
            loads[kind, member] = pltpu.make_async_copy(
                place(kind, block_of(me, pairs[kind], member, bits)), own.at[kind, member], own_sem.at[kind, member]
            )
    sends = []

    def send(kind, member, source):
        step = top_place(member)
        copy = pltpu.make_async_remote_copy(
            src_ref=source,
            dst_ref=recv.at[kind, member],
            send_sem=send_sem.at[kind, member],
            recv_sem=recv_sem.at[kind, member],
            device_id=device(partner_of(me, pairs[kind], step)),
            device_id_type=MESH,
        )
        copy.start()
        sends.append(copy)

    for kind in kinds:
        loads[kind, half - 1].start()
    greet(me, bits)
    for member in range(half - 1, -1, -1):
        for kind in kinds:
            send(kind, member + half, place(kind, block_of(me, pairs[kind], member + half, bits)))
            if member < half - 1:
                loads[kind, member].start()

    padded, columns = own.shape[2:]

    def ready(kind, member):
        loads[kind, member].wait()
        parts = [member | 1 << step for step in range(top_place(member) + 1, bits)]
        for part in parts:
            pltpu.make_async_copy(recv.at[kind, part], recv.at[kind, part], recv_sem.at[kind, part]).wait()
        return parts

    def summed(kind, member, parts, where):
        value = own[kind, member, where, :].astype(jnp.float32)
        for part in parts:
            value = value + recv[kind, part, where, :].astype(jnp.float32)
        return value

    for member in range(half - 1, 0, -1):
        for kind in kinds:
            parts = ready(kind, member)

            def strip(s, carry, kind=kind, member=member, parts=parts):
                where = pl.ds(pl.multiple_of(s * 16, 16), 16)
                own[kind, member, where, :] = summed(kind, member, parts, where).astype(jnp.bfloat16)
                return carry

            lax.fori_loop(0, padded // 16, strip, 0)
            send(kind, member, own.at[kind, member])

    copies = []
    for kind in kinds:
        parts = ready(kind, 0)

        def strip(s, carry, kind=kind, parts=parts):
            where = pl.ds(pl.multiple_of(s * 16, 16), 16)
            total[kind, where, :] = summed(kind, 0, parts, where)
            return carry

        lax.fori_loop(0, padded // 16, strip, 0)
        if kind == 2:
            copy = pltpu.make_async_copy(total.at[2], c_out, total_sem)
            copy.start()
            copies.append(copy)
            continue
        out = (a_out, b_out)[kind]
        for lane in range(0, columns, 128):
            for q in range(4):
                quad_block[kind, q, :, lane:lane + 128] = total[kind, q * rows:(q + 1) * rows, lane:lane + 128].astype(jnp.bfloat16)
        copy = pltpu.make_async_copy(quad_block.at[kind, quad], out.at[quad], quad_own.at[kind])
        copy.start()
        copies.append(copy)
        for other in (1, 2, 3):
            copy = pltpu.make_async_remote_copy(
                src_ref=quad_block.at[kind, flip(quad, other)],
                dst_ref=out.at[quad],
                send_sem=quad_send.at[kind, other],
                recv_sem=quad_recv.at[kind, other],
                device_id=device(flip(me, other)),
                device_id_type=MESH,
            )
            copy.start()
            copies.append(copy)
    for copy in copies:
        copy.wait()
    for copy in sends:
        copy.wait_send()


def reduce(a_in, b_in, c_in, rows, lates=(False, False, False)):
    count = a_in.shape[1] * 4
    bits = count.bit_length() - 1
    padded, columns = a_in.shape[2:]
    anywhere = pl.BlockSpec(memory_space=pl.ANY)
    share = jax.ShapeDtypeStruct((4, rows, columns), jnp.bfloat16)
    return pl.pallas_call(
        functools.partial(reduce_kernel, bits, rows, lates),
        out_shape=(share, share, jax.ShapeDtypeStruct((padded, columns), jnp.float32)),
        in_specs=[anywhere] * 3,
        out_specs=(anywhere,) * 3,
        scratch_shapes=[
            pltpu.VMEM((3, count // 2, padded, columns), jnp.bfloat16),
            pltpu.VMEM((3, count, padded, columns), jnp.bfloat16),
            pltpu.VMEM((2, 4, rows, columns), jnp.bfloat16),
            pltpu.VMEM((3, padded, columns), jnp.float32),
            pltpu.SemaphoreType.DMA((3, count // 2)),
            pltpu.SemaphoreType.DMA((3, count)),
            pltpu.SemaphoreType.DMA((3, count)),
            pltpu.SemaphoreType.DMA((2, 4)),
            pltpu.SemaphoreType.DMA((2, 4)),
            pltpu.SemaphoreType.DMA((2,)),
            pltpu.SemaphoreType.DMA,
        ],
        compiler_params=pltpu.CompilerParams(collective_id=3, has_side_effects=True, vmem_limit_bytes=62 * 1024 * 1024),
        cost_estimate=pl.CostEstimate(flops=0, bytes_accessed=400_000_000, transcendentals=0),
        name="reduce_gradients",
    )(a_in, b_in, c_in)


def layer_norm(values):
    centre = jnp.mean(values, axis=-1, keepdims=True)
    centred = values - centre
    spread = jnp.mean(centred * centred, axis=-1, keepdims=True)
    return centred * lax.rsqrt(spread + NORM_EPS)


def modulate(values, shift_part, scale_part):
    return layer_norm(values) * (1.0 + scale_part) + shift_part


def silu_act(values):
    return values * jax.nn.sigmoid(values)


def gelu_tanh(values):
    inner = 0.7978845608028654 * (values + 0.044715 * values * values * values)
    return 0.5 * values * (1.0 + jnp.tanh(inner))


def slot_mask(grid, frame_len):
    area = grid[:, 0] * grid[:, 1]
    return lax.broadcasted_iota(jnp.int32, (grid.shape[0], frame_len), 1) < area[:, None]


def split_biases(biases, model_width, hidden_width):
    edges = [
        6 * model_width,
        7 * model_width,
        8 * model_width,
        9 * model_width,
        9 * model_width + hidden_width,
    ]
    return jnp.split(biases, edges)


def adam_update(weight, state, grad):
    first = FIRST_DECAY * state[0] + (1.0 - FIRST_DECAY) * grad
    second = SECOND_DECAY * state[1] + (1.0 - SECOND_DECAY) * grad * grad
    first_hat = first / (1.0 - FIRST_DECAY**STEPS)
    second_hat = second / (1.0 - SECOND_DECAY**STEPS)
    new_weight = weight - RATE * (
        first_hat / (jnp.sqrt(second_hat) + ADAM_EPS) + WEIGHT_DECAY * weight
    )
    average = AVERAGE_DECAY * state[2] + (1.0 - AVERAGE_DECAY) * new_weight
    return (new_weight, jnp.stack([first, second, average]))


def attention_scores(query_heads, key_heads, valid_slots, score_scale):
    scores = (
        jnp.einsum("fqhs,fkhs->fhqk", query_heads, key_heads, preferred_element_type=jnp.float32)
        * score_scale
    )
    return jnp.where(valid_slots[:, None, None, :], scores, MASK_VALUE)


def token_sum(values):
    return jnp.sum(values, axis=(0, 1), dtype=jnp.float32)


def exchange(packets):
    return lax.all_to_all(packets, AXES, split_axis=0, concat_axis=0, tiled=True)


def plain_shards(
    frames_in,
    conditioning,
    grid,
    cotangent,
    mod_weight,
    qkv_weight,
    out_weight,
    up_weight,
    down_weight,
    biases,
    mod_state,
    qkv_state,
    out_state,
    up_state,
    down_state,
    bias_state,
):
    frame_count, frame_len, model_width = frames_in.shape
    hidden_width = up_weight.shape[1]
    head_size = model_width // HEADS
    score_scale = head_size ** (-0.5)
    head_shape = (frame_count, frame_len, HEADS, head_size)
    count = lax.axis_size("wide") * lax.axis_size("narrow")
    rows = mod_weight.shape[0]
    tall_rows = down_weight.shape[0]
    low = jnp.bfloat16

    def slices(member):
        return member.reshape(rows, 4, model_width).transpose(1, 0, 2)

    a_src = slices(jnp.concatenate([qkv_weight.astype(low), out_weight.astype(low)], axis=1))
    b_src = slices(up_weight.astype(low))
    a_all, b_all, c_all = gather(a_src, b_src, down_weight.astype(low), count, (False, False, True))
    a_all = a_all[:, :, : 4 * rows].reshape(4, model_width, model_width)
    up_low = b_all[:, :, : 4 * rows].reshape(4, model_width, model_width)
    down_low = c_all[:, :, :tall_rows].reshape(hidden_width, model_width)
    query_low, key_low, value_low, out_low = (a_all[index] for index in range(4))

    cond_f = conditioning.astype(jnp.float32)
    silu_low = silu_act(cond_f).astype(low)
    mod_low = mod_weight.astype(low)
    first = exchange(
        jnp.concatenate(
            [
                silu_low.reshape(count, rows),
                jnp.broadcast_to(biases.astype(low)[None], (count, biases.shape[0])),
            ],
            axis=1,
        )
    )
    silu_rows = first[:, :rows]
    bias_low = first[:, rows:].reshape(-1)
    mod_terms = exchange(jnp.dot(silu_rows, mod_low, preferred_element_type=jnp.float32))
    mod_bias, query_bias, value_bias, out_bias, up_bias, down_bias = split_biases(
        bias_low.astype(jnp.float32), model_width, hidden_width
    )
    modulation = jnp.sum(mod_terms, axis=0, keepdims=True) + mod_bias
    valid_slots = slot_mask(grid, frame_len)
    row_mask = valid_slots[:, :, None].astype(jnp.float32)
    frames_f = frames_in.astype(jnp.float32)
    shift_attn, scale_attn, gate_attn, shift_mlp, scale_mlp, gate_mlp = jnp.split(
        modulation[:, None, :], 6, axis=-1
    )
    norm_one = modulate(frames_f, shift_attn, scale_attn).astype(low)

    def project(values, weight):
        return jnp.einsum("fbd,de->fbe", values, weight, preferred_element_type=jnp.float32)

    query_heads = (project(norm_one, query_low) + query_bias).astype(low).reshape(head_shape)
    key_heads = project(norm_one, key_low).astype(low).reshape(head_shape)
    value_heads = (project(norm_one, value_low) + value_bias).astype(low).reshape(head_shape)
    scores = attention_scores(query_heads, key_heads, valid_slots, score_scale)
    row_max = jnp.max(scores, axis=-1, keepdims=True)
    exponent = jnp.exp(scores - row_max)
    row_total = jnp.sum(exponent, axis=-1, keepdims=True)
    log_total = row_max + jnp.log(row_total)
    attention = (exponent / row_total).astype(low)
    attended = jnp.einsum(
        "fhqk,fkhs->fqhs", attention, value_heads, preferred_element_type=jnp.float32
    )
    attended = attended.reshape(frame_count, frame_len, model_width).astype(low)
    branch = project(attended, out_low) + out_bias
    midway = frames_f + gate_attn * branch
    norm_two = modulate(midway, shift_mlp, scale_mlp).astype(low)
    up_values = (
        jnp.einsum("fbd,sde->fbse", norm_two, up_low, preferred_element_type=jnp.float32).reshape(
            frame_count, frame_len, hidden_width
        )
        + up_bias
    )
    activated = gelu_tanh(up_values).astype(low)
    down_values = project(activated, down_low) + down_bias
    block_out = ((midway + gate_mlp * down_values) * row_mask).astype(low)
    upstream = cotangent.astype(jnp.float32) * row_mask
    d_gate_mlp = jnp.sum(upstream * down_values, axis=1, keepdims=True)
    d_down = (upstream * gate_mlp).astype(low)
    grad_down = jnp.einsum("fbe,fbd->ed", activated, d_down, preferred_element_type=jnp.float32)
    grad_down_bias = token_sum(d_down)
    d_activated = jnp.einsum("fbd,ed->fbe", d_down, down_low, preferred_element_type=jnp.float32)
    gelu_pull = jax.vjp(gelu_tanh, up_values)[1]
    d_up = gelu_pull(d_activated)[0].astype(low)
    d_up_parts = d_up.reshape(frame_count, frame_len, 4, model_width)
    grad_up = jnp.einsum("fbd,fbse->sde", norm_two, d_up_parts, preferred_element_type=jnp.float32)
    grad_up_bias = token_sum(d_up)
    d_norm_two = jnp.einsum("fbse,sde->fbd", d_up_parts, up_low, preferred_element_type=jnp.float32)
    second_pull = jax.vjp(modulate, midway, shift_mlp, scale_mlp)[1]
    d_midway, d_shift_mlp, d_scale_mlp = second_pull(d_norm_two)
    d_midway = d_midway + upstream
    d_gate_attn = jnp.sum(d_midway * branch, axis=1, keepdims=True)
    d_branch = (d_midway * gate_attn).astype(low)
    grad_out = jnp.einsum("fbd,fbe->de", attended, d_branch, preferred_element_type=jnp.float32)
    grad_out_bias = token_sum(d_branch)
    d_attended = jnp.einsum("fbe,de->fbd", d_branch, out_low, preferred_element_type=jnp.float32)
    d_attended = d_attended.astype(low).reshape(head_shape)
    scores = attention_scores(query_heads, key_heads, valid_slots, score_scale)
    soft = jnp.exp(scores - log_total)
    d_soft = jnp.einsum(
        "fqhs,fkhs->fhqk", d_attended, value_heads, preferred_element_type=jnp.float32
    )
    d_value_heads = jnp.einsum(
        "fhqk,fqhs->fkhs", attention, d_attended, preferred_element_type=jnp.float32
    )
    d_scores = (soft * (d_soft - jnp.sum(soft * d_soft, axis=-1, keepdims=True))).astype(low)
    d_query_heads = (
        jnp.einsum("fhqk,fkhs->fqhs", d_scores, key_heads, preferred_element_type=jnp.float32)
        * score_scale
    )
    d_key_heads = (
        jnp.einsum("fhqk,fqhs->fkhs", d_scores, query_heads, preferred_element_type=jnp.float32)
        * score_scale
    )
    flat_shape = (frame_count, frame_len, model_width)
    d_query = d_query_heads.reshape(flat_shape).astype(low)
    d_key = d_key_heads.reshape(flat_shape).astype(low)
    d_value = d_value_heads.reshape(flat_shape).astype(low)
    grad_query, grad_key, grad_value = (
        jnp.einsum("fbd,fbe->de", norm_one, member, preferred_element_type=jnp.float32)
        for member in (d_query, d_key, d_value)
    )
    grad_query_bias = token_sum(d_query)
    grad_value_bias = token_sum(d_value)
    d_norm_one = sum(
        jnp.einsum("fbe,de->fbd", member, weight, preferred_element_type=jnp.float32)
        for member, weight in ((d_query, query_low), (d_key, key_low), (d_value, value_low))
    )
    first_pull = jax.vjp(modulate, frames_f, shift_attn, scale_attn)[1]
    d_frames, d_shift_attn, d_scale_attn = first_pull(d_norm_one)
    frames_grad = (d_frames + d_midway).astype(low)
    d_modulation = jnp.concatenate(
        [d_shift_attn, d_scale_attn, d_gate_attn, d_shift_mlp, d_scale_mlp, d_gate_mlp], axis=-1
    )[:, 0, :].astype(low)
    grad_mod_bias = d_modulation[0].astype(jnp.float32)
    grad_bias = jnp.concatenate(
        [
            grad_mod_bias,
            grad_query_bias,
            grad_value_bias,
            grad_out_bias,
            grad_up_bias,
            grad_down_bias,
        ]
    )
    terms = exchange(
        jnp.concatenate(
            [
                jnp.broadcast_to(d_modulation, (count, d_modulation.shape[1])),
                grad_bias.reshape(count, -1).astype(low),
            ],
            axis=1,
        )
    )
    d_mod_all, bias_terms = terms[:, : d_modulation.shape[1]], terms[:, d_modulation.shape[1] :]

    def grouped(member, group_rows):
        member = member.astype(low).reshape(4, count // 4, 4 * rows, model_width)
        return jnp.pad(member, ((0, 0), (0, 0), (0, group_rows - 4 * rows), (0, 0)))

    group_rows = -(-4 * rows // 16) * 16
    tall_group = -(-tall_rows // 16) * 16
    a_sum, b_sum, c_sum = reduce(
        grouped(jnp.stack([grad_query, grad_key, grad_value, grad_out]), group_rows),
        grouped(grad_up, group_rows),
        jnp.pad(
            grad_down.astype(low).reshape(count // 4, 4, tall_rows, model_width),
            ((0, 0), (0, 0), (0, tall_group - tall_rows), (0, 0)),
        ),
        rows,
        (True, False, False),
    )
    red_mod = lax.dot_general(
        silu_rows, d_mod_all, (((0,), (0,)), ((), ())), preferred_element_type=jnp.float32
    )
    a_sum = a_sum.astype(jnp.float32)
    red_qkv = a_sum[:3].transpose(1, 0, 2).reshape(rows, 3 * model_width)
    red_out = a_sum[3]
    red_up = b_sum.astype(jnp.float32).transpose(1, 0, 2).reshape(rows, hidden_width)
    red_down = c_sum[:tall_rows]
    red_bias = jnp.sum(bias_terms.astype(jnp.float32), axis=0)
    d_silu = lax.dot_general(
        d_mod_all, mod_low, (((1,), (1,)), ((), ())), preferred_element_type=jnp.float32
    )
    reduced = (red_mod, red_qkv, red_out, red_up, red_down, red_bias)
    partial_sq = sum((jnp.sum(member * member) for member in reduced))
    last = exchange(
        jnp.concatenate([d_silu, jnp.broadcast_to(partial_sq, (count, 1))], axis=1)
    )
    total_sq = jnp.sum(last[:, rows])
    silu_pull = jax.vjp(silu_act, cond_f)[1]
    cond_grad = silu_pull(last[:, :rows].reshape(1, model_width))[0]
    grad_norm = jnp.sqrt(total_sq)
    factor = jnp.minimum(1.0, CLIP / (grad_norm + 1e-06))
    clipped = tuple((member * factor for member in reduced))
    masters = (mod_weight, qkv_weight, out_weight, up_weight, down_weight, biases)
    states = (mod_state, qkv_state, out_state, up_state, down_state, bias_state)
    updated = [adam_update(masters[index], states[index], clipped[index]) for index in range(6)]
    return (
        (block_out, frames_grad, cond_grad, grad_norm)
        + clipped
        + tuple(pair[0] for pair in updated)
        + tuple(pair[1] for pair in updated)
    )


def fused_shards(
    frames_in,
    conditioning,
    grid,
    cotangent,
    mod_weight,
    qkv_weight,
    out_weight,
    up_weight,
    down_weight,
    biases,
    mod_state,
    qkv_state,
    out_state,
    up_state,
    down_state,
    bias_state,
):
    frame_count, frame_len, model_width = frames_in.shape
    hidden_width = up_weight.shape[1]
    count = lax.axis_size("wide") * lax.axis_size("narrow")
    rows = mod_weight.shape[0]
    tall_rows = down_weight.shape[0]
    low = jnp.bfloat16

    def slices(member):
        return member.reshape(rows, 4, model_width).transpose(1, 0, 2)

    a_src = slices(jnp.concatenate([qkv_weight.astype(low), out_weight.astype(low)], axis=1))
    b_src = slices(up_weight.astype(low))
    cond_f = conditioning.astype(jnp.float32)
    silu_low = silu_act(cond_f).astype(low)
    mod_low = mod_weight.astype(low)
    first = exchange(
        jnp.concatenate(
            [
                silu_low.reshape(count, rows),
                jnp.broadcast_to(biases.astype(low)[None], (count, biases.shape[0])),
            ],
            axis=1,
        )
    )
    silu_rows = first[:, :rows]
    bias_f = first[:, rows:].reshape(-1).astype(jnp.float32)
    bits = count.bit_length() - 1
    crossed = [CORE, 0] + list(range(2, bits))
    sorted_rows = silu_rows.reshape((2,) * bits + (rows,)).transpose(
        [bits - 1 - bit for bit in crossed] + [bits]
    )
    terms = jnp.dot(
        sorted_rows.reshape(count, rows), mod_low, preferred_element_type=jnp.float32
    ).reshape((2,) * bits + (6 * model_width // 128, 128))
    mod_bias = bias_f[: 6 * model_width].reshape(-1, 128)
    bias_rows = bias_f[6 * model_width :].reshape(-1, model_width)
    valid_slots = slot_mask(grid, frame_len)
    row_mask = valid_slots[:, :, None].astype(jnp.float32)
    key_mask = jnp.broadcast_to(valid_slots.astype(jnp.float32), (8, frame_len))
    forward_out = forward(
        a_src, b_src, down_weight.astype(low), terms, mod_bias, bias_rows, frames_in[0], cotangent[0], key_mask, row_mask[0],
    )
    weights, mod_parts, kept, down_sums = forward_out[:3], forward_out[3], forward_out[4:-1], forward_out[-1]
    me = lax.axis_index("wide") * 2 + lax.axis_index("narrow")
    near_rows = silu_rows.reshape((2,) * bits + (rows,))
    for bit in range(bits):
        axis = bits - 1 - bit
        near_rows = jnp.where(me // (1 << bit) % 2 == 1, jnp.flip(near_rows, axis), near_rows)
    near_rows = near_rows.transpose([bits - 1 - bit for bit in reversed(SPREAD(bits))] + [bits])
    near_rows = near_rows.reshape(count, rows).T
    lift = near_rows[None, :, :, None] * jnp.eye(6, 16, dtype=low)[:, None, None, :]
    lift = lift.reshape(6, rows, 16 * count)
    block_out, frames_grad, spread, *sums, ordered, norm = backward(
        weights, mod_parts, bias_rows, down_sums, key_mask, row_mask[0], lift, mod_low, frames_in[0], cotangent[0], kept,
        rows, bits,
    )
    grads, news, news_state = update(
        sums, spread, lift, norm,
        (mod_weight, qkv_weight, out_weight, up_weight, down_weight, biases),
        (mod_state, qkv_state, out_state, up_state, down_state, bias_state),
    )
    silu_pull = jax.vjp(silu_act, cond_f)[1]
    cond_grad = silu_pull(ordered[:, :rows].reshape(1, model_width))[0]
    return (block_out[None], frames_grad[None], cond_grad, norm[0, 0]) + grads + news + news_state


def shards(*arrays):
    rows, tall_rows = arrays[4].shape[0], arrays[8].shape[0]
    fits = 4 * rows % ROUND == 0 and tall_rows % ROUND == 0
    return (fused_shards if fits else plain_shards)(*arrays)


def solution(mesh):
    tokens = P(AXES, None, None)
    matrix = P(AXES, None)
    vector = P(AXES)
    state = P(None, AXES, None)
    weights = (matrix,) * 5 + (vector,)
    states = (state,) * 5 + (P(None, AXES),)
    return jax.shard_map(
        shards,
        mesh=mesh,
        in_specs=(tokens, matrix, matrix, tokens) + weights + states,
        out_specs=(tokens, tokens, matrix, P()) + weights + weights + states,
        check_vma=False,
    )
```
